128 devices in a mesh: agent: 4 (over x_lo, core), tile: 32 (over x_hi, y, z).
Axes of the slice: x: 4 (x_hi: 2, x_lo: 2; x = x_hi * 2 + x_lo), y: 4, z: 4, core: 2. Of those that a mesh axis runs over, the one named last changes fastest.
Arguments:
- states: float32 [4, 4, 512, 512], P('agent', None, 'tile'), may hold values from -6 to 6
- sinogram: float32 [256, 4, 128], P('tile'), may hold values from -6 to 6
- blocks: bfloat16 [8192, 128, 128], P('tile'), may hold values from -0.09375 to 0.09375
- block_angle: int32 [8192], P('tile'), may hold values from 0 to 63
- block_detector: int32 [8192], P('tile'), may hold values from 0 to 3
- block_tile: int32 [8192], P('tile'), may hold values from 0 to 63
- conv_first: bfloat16 [3, 3, 3, 32], replicated, may hold values from -3 to 3
- conv_hidden: bfloat16 [3, 2, 3, 3, 32, 32], replicated, may hold values from -0.5 to 0.5
- conv_last: bfloat16 [3, 3, 3, 32], replicated, may hold values from -0.375 to 0.375
Outputs:
- new_states: float32 [4, 4, 512, 512], P('agent', None, 'tile')
The draws below stay inside these ranges and needn't reach their ends.
Inputs may be any that keep to these rules, and one draw needn't show every extreme that they name: `block_angle`: each block's angle index. `block_detector`: each block's detector block. `block_tile`: tile index among the 64 pixel tiles of the block's device.
All inputs are finite; a program needn't handle non-finite values.
Results may differ from the reference program's by a relative error of at most 0.0051.
Values may be sent and summed in bfloat16 or wider, within the bound.
No kernel may reach another device: no remote copies, remote signals or barrier semaphores. Data moves between devices by JAX's collectives and lax.ppermute only.
A program may use at most 128 MiB of HBM per device.

```python
import jax
import jax.numpy as jnp
from jax import lax

IMG = 512
SLICES = 4
ANGLES = 64
NB_DEV = 256
WIDTH = 32
MID_LAYERS = 2
DATA_STEPS = 2
TILES_DEV = 64
RAY_BLOCKS = 256
BLOCKS = 8192
BLOCKS_PER_RAY = 32


def with_ends(values, own_key, least, largest):
    place = [jax.random.randint(jax.random.fold_in(own_key, axis), (), 0, length) for axis, length in enumerate(values.shape)]
    main_axis = values.shape.index(max(values.shape))
    neighbour = place[:main_axis] + [(place[main_axis] + 1) % values.shape[main_axis]] + place[main_axis + 1:]
    return values.at[tuple(place)].set(least).at[tuple(neighbour)].set(largest)


def level_of(key, extent, shards, low, top_value):
    level, own = 1.0, jax.random.fold_in(key, 6)
    for dim, parts in shards:
        heights = jnp.exp(jax.random.uniform(jax.random.fold_in(own, dim), (parts,), jnp.float32, low / len(shards), top_value / len(shards)))
        level = level * jnp.repeat(heights, extent[dim] // parts).reshape([-1 if axis == dim else 1 for axis in range(len(extent))])
    return level


def noise(key, extent, scale, most, cuts=(), kind=jnp.bfloat16):
    drawn = jax.random.normal(key, extent, jnp.float32) * scale
    if len(cuts) > 0:
        drawn = level_of(key, extent, cuts, -0.22, 0.18) * drawn
    return jnp.clip(drawn, min=-most, max=most).astype(kind)


def setup_inputs(seed: int = 0) -> dict:
    keys = jax.random.split(jax.random.key(seed), 10)
    states = noise(keys[0], (4, SLICES, IMG, IMG), 1.0, 6.0, ((0, 4), (2, 32)), jnp.float32)
    sinogram = noise(keys[1], (RAY_BLOCKS, SLICES, 128), 1.0, 6.0, ((0, 32),), jnp.float32)
    blocks = noise(keys[2], (BLOCKS, 128, 128), (128 * BLOCKS_PER_RAY) ** -0.5, 0.09375, ((0, 32),))
    block_angle = with_ends(jax.random.randint(keys[3], (BLOCKS,), 0, ANGLES), jax.random.fold_in(keys[3], 1), 0, ANGLES - 1).astype(jnp.int32)
    block_detector = with_ends(jax.random.randint(keys[4], (BLOCKS,), 0, IMG // 128), jax.random.fold_in(keys[4], 1), 0, (IMG // 128) - 1).astype(jnp.int32)
    block_tile = with_ends(jax.random.randint(keys[5], (BLOCKS,), 0, TILES_DEV), jax.random.fold_in(keys[5], 1), 0, TILES_DEV - 1).astype(jnp.int32)
    conv_first = noise(keys[6], (3, 3, 3, WIDTH), 4 ** -0.5, 3.0)
    conv_hidden = noise(keys[7], (3, MID_LAYERS, 3, 3, WIDTH, WIDTH), (9 * WIDTH // 2) ** -0.5, 0.5)
    conv_last = noise(keys[8], (3, 3, 3, WIDTH), (9 * WIDTH) ** -0.5, 0.375)
    return {"states": states, "sinogram": sinogram, "blocks": blocks, "block_angle": block_angle, "block_detector": block_detector, "block_tile": block_tile, "conv_first": conv_first, "conv_hidden": conv_hidden, "conv_last": conv_last}


def conv_plane(feature, weight):
    padded = jnp.pad(feature.astype(jnp.float32), ((0, 0), (1, 1), (1, 1)))
    row_count = feature.shape[1]
    columns = feature.shape[2]
    weight_float = weight.astype(jnp.float32)
    summed = jnp.zeros((weight.shape[3], row_count, columns), jnp.float32)
    for offset_row in range(3):
        for offset_column in range(3):
            window = padded[:, offset_row:offset_row + row_count, offset_column:offset_column + columns]
            summed = summed + jnp.einsum("cd,cab->dab", weight_float[offset_row, offset_column], window, precision=lax.Precision.HIGHEST)
    return summed


def denoise_plane(single_plane, first, hidden, last):
    feature = single_plane[None]
    feature = jnp.maximum(conv_plane(feature, first[:, :, None, :]), 0.0).astype(jnp.bfloat16)
    for layer_index in range(hidden.shape[0]):
        feature = jnp.maximum(conv_plane(feature, hidden[layer_index]), 0.0).astype(jnp.bfloat16)
    return conv_plane(feature, last[:, :, :, None])[0]


def denoise_volume(volume, orient, conv_first, conv_hidden, conv_last):
    rounded = volume.astype(jnp.bfloat16)
    if orient == 0:
        planes = rounded
    elif orient == 1:
        planes = jnp.transpose(rounded, (2, 0, 1))
    else:
        planes = jnp.transpose(rounded, (1, 0, 2))
    result = lax.map(lambda single_plane: denoise_plane(single_plane, conv_first[orient], conv_hidden[orient], conv_last[orient]), planes)
    if orient == 0:
        return result
    if orient == 1:
        return jnp.transpose(result, (1, 2, 0))
    return jnp.transpose(result, (1, 0, 2))


def reference(states, sinogram, blocks, block_angle, block_detector, block_tile, conv_first, conv_hidden, conv_last):
    tiles_per_row = IMG // 128
    ray_index = (block_angle * tiles_per_row + block_detector).astype(jnp.int32)
    owner_device = (jnp.arange(BLOCKS, dtype=jnp.int32) // NB_DEV).astype(jnp.int32)
    pixel_index = (owner_device * TILES_DEV + block_tile).astype(jnp.int32)
    blocks_float = blocks.astype(jnp.float32)
    x_data = states[0]
    for step_index in range(DATA_STEPS):
        pixels = x_data.astype(jnp.bfloat16).reshape(SLICES, IMG * IMG // 128, 128)
        picked = jnp.take(pixels, pixel_index, axis=1).astype(jnp.float32)
        projected = jnp.einsum("zbp,bqp->bzq", picked, blocks_float, precision=lax.Precision.HIGHEST)
        ray_sums = jax.ops.segment_sum(projected, ray_index, num_segments=RAY_BLOCKS)
        residual = (ray_sums - sinogram).astype(jnp.bfloat16)
        spread = jnp.take(residual, ray_index, axis=0).astype(jnp.float32)
        contribution = jnp.einsum("bzq,bqp->bzp", spread, blocks_float, precision=lax.Precision.HIGHEST)
        summed = jax.ops.segment_sum(contribution, pixel_index, num_segments=IMG * IMG // 128)
        back_projected = jnp.transpose(summed, (1, 0, 2)).reshape(SLICES, IMG, IMG)
        x_data = x_data - 0.8 * back_projected
    fixed_points = [x_data]
    for orient in range(3):
        net_volume = denoise_volume(states[orient + 1], orient, conv_first, conv_hidden, conv_last)
        fixed_points.append(states[orient + 1] - net_volume)
    reflected = []
    for agent_index in range(4):
        reflected.append(2.0 * fixed_points[agent_index] - states[agent_index])
    average = (reflected[0] + reflected[1] + reflected[2] + reflected[3]) / 4.0
    results = []
    for agent_index in range(4):
        results.append(0.5 * states[agent_index] + 0.5 * (2.0 * average - reflected[agent_index]))
    return jnp.stack(results, axis=0)
```

```python
import functools

import jax
import jax.numpy as jnp
import numpy as np
from jax import lax
from jax.experimental import pallas as pl
from jax.experimental.pallas import tpu as pltpu
from jax.sharding import PartitionSpec as P

DATA_STEPS = 2
F32, BF16 = jnp.float32, jnp.bfloat16
VMEM_LIMIT = 40 << 20
TOGETHER = 4


def params():
    return pltpu.CompilerParams(vmem_limit_bytes=VMEM_LIMIT)


def in_vmem():
    return pl.BlockSpec(memory_space=pltpu.VMEM)


def in_smem():
    return pl.BlockSpec(memory_space=pltpu.SMEM)


def low_rows():
    return lax.broadcasted_iota(jnp.int32, (8, 128), 0) < 4


def twice(ref, place, value):
    ref[place, 0:4] = value
    ref[place, 4:8] = value


def four_blocks(blk, b):
    size = blk.shape[1]
    left = blk[pl.ds(b, 2)].reshape(2 * size, size)
    right = blk[pl.ds(b + 2, 2)].reshape(2 * size, size)
    return jnp.concatenate([left, right], axis=1)


def add_rows(acc, index, value):
    acc[index] = acc[index] + value


def project_blocks(count, first, unroll, ray_ref, tile_ref, pix, blk, acc):
    low = low_rows()
    zero = jnp.zeros((8, 128), F32)

    def body(i, carry):
        outs = []
        for u in range(unroll):
            b = (i * unroll + u) * TOGETHER
            t = [pix[tile_ref[first + b + k]] for k in range(TOGETHER)]
            upper = jnp.concatenate([jnp.where(low, t[0], t[1]), zero], axis=0)
            lower = jnp.concatenate([zero, jnp.where(low, t[2], t[3])], axis=0)
            lhs = jnp.concatenate([upper.astype(BF16), lower.astype(BF16)], axis=1)
            outs.append(
                lax.dot_general(
                    lhs, four_blocks(blk, b), (((1,), (1,)), ((), ())), preferred_element_type=F32
                )
            )
        for u in range(unroll):
            b = first + (i * unroll + u) * TOGETHER
            out = outs[u]
            add_rows(acc, ray_ref[b], jnp.where(low, out[0:8, 0:128], 0.0))
            add_rows(acc, ray_ref[b + 1], jnp.where(low, 0.0, out[0:8, 128:256]))
            add_rows(acc, ray_ref[b + 2], jnp.where(low, out[8:16, 0:128], 0.0))
            add_rows(acc, ray_ref[b + 3], jnp.where(low, 0.0, out[8:16, 128:256]))
        return carry

    lax.fori_loop(0, count // (TOGETHER * unroll), body, 0)


def back_blocks(count, first, unroll, ray_ref, tile_ref, res, blk, acc):
    low = low_rows()

    def body(i, carry):
        outs = []
        for u in range(unroll):
            b = (i * unroll + u) * TOGETHER
            t = [res[ray_ref[first + b + k]] for k in range(TOGETHER)]
            left = jnp.concatenate([jnp.where(low, t[0], 0.0), jnp.where(low, t[2], 0.0)], axis=0)
            right = jnp.concatenate([jnp.where(low, 0.0, t[1]), jnp.where(low, 0.0, t[3])], axis=0)
            lhs = jnp.concatenate([left.astype(BF16), right.astype(BF16)], axis=1)
            outs.append(jnp.dot(lhs, four_blocks(blk, b), preferred_element_type=F32))
        for u in range(unroll):
            b = first + (i * unroll + u) * TOGETHER
            upper, lower = outs[u][0:8, 0:128], outs[u][8:16, 128:256]
            add_rows(acc, tile_ref[b], jnp.where(low, upper, 0.0))
            add_rows(acc, tile_ref[b + 1], jnp.where(low, 0.0, upper))
            add_rows(acc, tile_ref[b + 2], jnp.where(low, lower, 0.0))
            add_rows(acc, tile_ref[b + 3], jnp.where(low, 0.0, lower))
        return carry

    lax.fori_loop(0, count // (TOGETHER * unroll), body, 0)


def tiles_of(x_shape):
    wide = x_shape[2] // 128
    return [(r * wide + c, r, slice(c * 128, c * 128 + 128)) for r in range(x_shape[1]) for c in range(wide)]


def load_pixels(x_ref, pix):
    for t, r, columns in tiles_of(x_ref.shape):
        twice(pix, t, x_ref[:, r, columns])


def load_residual(r_ref, res):
    for z in range(4):
        value = r_ref[:, z * 128 : z * 128 + 128].astype(F32)
        res[:, z, :] = value
        res[:, z + 4, :] = value


def store_rays(acc, o_ref):
    for z in range(4):
        o_ref[:, z * 128 : z * 128 + 128] = (acc[:, z, :] + acc[:, z + 4, :]).astype(o_ref.dtype)


def project_kernel(steps, unroll, ray_ref, tile_ref, x_ref, blk, o_ref, pix, acc):
    step = pl.program_id(0)

    @pl.when(step == 0)
    def _():
        load_pixels(x_ref, pix)
        acc[...] = jnp.zeros_like(acc)

    count = blk.shape[0]
    project_blocks(count, step * count, unroll, ray_ref, tile_ref, pix, blk, acc)

    @pl.when(step == steps - 1)
    def _():
        store_rays(acc, o_ref)


def project(ray_index, tile_index, x, blocks, ray_total):
    steps = 2
    count = blocks.shape[0] // steps
    slices, _, _ = x.shape
    tiles = x.shape[1] * x.shape[2] // 128
    return pl.pallas_call(
        functools.partial(project_kernel, steps, 16),
        grid=(steps,),
        out_shape=jax.ShapeDtypeStruct((ray_total, slices * 128), BF16),
        in_specs=[
            in_smem(),
            in_smem(),
            pl.BlockSpec(x.shape, lambda g: (0, 0, 0)),
            pl.BlockSpec((count, 128, 128), lambda g: (g, 0, 0)),
        ],
        out_specs=pl.BlockSpec((ray_total, slices * 128), lambda g: (0, 0)),
        scratch_shapes=[pltpu.VMEM((tiles, 8, 128), F32), pltpu.VMEM((ray_total, 8, 128), F32)],
        compiler_params=params(),
        name="project",
    )(ray_index, tile_index, x, blocks)


def back_project_kernel(unroll, ray_ref, tile_ref, r_ref, x_ref, blk, x_out, o_ref, res, pix, back, acc):
    load_residual(r_ref, res)
    back[...] = jnp.zeros_like(back)
    count = blk.shape[0]
    back_blocks(count, 0, unroll, ray_ref, tile_ref, res, blk, back)
    for t, r, columns in tiles_of(x_ref.shape):
        moved = x_ref[:, r, columns] - 0.8 * (back[t, 0:4] + back[t, 4:8])
        x_out[:, r, columns] = moved
        twice(pix, t, moved)
    acc[...] = jnp.zeros_like(acc)
    project_blocks(count, 0, unroll, ray_ref, tile_ref, pix, blk, acc)
    store_rays(acc, o_ref)


def back_project(ray_index, tile_index, residual, x, blocks):
    ray_total = residual.shape[0]
    tiles = x.shape[1] * x.shape[2] // 128
    return pl.pallas_call(
        functools.partial(back_project_kernel, 16),
        out_shape=(
            jax.ShapeDtypeStruct(x.shape, F32),
            jax.ShapeDtypeStruct(residual.shape, BF16),
        ),
        in_specs=[in_smem(), in_smem(), in_vmem(), in_vmem(), in_vmem()],
        out_specs=(in_vmem(), in_vmem()),
        scratch_shapes=[
            pltpu.VMEM((ray_total, 8, 128), F32),
            pltpu.VMEM((tiles, 8, 128), F32),
            pltpu.VMEM((tiles, 8, 128), F32),
            pltpu.VMEM((ray_total, 8, 128), F32),
        ],
        compiler_params=params(),
        name="back_project",
    )(ray_index, tile_index, residual, x, blocks)


def back_kernel(unroll, ray_ref, tile_ref, r_ref, x_ref, start_ref, blk, o_ref, res, back):
    load_residual(r_ref, res)
    back[...] = jnp.zeros_like(back)
    back_blocks(blk.shape[0], 0, unroll, ray_ref, tile_ref, res, blk, back)
    for t, r, columns in tiles_of(x_ref.shape):
        moved = x_ref[:, r, columns] - 0.8 * (back[t, 0:4] + back[t, 4:8])
        o_ref[:, r, columns] = 2.0 * moved - start_ref[:, r, columns]


def back_reflect(ray_index, tile_index, residual, x, start, blocks):
    ray_total = residual.shape[0]
    tiles = x.shape[1] * x.shape[2] // 128
    return pl.pallas_call(
        functools.partial(back_kernel, 16),
        out_shape=jax.ShapeDtypeStruct(x.shape, F32),
        in_specs=[in_smem(), in_smem(), in_vmem(), in_vmem(), in_vmem(), in_vmem()],
        out_specs=in_vmem(),
        scratch_shapes=[
            pltpu.VMEM((ray_total, 8, 128), F32),
            pltpu.VMEM((tiles, 8, 128), F32),
        ],
        compiler_params=params(),
        name="back_reflect",
    )(ray_index, tile_index, residual, x, start, blocks)


def residual_everywhere(partial_sums, sinogram):
    count = lax.axis_size("tile")
    own = partial_sums.shape[0] // count
    parts = lax.all_to_all(partial_sums.reshape(count, own, -1), "tile", 0, 0, tiled=True)
    total = jnp.sum(parts.astype(F32), axis=0)
    residual = (total - sinogram.reshape(own, -1)).astype(BF16)
    copies = jnp.broadcast_to(residual, (count, *residual.shape))
    return lax.all_to_all(copies, "tile", 0, 0, tiled=True).reshape(partial_sums.shape)


def banded(size):
    return np.stack([np.eye(size, k=i - 1, dtype=np.float32) for i in range(3)])


def widened(matrix, groups, stride, width):
    rows = []
    for g in range(groups):
        rows.append(jnp.pad(matrix, ((0, 0), (g * stride, width - matrix.shape[1] - g * stride))))
    return jnp.concatenate(rows, axis=0)


def slice_weights(first, hidden, last):
    band = banded(4)
    width = first.shape[2]
    first_m = jnp.einsum("iyz,ijd->ydjz", band, first.astype(F32)).reshape(4 * width, 12)
    hidden_m = jnp.einsum("iyz,lijcd->lydjzc", band, hidden.astype(F32)).reshape(
        hidden.shape[0], 4 * width, 12 * width
    )
    last_m = jnp.einsum("iyz,ijc->yjzc", band, last.astype(F32)).reshape(4, 12 * width)
    return first_m, hidden_m, last_m


def relu_rows(value, keep):
    value = jnp.maximum(value, 0.0)
    return value if keep is None else jnp.where(keep, value, 0.0)


def sagittal_kernel(edge_ref, x_ref, cur_ref, wf, wh, wl, o_ref, ha, hb):
    rows = cur_ref.shape[1]
    width = wf.shape[0]
    depth = wh.shape[0] + 1
    above, below = edge_ref[0] != 0, edge_ref[1] != 0

    def kept(layer, y):
        reach = depth - layer
        return above if y < reach else below if y >= reach + rows else None

    for y in range(rows + 2 * depth):
        value = jnp.dot(wf[...], x_ref[y], preferred_element_type=F32)
        ha[y * width : (y + 1) * width] = relu_rows(value, kept(0, y)).astype(BF16)
    source, target = ha, hb
    for layer in range(wh.shape[0]):
        for y in range(0, rows + 2 * (depth - 1 - layer), 2):
            value = jnp.dot(
                wh[layer], source[y * width : (y + 4) * width], preferred_element_type=F32
            )
            for k in range(2):
                part = value[k * width : (k + 1) * width]
                target[(y + k) * width : (y + k + 1) * width] = relu_rows(
                    part, kept(layer + 1, y + k)
                ).astype(BF16)
        source, target = target, source
    for y in range(0, rows, 4):
        net = jnp.dot(wl[...], source[y * width : (y + 6) * width], preferred_element_type=F32)
        for z in range(4):
            o_ref[z, y : y + 4] = cur_ref[z, y : y + 4] - 2.0 * net[z * 4 : z * 4 + 4]


def sagittal_reflect(current, rimmed, edges, first, hidden, last):
    slices, rows, columns = current.shape
    first_m, hidden_m, last_m = slice_weights(first, hidden, last)
    width = first_m.shape[0]
    first_m = jnp.pad(first_m, ((0, 0), (0, 4))).astype(BF16)
    hidden_m = jax.vmap(lambda m: widened(m, 2, width, 4 * width))(hidden_m).astype(BF16)
    last_m = widened(last_m, 4, width, 6 * width)
    last_m = last_m.reshape(4, 4, -1).swapaxes(0, 1).reshape(16, -1).astype(BF16)
    by_row = jnp.transpose(rimmed, (1, 0, 2))
    reach = rimmed.shape[1] - 2
    taps = jnp.concatenate([by_row[j : j + reach] for j in range(3)], axis=1)
    taps = jnp.pad(taps, ((0, 0), (0, 4), (0, 0)))
    return pl.pallas_call(
        sagittal_kernel,
        out_shape=jax.ShapeDtypeStruct(current.shape, F32),
        in_specs=[in_smem()] + [in_vmem()] * 5,
        out_specs=in_vmem(),
        scratch_shapes=[pltpu.VMEM((reach * width, columns), BF16)] * 2,
        compiler_params=params(),
        name="sagittal",
    )(edges, taps, current, first_m, hidden_m, last_m)


def side_by_side(value):
    columns = value.shape[1]
    place = lax.broadcasted_iota(jnp.int32, value.shape, 1)
    before = jnp.where(place == 0, 0.0, pltpu.roll(value, 1, axis=1))
    after = jnp.where(place == columns - 1, 0.0, pltpu.roll(value, columns - 1, axis=1))
    return before, value, after


def coronal_kernel(x_ref, cur_ref, wf, wh, wl, o_ref, h):
    rows = cur_ref.shape[1]
    width = wf.shape[0]

    def body(y, carry):
        value = jnp.dot(wf[...], x_ref[y], preferred_element_type=F32)
        for layer in range(wh.shape[0] + 1):
            value = jnp.maximum(value, 0.0)
            for j, moved in enumerate(side_by_side(value)):
                h[j * width : (j + 1) * width] = moved.astype(BF16)
            matrix = wh[layer] if layer < wh.shape[0] else wl[...]
            value = jnp.dot(matrix, h[...], preferred_element_type=F32)
        o_ref[y] = cur_ref[y] - 2.0 * value[0 : cur_ref.shape[1]]
        return carry

    lax.fori_loop(0, cur_ref.shape[0], body, 0)


def shifted_columns(planes, dim):
    pads = [(0, 0)] * planes.ndim
    pads[-1] = (1, 1)
    padded = jnp.pad(planes, pads)
    columns = planes.shape[-1]
    return jnp.concatenate([padded[..., j : j + columns] for j in range(3)], axis=dim)


def coronal_reflect(current, first, hidden, last):
    slices, rows, columns = current.shape
    first_m, hidden_m, last_m = slice_weights(first, hidden, last)
    width = first_m.shape[0]
    first_m = jnp.pad(first_m, ((0, 0), (0, 4))).astype(BF16)
    last_m = jnp.pad(last_m, ((0, 4), (0, 0))).astype(BF16)
    by_row = jnp.transpose(current, (1, 0, 2))
    taps = jnp.pad(shifted_columns(by_row.astype(BF16), 1), ((0, 0), (0, 4), (0, 0)))
    reflect = pl.pallas_call(
        coronal_kernel,
        out_shape=jax.ShapeDtypeStruct(by_row.shape, F32),
        in_specs=[in_vmem()] * 5,
        out_specs=in_vmem(),
        scratch_shapes=[pltpu.VMEM((3 * width, columns), BF16)],
        compiler_params=params(),
        name="coronal",
    )(taps, by_row, first_m, hidden_m.astype(BF16), last_m)
    return jnp.transpose(reflect, (1, 0, 2))


SPAN = 6


def spans(rows):
    starts = list(range(0, rows - SPAN, SPAN))
    return starts + [rows - SPAN]


def axial_kernel(edge_ref, x_ref, cur_ref, wf, wh, wl, o_ref, ha, hb):
    rows = cur_ref.shape[1]
    channels = wh.shape[3] // (SPAN + 2)
    depth = wh.shape[0] + 1
    above, below = edge_ref[0] != 0, edge_ref[1] != 0

    def put(target, layer, start, value):
        value = jnp.maximum(value, 0.0)
        reach = depth - layer
        parts = []
        for k in range(SPAN):
            part = value[k * channels : (k + 1) * channels]
            y = start + k
            if y < reach:
                part = jnp.where(above, part, 0.0)
            elif y >= reach + rows:
                part = jnp.where(below, part, 0.0)
            parts.append(part)
        value = jnp.concatenate(parts, axis=0)
        for j, moved in enumerate(side_by_side(value)):
            target[j, start * channels : (start + SPAN) * channels] = moved.astype(BF16)

    def over_columns(matrices, source, start):
        total = None
        for j in range(3):
            window = source[j, start * channels : (start + SPAN + 2) * channels]
            part = jnp.dot(matrices[j], window, preferred_element_type=F32)
            total = part if total is None else total + part
        return total

    def body(z, carry):
        for n, start in enumerate(spans(rows + 2 * depth)):
            put(ha, 0, start, jnp.dot(wf[...], x_ref[z, n], preferred_element_type=F32))
        source, target = ha, hb
        for layer in range(wh.shape[0]):
            for start in spans(rows + 2 * (depth - 1 - layer)):
                put(target, layer + 1, start, over_columns(wh[layer], source, start))
            source, target = target, source
        for start in spans(rows):
            net = over_columns(wl[...], source, start)
            o_ref[z, start : start + SPAN] = cur_ref[z, start : start + SPAN] - 2.0 * net[0:SPAN]
        return carry

    lax.fori_loop(0, cur_ref.shape[0], body, 0)


def axial_reflect(current, rimmed, edges, first, hidden, last):
    slices, rows, columns = current.shape
    channels = first.shape[2]
    band = np.stack([np.eye(SPAN, SPAN + 2, k=i, dtype=np.float32) for i in range(3)])
    first_m = jnp.einsum("iyz,ijd->ydjz", band, first.astype(F32)).reshape(SPAN * channels, -1)
    first_m = jnp.pad(first_m, ((0, 0), (0, 32 - first_m.shape[1]))).astype(BF16)
    hidden_m = jnp.einsum("iyz,lijcd->ljydzc", band, hidden.astype(F32))
    hidden_m = hidden_m.reshape(*hidden_m.shape[:2], SPAN * channels, -1).astype(BF16)
    last_m = jnp.einsum("iyz,ijc->jyzc", band, last.astype(F32)).reshape(3, SPAN, -1)
    last_m = jnp.pad(last_m, ((0, 0), (0, 2), (0, 0))).astype(BF16)
    reach = rimmed.shape[1] - 2
    windows = jnp.stack([rimmed[:, s : s + SPAN + 2] for s in spans(reach)], axis=1)
    taps = shifted_columns(windows, 2)
    taps = jnp.pad(taps, ((0, 0), (0, 0), (0, 32 - taps.shape[2]), (0, 0)))
    return pl.pallas_call(
        axial_kernel,
        out_shape=jax.ShapeDtypeStruct(current.shape, F32),
        in_specs=[in_smem()] + [in_vmem()] * 5,
        out_specs=in_vmem(),
        scratch_shapes=[pltpu.VMEM((3, reach * channels, columns), BF16)] * 2,
        compiler_params=params(),
        name="axial",
    )(edges, taps, current, first_m, hidden_m, last_m)


def with_rim(cells, axis, dim, depth):
    count = lax.axis_size(axis)
    head = lax.slice_in_dim(cells, 0, depth, axis=dim)
    tail = lax.slice_in_dim(cells, cells.shape[dim] - depth, cells.shape[dim], axis=dim)
    before = lax.ppermute(tail, axis, [(i, i + 1) for i in range(count - 1)])
    after = lax.ppermute(head, axis, [(i + 1, i) for i in range(count - 1)])
    return jnp.concatenate([before, cells, after], axis=dim)


def per_device(
    states,
    sinogram,
    blocks,
    block_angle,
    block_detector,
    block_tile,
    conv_first,
    conv_hidden,
    conv_last,
):
    current = states[0]
    tile_count = lax.axis_size("tile")
    tile_place = lax.axis_index("tile")
    agent_place = lax.axis_index("agent")
    halo_depth = conv_hidden.shape[1] + 2
    edges = jnp.stack([tile_place > 0, tile_place < tile_count - 1]).astype(jnp.int32)

    def data():
        ray_total = sinogram.shape[0] * tile_count
        ray_index = block_angle * (current.shape[2] // 128) + block_detector
        x_data = current
        partial_sums = project(ray_index, block_tile, x_data, blocks, ray_total)
        for _ in range(DATA_STEPS - 1):
            residual = residual_everywhere(partial_sums, sinogram)
            x_data, partial_sums = back_project(ray_index, block_tile, residual, x_data, blocks)
        residual = residual_everywhere(partial_sums, sinogram)
        return back_reflect(ray_index, block_tile, residual, x_data, current, blocks)

    def axial():
        rimmed = with_rim(current.astype(BF16), "tile", 1, halo_depth)
        return axial_reflect(current, rimmed, edges, conv_first[0], conv_hidden[0], conv_last[0])

    def sagittal():
        rimmed = with_rim(current.astype(BF16), "tile", 1, halo_depth)
        return sagittal_reflect(current, rimmed, edges, conv_first[1], conv_hidden[1], conv_last[1])

    def coronal():
        return coronal_reflect(current, conv_first[2], conv_hidden[2], conv_last[2])

    reflect = lax.switch(agent_place, [data, axial, sagittal, coronal])
    everything = lax.all_gather(reflect, "agent")
    average = jnp.sum(everything, axis=0) / 4.0
    new_states = 0.5 * current + 0.5 * (2.0 * average - reflect)
    return new_states[None]


def solution(mesh):
    placed = (
        P("agent", None, "tile", None),
        P("tile", None, None),
        P("tile", None, None),
        P("tile"),
        P("tile"),
        P("tile"),
        P(),
        P(),
        P(),
    )
    return jax.shard_map(
        per_device,
        mesh=mesh,
        in_specs=placed,
        out_specs=P("agent", None, "tile", None),
        check_vma=False,
    )
```

```python
import functools

import jax
import jax.numpy as jnp
import numpy as np
from jax import lax
from jax.experimental import pallas as pl
from jax.experimental.pallas import tpu as pltpu
from jax.sharding import PartitionSpec as P

DATA_STEPS = 2
F32, BF16 = jnp.float32, jnp.bfloat16
VMEM_LIMIT = 32 << 20
TOGETHER = 4
UNROLL = 16
SPAN = 6


def params():
    return pltpu.CompilerParams(vmem_limit_bytes=VMEM_LIMIT)


def in_vmem():
    return pl.BlockSpec(memory_space=pltpu.VMEM)


def in_smem():
    return pl.BlockSpec(memory_space=pltpu.SMEM)


def low_rows():
    return lax.broadcasted_iota(jnp.int32, (8, 128), 0) < 4


def four_blocks(blk, b):
    size = blk.shape[1]
    left = blk[pl.ds(b, 2)].reshape(2 * size, size)
    right = blk[pl.ds(b + 2, 2)].reshape(2 * size, size)
    return jnp.concatenate([left, right], axis=1)


def row(ref, index):
    return ref[pl.ds(index, 8, stride=0), :]


def add_rows(acc, index, value):
    acc[index] = acc[index] + value


def project_blocks(ray_ref, tile_ref, pix, blk, acc):
    low = low_rows()
    zero = jnp.zeros((8, 128), F32)

    def body(i, carry):
        outs = []
        for u in range(UNROLL):
            b = (i * UNROLL + u) * TOGETHER
            t = [row(pix, tile_ref[b + k]) for k in range(TOGETHER)]
            upper = jnp.concatenate([jnp.where(low, t[0], t[1]), zero], axis=0)
            lower = jnp.concatenate([zero, jnp.where(low, t[2], t[3])], axis=0)
            lhs = jnp.concatenate([upper.astype(BF16), lower.astype(BF16)], axis=1)
            outs.append(
                lax.dot_general(
                    lhs, four_blocks(blk, b), (((1,), (1,)), ((), ())), preferred_element_type=F32
                )
            )
        for u in range(UNROLL):
            b = (i * UNROLL + u) * TOGETHER
            out = outs[u]
            add_rows(acc, ray_ref[b], jnp.where(low, out[0:8, 0:128], 0.0))
            add_rows(acc, ray_ref[b + 1], jnp.where(low, 0.0, out[0:8, 128:256]))
            add_rows(acc, ray_ref[b + 2], jnp.where(low, out[8:16, 0:128], 0.0))
            add_rows(acc, ray_ref[b + 3], jnp.where(low, 0.0, out[8:16, 128:256]))
        return carry

    lax.fori_loop(0, blk.shape[0] // (TOGETHER * UNROLL), body, 0)


def back_blocks(ray_ref, tile_ref, res, blk, acc):
    low = low_rows()

    def body(i, carry):
        outs = []
        for u in range(UNROLL):
            b = (i * UNROLL + u) * TOGETHER
            t = [row(res, ray_ref[b + k]) for k in range(TOGETHER)]
            left = jnp.concatenate([jnp.where(low, t[0], 0.0), jnp.where(low, t[2], 0.0)], axis=0)
            right = jnp.concatenate([jnp.where(low, 0.0, t[1]), jnp.where(low, 0.0, t[3])], axis=0)
            lhs = jnp.concatenate([left.astype(BF16), right.astype(BF16)], axis=1)
            outs.append(jnp.dot(lhs, four_blocks(blk, b), preferred_element_type=F32))
        for u in range(UNROLL):
            b = (i * UNROLL + u) * TOGETHER
            upper, lower = outs[u][0:8, 0:128], outs[u][8:16, 128:256]
            add_rows(acc, tile_ref[b], jnp.where(low, upper, 0.0))
            add_rows(acc, tile_ref[b + 1], jnp.where(low, 0.0, upper))
            add_rows(acc, tile_ref[b + 2], jnp.where(low, lower, 0.0))
            add_rows(acc, tile_ref[b + 3], jnp.where(low, 0.0, lower))
        return carry

    lax.fori_loop(0, blk.shape[0] // (TOGETHER * UNROLL), body, 0)


def tiles_of(x_shape):
    wide = x_shape[1] // 128
    return [(r, c, slice(c * 128, c * 128 + 128)) for r in range(x_shape[0]) for c in range(wide)]


def load_pixels(value, pix):
    wide = value.shape[1] // 128
    for r, c, columns in tiles_of(value.shape):
        pix[r * wide + c : r * wide + c + 1] = value[r : r + 1, columns]


def moved_by(x, back):
    wide = x.shape[1] // 128
    rows = back.shape[0]
    columns = []
    for c in range(wide):
        own = pl.ds(c, rows // wide, stride=wide)
        columns.append(back[own, 0, :] + back[own, 4, :])
    return x - 0.8 * jnp.concatenate(columns, axis=1)


def store_rays(place_ref, sino_ref, acc, total, o_ref):
    total[0 : acc.shape[0]] = acc[:, 0, :] + acc[:, 4, :]
    own = sino_ref.shape[0]
    mine = pl.ds(pl.multiple_of(place_ref[1] * own, own), own)
    for z in range(sino_ref.shape[1]):

        @pl.when(place_ref[0] == z)
        def _():
            total[mine] = total[mine] - sino_ref[:, z, :]

    o_ref[...] = total[0 : acc.shape[0]].astype(o_ref.dtype)


def project_kernel(place_ref, ray_ref, tile_ref, x_ref, sino_ref, blk, o_ref, pix, acc, total):
    load_pixels(x_ref[...], pix)
    acc[...] = jnp.zeros_like(acc)
    project_blocks(ray_ref, tile_ref, pix, blk, acc)
    store_rays(place_ref, sino_ref, acc, total, o_ref)


def project(place, ray_index, tile_index, x, sinogram, blocks, ray_total):
    tiles = x.size // 128
    return pl.pallas_call(
        project_kernel,
        out_shape=jax.ShapeDtypeStruct((ray_total, 128), BF16),
        in_specs=[in_smem()] * 3 + [in_vmem()] * 3,
        out_specs=in_vmem(),
        scratch_shapes=[
            pltpu.VMEM((tiles + 8, 128), F32),
            pltpu.VMEM((ray_total, 8, 128), F32),
            pltpu.VMEM((ray_total + 8, 128), F32),
        ],
        compiler_params=params(),
        name="project",
    )(place, ray_index, tile_index, x, sinogram, blocks)


def back_project_kernel(
    place_ref, ray_ref, tile_ref, r_ref, x_ref, sino_ref, blk, x_out, o_ref, res, pix, back, acc
):
    res[0 : r_ref.shape[0]] = r_ref[...].astype(F32)
    back[...] = jnp.zeros_like(back)
    back_blocks(ray_ref, tile_ref, res, blk, back)
    moved = moved_by(x_ref[...], back)
    x_out[...] = moved
    load_pixels(moved, pix)
    acc[...] = jnp.zeros_like(acc)
    project_blocks(ray_ref, tile_ref, pix, blk, acc)
    store_rays(place_ref, sino_ref, acc, res, o_ref)


def back_project(place, ray_index, tile_index, residual, x, sinogram, blocks):
    ray_total = residual.shape[0]
    tiles = x.size // 128
    return pl.pallas_call(
        back_project_kernel,
        out_shape=(
            jax.ShapeDtypeStruct(x.shape, F32),
            jax.ShapeDtypeStruct(residual.shape, BF16),
        ),
        in_specs=[in_smem()] * 3 + [in_vmem()] * 4,
        out_specs=(in_vmem(), in_vmem()),
        scratch_shapes=[
            pltpu.VMEM((ray_total + 8, 128), F32),
            pltpu.VMEM((tiles + 8, 128), F32),
            pltpu.VMEM((tiles, 8, 128), F32),
            pltpu.VMEM((ray_total, 8, 128), F32),
        ],
        compiler_params=params(),
        name="back_project",
    )(place, ray_index, tile_index, residual, x, sinogram, blocks)


def back_kernel(ray_ref, tile_ref, r_ref, x_ref, start_ref, blk, o_ref, res, back):
    res[0 : r_ref.shape[0]] = r_ref[...].astype(F32)
    back[...] = jnp.zeros_like(back)
    back_blocks(ray_ref, tile_ref, res, blk, back)
    o_ref[...] = 2.0 * moved_by(x_ref[...], back) - start_ref[...]


def back_reflect(ray_index, tile_index, residual, x, start, blocks):
    ray_total = residual.shape[0]
    tiles = x.size // 128
    return pl.pallas_call(
        back_kernel,
        out_shape=jax.ShapeDtypeStruct(x.shape, F32),
        in_specs=[in_smem()] * 2 + [in_vmem()] * 4,
        out_specs=in_vmem(),
        scratch_shapes=[
            pltpu.VMEM((ray_total + 8, 128), F32),
            pltpu.VMEM((tiles, 8, 128), F32),
        ],
        compiler_params=params(),
        name="back_reflect",
    )(ray_index, tile_index, residual, x, start, blocks)


def lanes(parts, count, height, width):
    empty = jnp.zeros((height, width), F32)
    return jnp.concatenate([parts.get(n, empty) for n in range(count)], axis=1)


def slice_band(first, hidden, last, o, zf, zh, zl, turn):
    turn[...] = jnp.zeros_like(turn)
    for j in range(3):
        for z in range(4):
            near = {y: z - y + 1 for y in range(4) if 0 <= z - y + 1 < 3}
            n = j * 4 + z
            parts = {y: first[o, i, j : j + 1, :].astype(F32) for y, i in near.items()}
            turn[n : n + 1, 0:128] = lanes(parts, 4, 1, 32)
    zf[...] = jnp.transpose(turn[0:128, 0:128])[:, 0:16].astype(BF16)
    for layer in range(hidden.shape[1]):
        for j in range(3):
            for z in range(4):
                near = {y: z - y + 1 for y in range(4) if 0 <= z - y + 1 < 3}
                parts = {y: hidden[o, layer, i, j].astype(F32) for y, i in near.items()}
                turn[z * 32 : z * 32 + 32, 0:128] = lanes(parts, 4, 32, 32)
            zh[layer, :, j * 128 : j * 128 + 128] = jnp.transpose(turn[0:128, 0:128]).astype(BF16)
    rows = []
    for y in range(4):
        parts = {
            j * 4 + z: last[o, z - y + 1, j : j + 1, :].astype(F32)
            for j in range(3)
            for z in range(4)
            if 0 <= z - y + 1 < 3
        }
        rows.append(lanes(parts, 12, 1, 32))
    zl[...] = jnp.concatenate(rows + [jnp.zeros((4, 384), F32)], axis=0).astype(BF16)


def widen(zh, zl, zw, zm):
    for layer in range(zh.shape[0]):
        zw[layer, 0:128, 0:384] = zh[layer]
        zw[layer, 0:128, 384:512] = jnp.zeros((128, 128), BF16)
        zw[layer, 128:256, 0:128] = jnp.zeros((128, 128), BF16)
        zw[layer, 128:256, 128:512] = zh[layer]
    plain = zl[...].astype(F32)
    rows = []
    for z in range(4):
        for a in range(4):
            parts = {a + n: plain[z : z + 1, n * 128 : n * 128 + 128] for n in range(3)}
            rows.append(lanes(parts, 6, 1, 128))
    zm[...] = jnp.concatenate(rows, axis=0).astype(BF16)


def row_band(first, hidden, last, af, ah, al, turn):
    turn[...] = jnp.zeros_like(turn)
    for j in range(3):
        for y in range(SPAN + 2):
            parts = {m: first[0, y - m, j : j + 1, :].astype(F32) for m in range(SPAN) if 0 <= y - m < 3}
            n = j * (SPAN + 2) + y
            turn[n : n + 1] = lanes(parts, 8, 1, 32)
    af[...] = jnp.transpose(turn[0:128])[0 : SPAN * 32, 0:32].astype(BF16)
    for layer in range(hidden.shape[1]):
        for j in range(3):
            for y in range(SPAN + 2):
                parts = {m: hidden[0, layer, y - m, j].astype(F32) for m in range(SPAN) if 0 <= y - m < 3}
                turn[y * 32 : y * 32 + 32] = lanes(parts, 8, 32, 32)
            ah[layer, j] = jnp.transpose(turn[...])[0 : SPAN * 32].astype(BF16)
    for j in range(3):
        rows = []
        for m in range(SPAN):
            parts = {m + i: last[0, i, j : j + 1, :].astype(F32) for i in range(3)}
            rows.append(lanes(parts, 8, 1, 32))
        rows.append(jnp.zeros((2, 256), F32))
        al[j] = jnp.concatenate(rows, axis=0).astype(BF16)


def prepare_kernel(
    place_ref, before, cur, after, first, hidden, last, rim, zf, zh, zl, zw, zm, af, ah, al, turn
):
    depth = before.shape[1]
    rows = cur.shape[1]
    rim[:, 0:depth] = before[...].astype(BF16).astype(F32)
    rim[:, depth : depth + rows] = cur[...].astype(BF16).astype(F32)
    rim[:, depth + rows :] = after[...].astype(BF16).astype(F32)

    @pl.when(place_ref[0] == 1)
    def _():
        row_band(first, hidden, last, af, ah, al, turn)

    @pl.when(place_ref[0] == 2)
    def _():
        slice_band(first, hidden, last, 1, zf, zh, zl, turn)
        widen(zh, zl, zw, zm)

    @pl.when(place_ref[0] == 3)
    def _():
        slice_band(first, hidden, last, 2, zf, zh, zl, turn)


def prepare(place, before, current, after, first, hidden, last):
    layers = hidden.shape[1]
    slices, rows, columns = current.shape
    rim = jax.ShapeDtypeStruct((slices, rows + 2 * before.shape[1], columns), F32)
    shapes = [
        (128, 16),
        (layers, 128, 384),
        (8, 384),
        (layers, 256, 512),
        (16, 768),
        (SPAN * 32, 32),
        (layers, 3, SPAN * 32, 256),
        (3, 8, 256),
    ]
    return pl.pallas_call(
        prepare_kernel,
        out_shape=[rim] + [jax.ShapeDtypeStruct(s, BF16) for s in shapes],
        in_specs=[in_smem()] + [in_vmem()] * 6,
        out_specs=[in_vmem()] * 9,
        scratch_shapes=[pltpu.VMEM((256, 256), F32)],
        compiler_params=params(),
        name="prepare",
    )(place, before, current, after, first, hidden, last)


def side_by_side(value):
    columns = value.shape[1]
    place = lax.broadcasted_iota(jnp.int32, value.shape, 1)
    before = jnp.where(place == 0, 0.0, pltpu.roll(value, 1, axis=1))
    after = jnp.where(place == columns - 1, 0.0, pltpu.roll(value, columns - 1, axis=1))
    return before, value, after


def relu_rows(value, keep):
    value = jnp.maximum(value, 0.0)
    return value if keep is None else jnp.where(keep, value, 0.0)


def sagittal_piece(part, columns, rows, above, below, rim, wf, wh, wl, o_ref, ha, hb):
    width = wf.shape[0]
    depth = wh.shape[0] + 1
    across = slice(part * columns, (part + 1) * columns)

    def kept(layer, y):
        reach = depth - layer
        return above if y < reach else below if y >= reach + rows else None

    empty = jnp.zeros((4, columns), F32)
    for y in range(rows + 2 * depth):
        taps = [rim[:, y + j, across] for j in range(3)] + [empty]
        taps = jnp.concatenate(taps, axis=0).astype(BF16)
        value = jnp.dot(wf[...], taps, preferred_element_type=F32)
        ha[y * width : (y + 1) * width] = relu_rows(value, kept(0, y)).astype(BF16)
    source, target = ha, hb
    for layer in range(wh.shape[0]):
        for y in range(0, rows + 2 * (depth - 1 - layer), 2):
            value = jnp.dot(
                wh[layer], source[y * width : (y + 4) * width], preferred_element_type=F32
            )
            for k in range(2):
                part_k = value[k * width : (k + 1) * width]
                target[(y + k) * width : (y + k + 1) * width] = relu_rows(
                    part_k, kept(layer + 1, y + k)
                ).astype(BF16)
        source, target = target, source
    for y in range(0, rows, 4):
        net = jnp.dot(wl[...], source[y * width : (y + 6) * width], preferred_element_type=F32)
        for z in range(4):
            o_ref[z, y : y + 4, across] = net[z * 4 : z * 4 + 4]


def coronal_piece(start, count, depth, rim, wf, wh, wl, o_ref, h):
    columns = rim.shape[2]
    width = wf.shape[0]
    empty = jnp.zeros((4, columns), F32)
    values = []
    for r in range(count):
        taps = jnp.concatenate([*side_by_side(rim[:, depth + start + r, :]), empty], axis=0)
        values.append(jnp.dot(wf[...], taps.astype(BF16), preferred_element_type=F32))
    for layer in range(wh.shape[0] + 1):
        matrix = wh[layer] if layer < wh.shape[0] else wl[...]
        for r in range(count):
            for j, moved in enumerate(side_by_side(jnp.maximum(values[r], 0.0))):
                h[r, j * width : (j + 1) * width] = moved.astype(BF16)
            values[r] = jnp.dot(matrix, h[r], preferred_element_type=F32)
    for r in range(count):
        o_ref[:, start + r, :] = values[r][0:4]


def spans(rows):
    starts = list(range(0, rows - SPAN, SPAN))
    return starts + [rows - SPAN]


def axial_piece(z, rows, above, below, rim, wf, wh, wl, o_ref, ha, hb):
    channels = wh.shape[3] // (SPAN + 2)
    depth = wh.shape[0] + 1

    def put(target, layer, start, value):
        value = jnp.maximum(value, 0.0)
        reach = depth - layer
        parts = []
        for k in range(SPAN):
            part = value[k * channels : (k + 1) * channels]
            y = start + k
            if y < reach:
                part = jnp.where(above, part, 0.0)
            elif y >= reach + rows:
                part = jnp.where(below, part, 0.0)
            parts.append(part)
        value = jnp.concatenate(parts, axis=0)
        for j, moved in enumerate(side_by_side(value)):
            target[j, start * channels : (start + SPAN) * channels] = moved.astype(BF16)

    def over_columns(matrices, source, start):
        total = None
        for j in range(3):
            window = source[j, start * channels : (start + SPAN + 2) * channels]
            part = jnp.dot(matrices[j], window, preferred_element_type=F32)
            total = part if total is None else total + part
        return total

    around = side_by_side(rim[z])
    empty = jnp.zeros((SPAN + 2, rim.shape[2]), F32)
    for start in spans(rows + 2 * depth):
        taps = [moved[start : start + SPAN + 2] for moved in around] + [empty]
        taps = jnp.concatenate(taps, axis=0).astype(BF16)
        put(ha, 0, start, jnp.dot(wf[...], taps, preferred_element_type=F32))
    source, target = ha, hb
    for layer in range(wh.shape[0]):
        for start in spans(rows + 2 * (depth - 1 - layer)):
            put(target, layer + 1, start, over_columns(wh[layer], source, start))
        source, target = target, source
    for start in spans(rows):
        o_ref[z, start : start + SPAN] = over_columns(wl[...], source, start)[0:SPAN]


def piece_kernel(
    k, place_ref, net, rim, zf, zh, zl, zw, zm, af, ah, al, o_ref, sa, sb, ca, xa, xb
):
    rows = o_ref.shape[1]
    depth = (rim.shape[1] - rows) // 2
    above, below = place_ref[1] > 0, place_ref[1] < place_ref[2] - 1
    o_ref[...] = net[...]

    @pl.when(place_ref[0] == 1)
    def _():
        axial_piece(k, rows, above, below, rim, af, ah, al, o_ref, xa, xb)

    if k < 2:

        @pl.when(place_ref[0] == 2)
        def _():
            half = o_ref.shape[2] // 2
            sagittal_piece(k, half, rows, above, below, rim, zf, zw, zm, o_ref, sa, sb)

    @pl.when(place_ref[0] == 3)
    def _():
        coronal_piece(k * (rows // 4), rows // 4, depth, rim, zf, zh, zl, o_ref, ca)


def piece(k, place, net, prepared):
    slices, rows, columns = net.shape
    reach = rows + 6
    return pl.pallas_call(
        functools.partial(piece_kernel, k),
        out_shape=jax.ShapeDtypeStruct(net.shape, F32),
        in_specs=[in_smem()] + [in_vmem()] * (1 + len(prepared)),
        out_specs=in_vmem(),
        scratch_shapes=[pltpu.VMEM((reach * 128, columns // 2), BF16)] * 2
        + [pltpu.VMEM((rows // 4, 384, columns), BF16)]
        + [pltpu.VMEM((3, reach * 32, columns), BF16)] * 2,
        compiler_params=params(),
        name=f"piece_{k}",
    )(place, net, *prepared)


def swapped(groups, k):
    return [(g[n], g[(n + k) % len(g)]) for g in groups for n in range(len(g))]


def stage_groups(count):
    near = 4
    strided = 4
    far = count // (near * strided)
    at = lambda f, s, n: (f * strided + s) * near + n
    return [
        [[at(f, s, n) for f in range(far)] for s in range(strided) for n in range(near)],
        [[at(f, s, n) for s in range(strided)] for f in range(far) for n in range(near)],
        [[at(f, s, n) for n in range(near)] for f in range(far) for s in range(strided)],
    ]


def added_up(values, groups):
    total = values.astype(F32)
    for k in range(1, len(groups[0])):
        total = total + lax.ppermute(values, "tile", swapped(groups, k)).astype(F32)
    return total.astype(values.dtype)


def rims(cells, depth):
    agents, count = 4, lax.axis_size("tile")
    pairs = [(a * count + t, a * count + t + 1) for a in (1, 2) for t in range(count - 1)]
    both = ("agent", "tile")
    before = lax.ppermute(cells[:, cells.shape[1] - depth :], both, pairs)
    after = lax.ppermute(cells[:, 0:depth], both, [(b, a) for a, b in pairs])
    return before, after


def own_slice(current, agent_place):
    start = current[0]
    for k in range(1, current.shape[0]):
        got = lax.ppermute(current[k], "agent", [(0, k)])
        start = jnp.where(agent_place == k, got, start)
    return start


def per_device(
    states,
    sinogram,
    blocks,
    block_angle,
    block_detector,
    block_tile,
    conv_first,
    conv_hidden,
    conv_last,
):
    current = states[0]
    tile_count = lax.axis_size("tile")
    tile_place = lax.axis_index("tile")
    agent_place = lax.axis_index("agent")
    place = jnp.stack([agent_place, tile_place, jnp.int32(tile_count)]).astype(jnp.int32)
    ray_total = sinogram.shape[0] * tile_count
    ray_index = block_angle * (current.shape[2] // 128) + block_detector

    start = own_slice(current, agent_place)
    before, after = rims(current, conv_hidden.shape[1] + 2)
    sums = project(place, ray_index, block_tile, start, sinogram, blocks, ray_total)

    groups = stage_groups(tile_count)
    net = jnp.zeros_like(current)
    x_data = start
    prepared = None
    k = 0
    for step in range(DATA_STEPS):
        for n, group in enumerate(groups):
            tied = lax.optimization_barrier((sums, net, before, after))
            sums, net, before, after = tied
            if n == 0 and step == 0:
                prepared = prepare(place, before, current, after, conv_first, conv_hidden, conv_last)
            elif n > 0:
                net = piece(k, place, net, prepared)
                k += 1
            sums = added_up(sums, group)
        if step < DATA_STEPS - 1:
            x_data, sums = back_project(place, ray_index, block_tile, sums, x_data, sinogram, blocks)
    reflect_data = back_reflect(ray_index, block_tile, sums, x_data, start, blocks)

    sent = jnp.concatenate([reflect_data[None], current - 2.0 * net], axis=0).astype(BF16)
    everything = lax.all_gather(sent, "agent").astype(F32)
    reflect_data = everything[:, 0]
    average = (reflect_data + everything[1, 1:] + everything[2, 1:] + everything[3, 1:]) / 4.0
    own = jnp.where(agent_place == 0, 0.5 * (current - reflect_data), net)
    return (average + own)[None]


def solution(mesh):
    placed = (
        P("agent", None, "tile", None),
        P("tile", None, None),
        P("tile", None, None),
        P("tile"),
        P("tile"),
        P("tile"),
        P(),
        P(),
        P(),
    )
    return jax.shard_map(
        per_device,
        mesh=mesh,
        in_specs=placed,
        out_specs=P("agent", None, "tile", None),
        check_vma=False,
    )
```

```python
import functools

import jax
import jax.numpy as jnp
import numpy as np
from jax import lax
from jax.experimental import pallas as pl
from jax.experimental.pallas import tpu as pltpu
from jax.sharding import PartitionSpec as P

DATA_STEPS = 2
F32, BF16 = jnp.float32, jnp.bfloat16
VMEM_LIMIT = 32 << 20
TOGETHER = 4
UNROLL = 16
SPAN = 6


def params():
    return pltpu.CompilerParams(vmem_limit_bytes=VMEM_LIMIT)


def in_vmem():
    return pl.BlockSpec(memory_space=pltpu.VMEM)


def near(x):
    return pltpu.with_memory_space_constraint(x, pltpu.VMEM)


def in_smem():
    return pl.BlockSpec(memory_space=pltpu.SMEM)


def low_rows():
    return lax.broadcasted_iota(jnp.int32, (8, 128), 0) < 4


def four_blocks(blk, b):
    size = blk.shape[1]
    left = blk[pl.ds(b, 2)].reshape(2 * size, size)
    right = blk[pl.ds(b + 2, 2)].reshape(2 * size, size)
    return jnp.concatenate([left, right], axis=1)


def row(ref, index):
    return ref[pl.ds(index, 8, stride=0), :]


def add_rows(acc, index, value):
    acc[index] = acc[index] + value


def project_blocks(ray_of, tile_ref, pix, blk, acc, ready=None):
    low = low_rows()
    zero = jnp.zeros((8, 128), F32)

    def body(i, carry):
        if ready is not None:
            ready(i)
        outs = []
        for u in range(UNROLL):
            b = (i * UNROLL + u) * TOGETHER
            t = [row(pix, tile_ref[b + k]) for k in range(TOGETHER)]
            upper = jnp.concatenate([jnp.where(low, t[0], t[1]), zero], axis=0)
            lower = jnp.concatenate([zero, jnp.where(low, t[2], t[3])], axis=0)
            lhs = jnp.concatenate([upper.astype(BF16), lower.astype(BF16)], axis=1)
            outs.append(
                lax.dot_general(
                    lhs, four_blocks(blk, b), (((1,), (1,)), ((), ())), preferred_element_type=F32
                )
            )
        for u in range(UNROLL):
            b = (i * UNROLL + u) * TOGETHER
            out = outs[u]
            add_rows(acc, ray_of(b), jnp.where(low, out[0:8, 0:128], 0.0))
            add_rows(acc, ray_of(b + 1), jnp.where(low, 0.0, out[0:8, 128:256]))
            add_rows(acc, ray_of(b + 2), jnp.where(low, out[8:16, 0:128], 0.0))
            add_rows(acc, ray_of(b + 3), jnp.where(low, 0.0, out[8:16, 128:256]))
        return carry

    lax.fori_loop(0, blk.shape[0] // (TOGETHER * UNROLL), body, 0)


def back_blocks(ray_ref, tile_ref, res, blk, acc):
    low = low_rows()

    def body(i, carry):
        outs = []
        for u in range(UNROLL):
            b = (i * UNROLL + u) * TOGETHER
            t = [row(res, ray_ref[b + k]) for k in range(TOGETHER)]
            left = jnp.concatenate([jnp.where(low, t[0], 0.0), jnp.where(low, t[2], 0.0)], axis=0)
            right = jnp.concatenate([jnp.where(low, 0.0, t[1]), jnp.where(low, 0.0, t[3])], axis=0)
            lhs = jnp.concatenate([left.astype(BF16), right.astype(BF16)], axis=1)
            outs.append(jnp.dot(lhs, four_blocks(blk, b), preferred_element_type=F32))
        for u in range(UNROLL):
            b = (i * UNROLL + u) * TOGETHER
            upper, lower = outs[u][0:8, 0:128], outs[u][8:16, 128:256]
            add_rows(acc, tile_ref[b], jnp.where(low, upper, 0.0))
            add_rows(acc, tile_ref[b + 1], jnp.where(low, 0.0, upper))
            add_rows(acc, tile_ref[b + 2], jnp.where(low, lower, 0.0))
            add_rows(acc, tile_ref[b + 3], jnp.where(low, 0.0, lower))
        return carry

    lax.fori_loop(0, blk.shape[0] // (TOGETHER * UNROLL), body, 0)


def tiles_of(x_shape):
    wide = x_shape[1] // 128
    return [(r, c, slice(c * 128, c * 128 + 128)) for r in range(x_shape[0]) for c in range(wide)]


def load_pixels(value, pix):
    wide = value.shape[1] // 128
    for r, c, columns in tiles_of(value.shape):
        pix[r * wide + c : r * wide + c + 1] = value[r : r + 1, columns]


def moved_by(x, back):
    wide = x.shape[1] // 128
    rows = back.shape[0]
    columns = []
    for c in range(wide):
        own = pl.ds(c, rows // wide, stride=wide)
        columns.append(back[own, 0, :] + back[own, 4, :])
    return x - 0.8 * jnp.concatenate(columns, axis=1)


def store_rays(place_ref, sino_ref, acc, total, o_ref):
    total[0 : acc.shape[0]] = acc[:, 0, :] + acc[:, 4, :]
    own = sino_ref.shape[0]
    mine = pl.ds(pl.multiple_of(place_ref[1] * own, own), own)
    for z in range(sino_ref.shape[1]):

        @pl.when(place_ref[0] == z)
        def _():
            total[mine] = total[mine] - sino_ref[:, z, :]

    o_ref[...] = total[0 : acc.shape[0]].astype(o_ref.dtype)


def project_kernel(
    place_ref,
    angle_in,
    detector_in,
    tile_in,
    states_in,
    got_1,
    got_2,
    got_3,
    sino_in,
    blk_in,
    o_ref,
    start_ref,
    blk,
    angle,
    detector,
    tile,
    first_slice,
    sino,
    pix,
    acc,
    total,
    small_sems,
    block_sems,
):
    small = [
        pltpu.make_async_copy(source, target, small_sems.at[n])
        for n, (source, target) in enumerate(
            [
                (states_in.at[0, 0], first_slice),
                (angle_in, angle),
                (detector_in, detector),
                (tile_in, tile),
                (sino_in, sino),
            ]
        )
    ]
    for copy in small:
        copy.start()
    chunk = TOGETHER * UNROLL

    def chunk_copy(i):
        part = pl.ds(i * chunk, chunk)
        return pltpu.make_async_copy(blk_in.at[part], blk.at[part], block_sems.at[i])

    for i in range(blk.shape[0] // chunk):
        chunk_copy(i).start()
    acc[...] = jnp.zeros_like(acc)
    for copy in small:
        copy.wait()
    start_ref[...] = got_1[...] + got_2[...] + got_3[...]

    @pl.when(place_ref[0] == 0)
    def _():
        start_ref[...] = first_slice[...]

    load_pixels(start_ref[...], pix)
    wide = first_slice.shape[1] // 128
    project_blocks(
        lambda b: angle[b] * wide + detector[b],
        tile,
        pix,
        blk,
        acc,
        lambda i: chunk_copy(i).wait(),
    )
    store_rays(place_ref, sino, acc, total, o_ref)


def project(place, angle, detector, tile, states, got, sinogram, blocks, ray_total):
    shape = got[0].shape
    count = blocks.shape[0]
    far = pl.BlockSpec(memory_space=pltpu.HBM)
    stay = lambda x: pltpu.with_memory_space_constraint(x, pltpu.HBM)
    return pl.pallas_call(
        project_kernel,
        out_shape=(
            jax.ShapeDtypeStruct((ray_total, 128), BF16),
            jax.ShapeDtypeStruct(shape, F32),
            pltpu.VMEM(blocks.shape, BF16),
        ),
        in_specs=[in_smem()] + [far] * 4 + [in_vmem()] * 3 + [far] * 2,
        out_specs=(in_vmem(),) * 3,
        scratch_shapes=[
            pltpu.SMEM((count,), jnp.int32),
            pltpu.SMEM((count,), jnp.int32),
            pltpu.SMEM((count,), jnp.int32),
            pltpu.VMEM(shape, F32),
            pltpu.VMEM(sinogram.shape, F32),
            pltpu.VMEM((shape[0] * shape[1] // 128 + 8, 128), F32),
            pltpu.VMEM((ray_total, 8, 128), F32),
            pltpu.VMEM((ray_total + 8, 128), F32),
            pltpu.SemaphoreType.DMA((5,)),
            pltpu.SemaphoreType.DMA((count // (TOGETHER * UNROLL),)),
        ],
        compiler_params=params(),
        name="project",
    )(
        place,
        stay(angle),
        stay(detector),
        stay(tile),
        stay(states),
        *got,
        stay(sinogram),
        stay(blocks),
    )


def back_project_kernel(
    place_ref, ray_ref, tile_ref, r_ref, x_ref, sino_ref, blk, x_out, o_ref, res, pix, back, acc
):
    res[0 : r_ref.shape[0]] = r_ref[...].astype(F32)
    back[...] = jnp.zeros_like(back)
    back_blocks(ray_ref, tile_ref, res, blk, back)
    moved = moved_by(x_ref[...], back)
    x_out[...] = moved
    load_pixels(moved, pix)
    acc[...] = jnp.zeros_like(acc)
    project_blocks(lambda b: ray_ref[b], tile_ref, pix, blk, acc)
    store_rays(place_ref, sino_ref, acc, res, o_ref)


def back_project(place, ray_index, tile_index, residual, x, sinogram, blocks):
    ray_total = residual.shape[0]
    tiles = x.size // 128
    return pl.pallas_call(
        back_project_kernel,
        out_shape=(
            jax.ShapeDtypeStruct(x.shape, F32),
            jax.ShapeDtypeStruct(residual.shape, BF16),
        ),
        in_specs=[in_smem()] * 3 + [in_vmem()] * 4,
        out_specs=(in_vmem(), in_vmem()),
        scratch_shapes=[
            pltpu.VMEM((ray_total + 8, 128), F32),
            pltpu.VMEM((tiles + 8, 128), F32),
            pltpu.VMEM((tiles, 8, 128), F32),
            pltpu.VMEM((ray_total, 8, 128), F32),
        ],
        compiler_params=params(),
        name="back_project",
    )(place, ray_index, tile_index, residual, x, sinogram, near(blocks))


def back_kernel(ray_ref, tile_ref, r_ref, x_ref, start_ref, cur_ref, net_ref, blk, o_ref, res, back):
    res[0 : r_ref.shape[0]] = r_ref[...].astype(F32)
    back[...] = jnp.zeros_like(back)
    for z in range(net_ref.shape[0]):
        o_ref[z + 1] = (cur_ref[z] - 2.0 * net_ref[z]).astype(o_ref.dtype)
    back_blocks(ray_ref, tile_ref, res, blk, back)
    o_ref[0] = (2.0 * moved_by(x_ref[...], back) - start_ref[...]).astype(o_ref.dtype)


def back_reflect(ray_index, tile_index, residual, x, start, current, net, blocks):
    ray_total = residual.shape[0]
    tiles = x.size // 128
    return pl.pallas_call(
        back_kernel,
        out_shape=jax.ShapeDtypeStruct((1 + net.shape[0], *x.shape), BF16),
        in_specs=[in_smem()] * 2 + [in_vmem()] * 6,
        out_specs=in_vmem(),
        scratch_shapes=[
            pltpu.VMEM((ray_total + 8, 128), F32),
            pltpu.VMEM((tiles, 8, 128), F32),
        ],
        compiler_params=params(),
        name="back_reflect",
    )(ray_index, tile_index, residual, x, start, current, net, near(blocks))


def finish_kernel(place_ref, all_ref, cur_ref, net_ref, o_ref):
    for z in range(o_ref.shape[0]):
        data = all_ref[z, 0].astype(F32)
        total = data
        for k in range(1, all_ref.shape[0]):
            total = total + all_ref[k, 1 + z].astype(F32)

        @pl.when(place_ref[0] == 0)
        def _():
            o_ref[z] = 0.25 * total + 0.5 * (cur_ref[z] - data)

        @pl.when(place_ref[0] != 0)
        def _():
            o_ref[z] = 0.25 * total + net_ref[z]


def finish(place, everything, current, net):
    return pl.pallas_call(
        finish_kernel,
        out_shape=jax.ShapeDtypeStruct(current.shape, F32),
        in_specs=[in_smem()] + [in_vmem()] * 3,
        out_specs=in_vmem(),
        compiler_params=params(),
        name="finish",
    )(place, everything, current, net)


def lanes(parts, count, height, width):
    empty = jnp.zeros((height, width), F32)
    return jnp.concatenate([parts.get(n, empty) for n in range(count)], axis=1)


def slice_band(first, hidden, last, o, zf, zh, zl, turn):
    turn[...] = jnp.zeros_like(turn)
    for j in range(3):
        for z in range(4):
            near = {y: z - y + 1 for y in range(4) if 0 <= z - y + 1 < 3}
            n = j * 4 + z
            parts = {y: first[o, i, j : j + 1, :].astype(F32) for y, i in near.items()}
            turn[n : n + 1, 0:128] = lanes(parts, 4, 1, 32)
    zf[...] = jnp.transpose(turn[0:128, 0:128])[:, 0:16].astype(BF16)
    for layer in range(hidden.shape[1]):
        for j in range(3):
            for z in range(4):
                near = {y: z - y + 1 for y in range(4) if 0 <= z - y + 1 < 3}
                parts = {y: hidden[o, layer, i, j].astype(F32) for y, i in near.items()}
                turn[z * 32 : z * 32 + 32, 0:128] = lanes(parts, 4, 32, 32)
            zh[layer, :, j * 128 : j * 128 + 128] = jnp.transpose(turn[0:128, 0:128]).astype(BF16)
    rows = []
    for y in range(4):
        parts = {
            j * 4 + z: last[o, z - y + 1, j : j + 1, :].astype(F32)
            for j in range(3)
            for z in range(4)
            if 0 <= z - y + 1 < 3
        }
        rows.append(lanes(parts, 12, 1, 32))
    zl[...] = jnp.concatenate(rows + [jnp.zeros((4, 384), F32)], axis=0).astype(BF16)


def widen(zh, zl, zw, zm):
    for layer in range(zh.shape[0]):
        zw[layer, 0:128, 0:384] = zh[layer]
        zw[layer, 0:128, 384:512] = jnp.zeros((128, 128), BF16)
        zw[layer, 128:256, 0:128] = jnp.zeros((128, 128), BF16)
        zw[layer, 128:256, 128:512] = zh[layer]
    plain = zl[...].astype(F32)
    rows = []
    for z in range(4):
        for a in range(4):
            parts = {a + n: plain[z : z + 1, n * 128 : n * 128 + 128] for n in range(3)}
            rows.append(lanes(parts, 6, 1, 128))
    zm[...] = jnp.concatenate(rows, axis=0).astype(BF16)


def row_band(first, hidden, last, af, ah, al, turn):
    turn[...] = jnp.zeros_like(turn)
    for j in range(3):
        for y in range(SPAN + 2):
            parts = {m: first[0, y - m, j : j + 1, :].astype(F32) for m in range(SPAN) if 0 <= y - m < 3}
            n = j * (SPAN + 2) + y
            turn[n : n + 1] = lanes(parts, 8, 1, 32)
    af[...] = jnp.transpose(turn[0:128])[0 : SPAN * 32, 0:32].astype(BF16)
    for layer in range(hidden.shape[1]):
        for j in range(3):
            for y in range(SPAN + 2):
                parts = {m: hidden[0, layer, y - m, j].astype(F32) for m in range(SPAN) if 0 <= y - m < 3}
                turn[y * 32 : y * 32 + 32] = lanes(parts, 8, 32, 32)
            ah[layer, j] = jnp.transpose(turn[...])[0 : SPAN * 32].astype(BF16)
    for j in range(3):
        rows = []
        for m in range(SPAN):
            parts = {m + i: last[0, i, j : j + 1, :].astype(F32) for i in range(3)}
            rows.append(lanes(parts, 8, 1, 32))
        rows.append(jnp.zeros((2, 256), F32))
        al[j] = jnp.concatenate(rows, axis=0).astype(BF16)


def prepare_kernel(
    place_ref, before, cur, after, first, hidden, last, rim, zf, zh, zl, zw, zm, af, ah, al, turn
):
    depth = before.shape[1]
    rows = cur.shape[1]
    rim[:, 0:depth] = before[...].astype(BF16).astype(F32)
    rim[:, depth : depth + rows] = cur[...].astype(BF16).astype(F32)
    rim[:, depth + rows :] = after[...].astype(BF16).astype(F32)

    @pl.when(place_ref[0] == 1)
    def _():
        row_band(first, hidden, last, af, ah, al, turn)

    @pl.when(place_ref[0] == 2)
    def _():
        slice_band(first, hidden, last, 1, zf, zh, zl, turn)
        widen(zh, zl, zw, zm)

    @pl.when(place_ref[0] == 3)
    def _():
        slice_band(first, hidden, last, 2, zf, zh, zl, turn)


def prepare(place, rim, current, first, hidden, last):
    before, after = rim
    layers = hidden.shape[1]
    slices, rows, columns = current.shape
    whole = jax.ShapeDtypeStruct((slices, rows + 2 * before.shape[1], columns), F32)
    shapes = [
        (128, 16),
        (layers, 128, 384),
        (8, 384),
        (layers, 256, 512),
        (16, 768),
        (SPAN * 32, 32),
        (layers, 3, SPAN * 32, 256),
        (3, 8, 256),
    ]
    return pl.pallas_call(
        prepare_kernel,
        out_shape=[whole] + [jax.ShapeDtypeStruct(s, BF16) for s in shapes],
        in_specs=[in_smem()] + [in_vmem()] * 6,
        out_specs=[in_vmem()] * 9,
        scratch_shapes=[pltpu.VMEM((256, 256), F32)],
        compiler_params=params(),
        name="prepare",
    )(place, before, current, after, first, hidden, last)


def side_by_side(value):
    columns = value.shape[1]
    place = lax.broadcasted_iota(jnp.int32, value.shape, 1)
    before = jnp.where(place == 0, 0.0, pltpu.roll(value, 1, axis=1))
    after = jnp.where(place == columns - 1, 0.0, pltpu.roll(value, columns - 1, axis=1))
    return before, value, after


def relu_rows(value, keep):
    value = jnp.maximum(value, 0.0)
    return value if keep is None else jnp.where(keep, value, 0.0)


def sagittal_piece(part, columns, rows, above, below, rim, wf, wh, wl, o_ref, ha, hb):
    width = wf.shape[0]
    depth = wh.shape[0] + 1
    across = slice(part * columns, (part + 1) * columns)

    def kept(layer, y):
        reach = depth - layer
        return above if y < reach else below if y >= reach + rows else None

    empty = jnp.zeros((4, columns), F32)
    for y in range(rows + 2 * depth):
        taps = [rim[:, y + j, across] for j in range(3)] + [empty]
        taps = jnp.concatenate(taps, axis=0).astype(BF16)
        value = jnp.dot(wf[...], taps, preferred_element_type=F32)
        ha[y * width : (y + 1) * width] = relu_rows(value, kept(0, y)).astype(BF16)
    source, target = ha, hb
    for layer in range(wh.shape[0]):
        for y in range(0, rows + 2 * (depth - 1 - layer), 2):
            value = jnp.dot(
                wh[layer], source[y * width : (y + 4) * width], preferred_element_type=F32
            )
            for k in range(2):
                part_k = value[k * width : (k + 1) * width]
                target[(y + k) * width : (y + k + 1) * width] = relu_rows(
                    part_k, kept(layer + 1, y + k)
                ).astype(BF16)
        source, target = target, source
    for y in range(0, rows, 4):
        net = jnp.dot(wl[...], source[y * width : (y + 6) * width], preferred_element_type=F32)
        for z in range(4):
            o_ref[z, y : y + 4, across] = net[z * 4 : z * 4 + 4]


def coronal_piece(start, count, depth, rim, wf, wh, wl, o_ref, h):
    columns = rim.shape[2]
    width = wf.shape[0]
    empty = jnp.zeros((4, columns), F32)
    values = []
    for r in range(count):
        taps = jnp.concatenate([*side_by_side(rim[:, depth + start + r, :]), empty], axis=0)
        values.append(jnp.dot(wf[...], taps.astype(BF16), preferred_element_type=F32))
    for layer in range(wh.shape[0] + 1):
        matrix = wh[layer] if layer < wh.shape[0] else wl[...]
        for r in range(count):
            for j, moved in enumerate(side_by_side(jnp.maximum(values[r], 0.0))):
                h[r, j * width : (j + 1) * width] = moved.astype(BF16)
            values[r] = jnp.dot(matrix, h[r], preferred_element_type=F32)
    for r in range(count):
        o_ref[:, start + r, :] = values[r][0:4]


def spans(rows):
    starts = list(range(0, rows - SPAN, SPAN))
    return starts + [rows - SPAN]


def axial_piece(z, rows, above, below, rim, wf, wh, wl, o_ref, ha, hb):
    channels = wh.shape[3] // (SPAN + 2)
    depth = wh.shape[0] + 1

    def put(target, layer, start, value):
        value = jnp.maximum(value, 0.0)
        reach = depth - layer
        parts = []
        for k in range(SPAN):
            part = value[k * channels : (k + 1) * channels]
            y = start + k
            if y < reach:
                part = jnp.where(above, part, 0.0)
            elif y >= reach + rows:
                part = jnp.where(below, part, 0.0)
            parts.append(part)
        value = jnp.concatenate(parts, axis=0)
        for j, moved in enumerate(side_by_side(value)):
            target[j, start * channels : (start + SPAN) * channels] = moved.astype(BF16)

    def over_columns(matrices, source, start):
        total = None
        for j in range(3):
            window = source[j, start * channels : (start + SPAN + 2) * channels]
            part = jnp.dot(matrices[j], window, preferred_element_type=F32)
            total = part if total is None else total + part
        return total

    around = side_by_side(rim[z])
    empty = jnp.zeros((SPAN + 2, rim.shape[2]), F32)
    for start in spans(rows + 2 * depth):
        taps = [moved[start : start + SPAN + 2] for moved in around] + [empty]
        taps = jnp.concatenate(taps, axis=0).astype(BF16)
        put(ha, 0, start, jnp.dot(wf[...], taps, preferred_element_type=F32))
    source, target = ha, hb
    for layer in range(wh.shape[0]):
        for start in spans(rows + 2 * (depth - 1 - layer)):
            put(target, layer + 1, start, over_columns(wh[layer], source, start))
        source, target = target, source
    for start in spans(rows):
        o_ref[z, start : start + SPAN] = over_columns(wl[...], source, start)[0:SPAN]


def piece_kernel(
    k, place_ref, blk, net, rim, zf, zh, zl, zw, zm, af, ah, al, o_ref, sa, sb, ca, xa, xb
):
    rows = o_ref.shape[1]
    depth = (rim.shape[1] - rows) // 2
    above, below = place_ref[1] > 0, place_ref[1] < place_ref[2] - 1
    o_ref[...] = net[...]

    @pl.when(place_ref[0] == 1)
    def _():
        axial_piece(k, rows, above, below, rim, af, ah, al, o_ref, xa, xb)

    if k < 2:

        @pl.when(place_ref[0] == 2)
        def _():
            half = o_ref.shape[2] // 2
            sagittal_piece(k, half, rows, above, below, rim, zf, zw, zm, o_ref, sa, sb)

    @pl.when(place_ref[0] == 3)
    def _():
        coronal_piece(k * (rows // 4), rows // 4, depth, rim, zf, zh, zl, o_ref, ca)


def piece(k, place, blocks, net, prepared):
    slices, rows, columns = net.shape
    reach = rows + 6
    return pl.pallas_call(
        functools.partial(piece_kernel, k),
        out_shape=jax.ShapeDtypeStruct(net.shape, F32),
        in_specs=[in_smem()] + [in_vmem()] * (2 + len(prepared)),
        out_specs=in_vmem(),
        scratch_shapes=[pltpu.VMEM((reach * 128, columns // 2), BF16)] * 2
        + [pltpu.VMEM((rows // 4, 384, columns), BF16)]
        + [pltpu.VMEM((3, reach * 32, columns), BF16)] * 2,
        compiler_params=params(),
        name=f"piece_{k}",
    )(place, near(blocks), net, *prepared)


def swapped(groups, k):
    return [(g[n], g[(n + k) % len(g)]) for g in groups for n in range(len(g))]


def stage_groups(count):
    near = 4
    strided = 4
    far = count // (near * strided)
    at = lambda f, s, n: (f * strided + s) * near + n
    return [
        [[at(f, s, n) for f in range(far)] for s in range(strided) for n in range(near)],
        [[at(f, s, n) for s in range(strided)] for f in range(far) for n in range(near)],
        [[at(f, s, n) for n in range(near)] for f in range(far) for s in range(strided)],
    ]


def added_up(values, groups):
    total = values.astype(F32)
    for k in range(1, len(groups[0])):
        total = total + lax.ppermute(values, "tile", swapped(groups, k)).astype(F32)
    return total.astype(values.dtype)


def rims(cells, depth):
    agents, count = 4, lax.axis_size("tile")
    pairs = [(a * count + t, a * count + t + 1) for a in (1, 2) for t in range(count - 1)]
    both = ("agent", "tile")
    before = lax.ppermute(cells[:, cells.shape[1] - depth :], both, pairs)
    after = lax.ppermute(cells[:, 0:depth], both, [(b, a) for a, b in pairs])
    return before, after


def slices_sent(current):
    return [lax.ppermute(current[k], "agent", [(0, k)]) for k in range(1, current.shape[0])]


def per_device(
    states,
    sinogram,
    blocks,
    block_angle,
    block_detector,
    block_tile,
    conv_first,
    conv_hidden,
    conv_last,
):
    current = states[0]
    tile_count = lax.axis_size("tile")
    tile_place = lax.axis_index("tile")
    agent_place = lax.axis_index("agent")
    place = jnp.stack([agent_place, tile_place, jnp.int32(tile_count)]).astype(jnp.int32)
    ray_total = sinogram.shape[0] * tile_count
    ray_index = block_angle * (current.shape[2] // 128) + block_detector

    got = slices_sent(current)
    sums, start, blocks_here = project(
        place, block_angle, block_detector, block_tile, states, got, sinogram, blocks, ray_total
    )

    groups = stage_groups(tile_count)
    net = jnp.zeros_like(current)
    x_data = start
    prepared, rim, k = None, None, 0
    for step in range(DATA_STEPS):
        for n, group in enumerate(groups):
            sums, net = lax.optimization_barrier((sums, net))
            if n == 0 and step == 0:
                around, sums = lax.optimization_barrier((current, sums))
                rim = rims(around, conv_hidden.shape[1] + 2)
            elif n > 0:
                if prepared is None:
                    prepared = prepare(place, rim, current, conv_first, conv_hidden, conv_last)
                net = piece(k, place, blocks_here, net, prepared)
                k += 1
            sums = added_up(sums, group)
        if step < DATA_STEPS - 1:
            x_data, sums = back_project(
                place, ray_index, block_tile, sums, x_data, sinogram, blocks_here
            )
    sent = back_reflect(ray_index, block_tile, sums, x_data, start, current, net, blocks_here)
    everything = lax.all_gather(sent, "agent")
    return finish(place, everything, current, net)[None]


def solution(mesh):
    placed = (
        P("agent", None, "tile", None),
        P("tile", None, None),
        P("tile", None, None),
        P("tile"),
        P("tile"),
        P("tile"),
        P(),
        P(),
        P(),
    )
    return jax.shard_map(
        per_device,
        mesh=mesh,
        in_specs=placed,
        out_specs=P("agent", None, "tile", None),
        check_vma=False,
    )
```

```python
import functools

import jax
import jax.numpy as jnp
import numpy as np
from jax import lax
from jax.experimental import pallas as pl
from jax.experimental.pallas import tpu as pltpu
from jax.sharding import PartitionSpec as P

DATA_STEPS = 2
F32, BF16 = jnp.float32, jnp.bfloat16
VMEM_LIMIT = 32 << 20
TOGETHER = 4
UNROLL = 16
CHUNK = 64
SPAN = 6


def params():
    return pltpu.CompilerParams(vmem_limit_bytes=VMEM_LIMIT)


def in_vmem():
    return pl.BlockSpec(memory_space=pltpu.VMEM)


def near(x):
    return pltpu.with_memory_space_constraint(x, pltpu.VMEM)


def in_smem():
    return pl.BlockSpec(memory_space=pltpu.SMEM)


def low_rows():
    return lax.broadcasted_iota(jnp.int32, (8, 128), 0) < 4


def four_blocks(blk, b):
    size = blk.shape[1]
    left = blk[pl.ds(b, 2)].reshape(2 * size, size)
    right = blk[pl.ds(b + 2, 2)].reshape(2 * size, size)
    return jnp.concatenate([left, right], axis=1)


def row(ref, index):
    return ref[pl.ds(index, 8, stride=0), :]


def add_rows(acc, index, value):
    acc[index] = acc[index] + value


def project_blocks(ray_of, tile_ref, pix, blk, acc, ready=None):
    low = low_rows()
    zero = jnp.zeros((8, 128), F32)

    def body(i, carry):
        if ready is not None:
            ready(i)
        outs = []
        for u in range(UNROLL):
            b = (i * UNROLL + u) * TOGETHER
            t = [row(pix, tile_ref[b + k]) for k in range(TOGETHER)]
            upper = jnp.concatenate([jnp.where(low, t[0], t[1]), zero], axis=0)
            lower = jnp.concatenate([zero, jnp.where(low, t[2], t[3])], axis=0)
            lhs = jnp.concatenate([upper.astype(BF16), lower.astype(BF16)], axis=1)
            outs.append(
                lax.dot_general(
                    lhs, four_blocks(blk, b), (((1,), (1,)), ((), ())), preferred_element_type=F32
                )
            )
        for u in range(UNROLL):
            b = (i * UNROLL + u) * TOGETHER
            out = outs[u]
            add_rows(acc, ray_of(b), jnp.where(low, out[0:8, 0:128], 0.0))
            add_rows(acc, ray_of(b + 1), jnp.where(low, 0.0, out[0:8, 128:256]))
            add_rows(acc, ray_of(b + 2), jnp.where(low, out[8:16, 0:128], 0.0))
            add_rows(acc, ray_of(b + 3), jnp.where(low, 0.0, out[8:16, 128:256]))
        return carry

    lax.fori_loop(0, blk.shape[0] // (TOGETHER * UNROLL), body, 0)


def back_blocks(ray_ref, tile_ref, res, blk, acc):
    low = low_rows()

    def body(i, carry):
        outs = []
        for u in range(UNROLL):
            b = (i * UNROLL + u) * TOGETHER
            t = [row(res, ray_ref[b + k]) for k in range(TOGETHER)]
            left = jnp.concatenate([jnp.where(low, t[0], 0.0), jnp.where(low, t[2], 0.0)], axis=0)
            right = jnp.concatenate([jnp.where(low, 0.0, t[1]), jnp.where(low, 0.0, t[3])], axis=0)
            lhs = jnp.concatenate([left.astype(BF16), right.astype(BF16)], axis=1)
            outs.append(jnp.dot(lhs, four_blocks(blk, b), preferred_element_type=F32))
        for u in range(UNROLL):
            b = (i * UNROLL + u) * TOGETHER
            upper, lower = outs[u][0:8, 0:128], outs[u][8:16, 128:256]
            add_rows(acc, tile_ref[b], jnp.where(low, upper, 0.0))
            add_rows(acc, tile_ref[b + 1], jnp.where(low, 0.0, upper))
            add_rows(acc, tile_ref[b + 2], jnp.where(low, lower, 0.0))
            add_rows(acc, tile_ref[b + 3], jnp.where(low, 0.0, lower))
        return carry

    lax.fori_loop(0, blk.shape[0] // (TOGETHER * UNROLL), body, 0)


def tiles_of(x_shape):
    wide = x_shape[1] // 128
    return [(r, c, slice(c * 128, c * 128 + 128)) for r in range(x_shape[0]) for c in range(wide)]


def load_pixels(value, pix):
    wide = value.shape[1] // 128
    for r, c, columns in tiles_of(value.shape):
        pix[r * wide + c : r * wide + c + 1] = value[r : r + 1, columns]


def moved_by(x, back):
    wide = x.shape[1] // 128
    rows = back.shape[0]
    columns = []
    for c in range(wide):
        own = pl.ds(c, rows // wide, stride=wide)
        columns.append(back[own, 0, :] + back[own, 4, :])
    return x - 0.8 * jnp.concatenate(columns, axis=1)


def store_rays(place_ref, sino_ref, acc, total, o_ref):
    total[0 : acc.shape[0]] = acc[:, 0, :] + acc[:, 4, :]
    own = sino_ref.shape[0]
    mine = pl.ds(pl.multiple_of(place_ref[1] * own, own), own)
    for z in range(sino_ref.shape[1]):

        @pl.when(place_ref[0] == z)
        def _():
            total[mine] = total[mine] - sino_ref[:, z, :]

    o_ref[...] = total[0 : acc.shape[0]].astype(o_ref.dtype)


def project_kernel(
    place_ref,
    angle_in,
    detector_in,
    tile_in,
    states_in,
    got_1,
    got_2,
    got_3,
    sino_in,
    blk_in,
    o_ref,
    start_ref,
    blk,
    angle,
    detector,
    tile,
    first_slice,
    sino,
    pix,
    acc,
    total,
    small_sems,
    block_sems,
):
    small = [
        pltpu.make_async_copy(source, target, small_sems.at[n])
        for n, (source, target) in enumerate(
            [
                (states_in.at[0, 0], first_slice),
                (angle_in, angle),
                (detector_in, detector),
                (tile_in, tile),
                (sino_in, sino),
            ]
        )
    ]
    for copy in small:
        copy.start()
    chunk = CHUNK

    def chunk_copy(i):
        part = pl.ds(i * chunk, chunk)
        return pltpu.make_async_copy(blk_in.at[part], blk.at[part], block_sems.at[i])

    ahead = 2
    count = blk.shape[0] // chunk
    for i in range(ahead):
        chunk_copy(i).start()

    def ready(i):
        chunk_copy(i).wait()

        @pl.when(i + ahead < count)
        def _():
            chunk_copy(i + ahead).start()

    acc[...] = jnp.zeros_like(acc)
    for copy in small:
        copy.wait()
    for k, value in enumerate((first_slice, got_1, got_2, got_3)):

        @pl.when(place_ref[0] == k)
        def _():
            start_ref[...] = value[...]

    load_pixels(start_ref[...], pix)
    wide = first_slice.shape[1] // 128
    project_blocks(
        lambda b: angle[b] * wide + detector[b],
        tile,
        pix,
        blk,
        acc,
        ready,
    )
    store_rays(place_ref, sino, acc, total, o_ref)


def project(place, angle, detector, tile, states, got, sinogram, blocks, ray_total):
    shape = got[0].shape
    count = blocks.shape[0]
    far = pl.BlockSpec(memory_space=pltpu.HBM)
    stay = lambda x: pltpu.with_memory_space_constraint(x, pltpu.HBM)
    return pl.pallas_call(
        project_kernel,
        out_shape=(
            jax.ShapeDtypeStruct((ray_total, 128), BF16),
            jax.ShapeDtypeStruct(shape, F32),
            pltpu.VMEM(blocks.shape, BF16),
        ),
        in_specs=[in_smem()] + [far] * 4 + [in_vmem()] * 3 + [far] * 2,
        out_specs=(in_vmem(),) * 3,
        scratch_shapes=[
            pltpu.SMEM((count,), jnp.int32),
            pltpu.SMEM((count,), jnp.int32),
            pltpu.SMEM((count,), jnp.int32),
            pltpu.VMEM(shape, F32),
            pltpu.VMEM(sinogram.shape, F32),
            pltpu.VMEM((shape[0] * shape[1] // 128 + 8, 128), F32),
            pltpu.VMEM((ray_total, 8, 128), F32),
            pltpu.VMEM((ray_total + 8, 128), F32),
            pltpu.SemaphoreType.DMA((5,)),
            pltpu.SemaphoreType.DMA((count // CHUNK,)),
        ],
        compiler_params=params(),
        name="project",
    )(
        place,
        stay(angle),
        stay(detector),
        stay(tile),
        stay(states),
        *got,
        stay(sinogram),
        stay(blocks),
    )


def back_project_kernel(
    place_ref, ray_ref, tile_ref, r_ref, x_ref, sino_ref, blk, x_out, o_ref, res, pix, back, acc
):
    res[0 : r_ref.shape[0]] = r_ref[...].astype(F32)
    back[...] = jnp.zeros_like(back)
    back_blocks(ray_ref, tile_ref, res, blk, back)
    moved = moved_by(x_ref[...], back)
    x_out[...] = moved
    load_pixels(moved, pix)
    acc[...] = jnp.zeros_like(acc)
    project_blocks(lambda b: ray_ref[b], tile_ref, pix, blk, acc)
    store_rays(place_ref, sino_ref, acc, res, o_ref)


def back_project(place, ray_index, tile_index, residual, x, sinogram, blocks):
    ray_total = residual.shape[0]
    tiles = x.size // 128
    return pl.pallas_call(
        back_project_kernel,
        out_shape=(
            jax.ShapeDtypeStruct(x.shape, F32),
            jax.ShapeDtypeStruct(residual.shape, BF16),
        ),
        in_specs=[in_smem()] * 3 + [in_vmem()] * 4,
        out_specs=(in_vmem(), in_vmem()),
        scratch_shapes=[
            pltpu.VMEM((ray_total + 8, 128), F32),
            pltpu.VMEM((tiles + 8, 128), F32),
            pltpu.VMEM((tiles, 8, 128), F32),
            pltpu.VMEM((ray_total, 8, 128), F32),
        ],
        compiler_params=params(),
        name="back_project",
    )(place, ray_index, tile_index, residual, x, sinogram, near(blocks))


def back_kernel(ray_ref, tile_ref, r_ref, x_ref, start_ref, cur_ref, net_ref, blk, o_ref, res, back):
    res[0 : r_ref.shape[0]] = r_ref[...].astype(F32)
    back[...] = jnp.zeros_like(back)
    for z in range(net_ref.shape[0]):
        o_ref[z + 1] = (cur_ref[z] - 2.0 * net_ref[z]).astype(o_ref.dtype)
    back_blocks(ray_ref, tile_ref, res, blk, back)
    o_ref[0] = (2.0 * moved_by(x_ref[...], back) - start_ref[...]).astype(o_ref.dtype)


def back_reflect(ray_index, tile_index, residual, x, start, current, net, blocks):
    ray_total = residual.shape[0]
    tiles = x.size // 128
    return pl.pallas_call(
        back_kernel,
        out_shape=jax.ShapeDtypeStruct((1 + net.shape[0], *x.shape), BF16),
        in_specs=[in_smem()] * 2 + [in_vmem()] * 6,
        out_specs=in_vmem(),
        scratch_shapes=[
            pltpu.VMEM((ray_total + 8, 128), F32),
            pltpu.VMEM((tiles, 8, 128), F32),
        ],
        compiler_params=params(),
        name="back_reflect",
    )(ray_index, tile_index, residual, x, start, current, net, near(blocks))


def finish_kernel(place_ref, all_ref, cur_ref, net_ref, o_ref):
    for z in range(o_ref.shape[0]):
        data = all_ref[z, 0].astype(F32)
        total = data
        for k in range(1, all_ref.shape[0]):
            total = total + all_ref[k, 1 + z].astype(F32)

        @pl.when(place_ref[0] == 0)
        def _():
            o_ref[z] = 0.25 * total + 0.5 * (cur_ref[z] - data)

        @pl.when(place_ref[0] != 0)
        def _():
            o_ref[z] = 0.25 * total + net_ref[z]


def finish(place, everything, current, net):
    return pl.pallas_call(
        finish_kernel,
        out_shape=jax.ShapeDtypeStruct(current.shape, F32),
        in_specs=[in_smem()] + [in_vmem()] * 3,
        out_specs=in_vmem(),
        compiler_params=params(),
        name="finish",
    )(place, everything, current, net)


def lanes(parts, count, height, width):
    empty = jnp.zeros((height, width), F32)
    return jnp.concatenate([parts.get(n, empty) for n in range(count)], axis=1)


def slice_band(first, hidden, last, o, zf, zh, zl, turn):
    turn[...] = jnp.zeros_like(turn)
    for j in range(3):
        for z in range(4):
            near = {y: z - y + 1 for y in range(4) if 0 <= z - y + 1 < 3}
            n = j * 4 + z
            parts = {y: first[o, i, j : j + 1, :].astype(F32) for y, i in near.items()}
            turn[n : n + 1, 0:128] = lanes(parts, 4, 1, 32)
    zf[...] = jnp.transpose(turn[0:128, 0:128])[:, 0:16].astype(BF16)
    for layer in range(hidden.shape[1]):
        for j in range(3):
            for z in range(4):
                near = {y: z - y + 1 for y in range(4) if 0 <= z - y + 1 < 3}
                parts = {y: hidden[o, layer, i, j].astype(F32) for y, i in near.items()}
                turn[z * 32 : z * 32 + 32, 0:128] = lanes(parts, 4, 32, 32)
            zh[layer, :, j * 128 : j * 128 + 128] = jnp.transpose(turn[0:128, 0:128]).astype(BF16)
    rows = []
    for y in range(4):
        parts = {
            j * 4 + z: last[o, z - y + 1, j : j + 1, :].astype(F32)
            for j in range(3)
            for z in range(4)
            if 0 <= z - y + 1 < 3
        }
        rows.append(lanes(parts, 12, 1, 32))
    zl[...] = jnp.concatenate(rows + [jnp.zeros((4, 384), F32)], axis=0).astype(BF16)


def widen(zh, zl, zw, zm):
    for layer in range(zh.shape[0]):
        zw[layer, 0:128, 0:384] = zh[layer]
        zw[layer, 0:128, 384:512] = jnp.zeros((128, 128), BF16)
        zw[layer, 128:256, 0:128] = jnp.zeros((128, 128), BF16)
        zw[layer, 128:256, 128:512] = zh[layer]
    plain = zl[...].astype(F32)
    rows = []
    for z in range(4):
        for a in range(4):
            parts = {a + n: plain[z : z + 1, n * 128 : n * 128 + 128] for n in range(3)}
            rows.append(lanes(parts, 6, 1, 128))
    zm[...] = jnp.concatenate(rows, axis=0).astype(BF16)


def row_band(first, hidden, last, af, ah, al, turn):
    turn[...] = jnp.zeros_like(turn)
    for j in range(3):
        for y in range(SPAN + 2):
            parts = {m: first[0, y - m, j : j + 1, :].astype(F32) for m in range(SPAN) if 0 <= y - m < 3}
            n = j * (SPAN + 2) + y
            turn[n : n + 1] = lanes(parts, 8, 1, 32)
    af[...] = jnp.transpose(turn[0:128])[0 : SPAN * 32, 0:32].astype(BF16)
    for layer in range(hidden.shape[1]):
        for j in range(3):
            for y in range(SPAN + 2):
                parts = {m: hidden[0, layer, y - m, j].astype(F32) for m in range(SPAN) if 0 <= y - m < 3}
                turn[y * 32 : y * 32 + 32] = lanes(parts, 8, 32, 32)
            ah[layer, j] = jnp.transpose(turn[...])[0 : SPAN * 32].astype(BF16)
    for j in range(3):
        rows = []
        for m in range(SPAN):
            parts = {m + i: last[0, i, j : j + 1, :].astype(F32) for i in range(3)}
            rows.append(lanes(parts, 8, 1, 32))
        rows.append(jnp.zeros((2, 256), F32))
        al[j] = jnp.concatenate(rows, axis=0).astype(BF16)


def prepare_kernel(
    place_ref, got_1, got_2, got_3, cur, first, hidden, last, rim, zf, zh, zl, zw, zm, af, ah, al, turn
):
    slices, rows = cur.shape[0:2]
    depth = got_3.shape[0] // slices
    rim[:, depth : depth + rows] = cur[...].astype(BF16).astype(F32)

    def rims(before, after):
        for z in range(slices):
            part = slice(z * depth, z * depth + depth)
            rim[z, 0:depth] = before[part].astype(BF16).astype(F32)
            rim[z, depth + rows :] = after[part].astype(BF16).astype(F32)

    @pl.when(place_ref[0] == 1)
    def _():
        rims(got_2, got_3)

    @pl.when(place_ref[0] == 2)
    def _():
        rims(got_1, got_3)

    @pl.when(place_ref[0] == 1)
    def _():
        row_band(first, hidden, last, af, ah, al, turn)

    @pl.when(place_ref[0] == 2)
    def _():
        slice_band(first, hidden, last, 1, zf, zh, zl, turn)
        widen(zh, zl, zw, zm)

    @pl.when(place_ref[0] == 3)
    def _():
        slice_band(first, hidden, last, 2, zf, zh, zl, turn)


def prepare(place, got, current, first, hidden, last):
    layers = hidden.shape[1]
    slices, rows, columns = current.shape
    depth = got[0].shape[0] // slices
    whole = jax.ShapeDtypeStruct((slices, rows + 2 * depth, columns), F32)
    shapes = [
        (128, 16),
        (layers, 128, 384),
        (8, 384),
        (layers, 256, 512),
        (16, 768),
        (SPAN * 32, 32),
        (layers, 3, SPAN * 32, 256),
        (3, 8, 256),
    ]
    return pl.pallas_call(
        prepare_kernel,
        out_shape=[whole] + [jax.ShapeDtypeStruct(s, BF16) for s in shapes],
        in_specs=[in_smem()] + [in_vmem()] * 7,
        out_specs=[in_vmem()] * 9,
        scratch_shapes=[pltpu.VMEM((256, 256), F32)],
        compiler_params=params(),
        name="prepare",
    )(place, *got, current, first, hidden, last)


def side_by_side(value):
    columns = value.shape[1]
    place = lax.broadcasted_iota(jnp.int32, value.shape, 1)
    before = jnp.where(place == 0, 0.0, pltpu.roll(value, 1, axis=1))
    after = jnp.where(place == columns - 1, 0.0, pltpu.roll(value, columns - 1, axis=1))
    return before, value, after


def relu_rows(value, keep):
    value = jnp.maximum(value, 0.0)
    return value if keep is None else jnp.where(keep, value, 0.0)


def sagittal_piece(part, columns, rows, above, below, rim, wf, wh, wl, o_ref, ha, hb):
    width = wf.shape[0]
    depth = wh.shape[0] + 1
    across = slice(part * columns, (part + 1) * columns)

    def kept(layer, y):
        reach = depth - layer
        return above if y < reach else below if y >= reach + rows else None

    empty = jnp.zeros((4, columns), F32)
    for y in range(rows + 2 * depth):
        taps = [rim[:, y + j, across] for j in range(3)] + [empty]
        taps = jnp.concatenate(taps, axis=0).astype(BF16)
        value = jnp.dot(wf[...], taps, preferred_element_type=F32)
        ha[y * width : (y + 1) * width] = relu_rows(value, kept(0, y)).astype(BF16)
    source, target = ha, hb
    for layer in range(wh.shape[0]):
        for y in range(0, rows + 2 * (depth - 1 - layer), 2):
            value = jnp.dot(
                wh[layer], source[y * width : (y + 4) * width], preferred_element_type=F32
            )
            for k in range(2):
                part_k = value[k * width : (k + 1) * width]
                target[(y + k) * width : (y + k + 1) * width] = relu_rows(
                    part_k, kept(layer + 1, y + k)
                ).astype(BF16)
        source, target = target, source
    for y in range(0, rows, 4):
        net = jnp.dot(wl[...], source[y * width : (y + 6) * width], preferred_element_type=F32)
        for z in range(4):
            o_ref[z, y : y + 4, across] = net[z * 4 : z * 4 + 4]


def coronal_piece(start, count, depth, rim, wf, wh, wl, o_ref, h):
    columns = rim.shape[2]
    width = wf.shape[0]
    empty = jnp.zeros((4, columns), F32)
    values = []
    for r in range(count):
        taps = jnp.concatenate([*side_by_side(rim[:, depth + start + r, :]), empty], axis=0)
        values.append(jnp.dot(wf[...], taps.astype(BF16), preferred_element_type=F32))
    for layer in range(wh.shape[0] + 1):
        matrix = wh[layer] if layer < wh.shape[0] else wl[...]
        for r in range(count):
            for j, moved in enumerate(side_by_side(jnp.maximum(values[r], 0.0))):
                h[r, j * width : (j + 1) * width] = moved.astype(BF16)
            values[r] = jnp.dot(matrix, h[r], preferred_element_type=F32)
    for r in range(count):
        o_ref[:, start + r, :] = values[r][0:4]


def spans(rows):
    starts = list(range(0, rows - SPAN, SPAN))
    return starts + [rows - SPAN]


def axial_piece(z, rows, above, below, rim, wf, wh, wl, o_ref, ha, hb):
    channels = wh.shape[3] // (SPAN + 2)
    depth = wh.shape[0] + 1

    def put(target, layer, start, value):
        value = jnp.maximum(value, 0.0)
        reach = depth - layer
        parts = []
        for k in range(SPAN):
            part = value[k * channels : (k + 1) * channels]
            y = start + k
            if y < reach:
                part = jnp.where(above, part, 0.0)
            elif y >= reach + rows:
                part = jnp.where(below, part, 0.0)
            parts.append(part)
        value = jnp.concatenate(parts, axis=0)
        for j, moved in enumerate(side_by_side(value)):
            target[j, start * channels : (start + SPAN) * channels] = moved.astype(BF16)

    def over_columns(matrices, source, start):
        total = None
        for j in range(3):
            window = source[j, start * channels : (start + SPAN + 2) * channels]
            part = jnp.dot(matrices[j], window, preferred_element_type=F32)
            total = part if total is None else total + part
        return total

    around = side_by_side(rim[z])
    empty = jnp.zeros((SPAN + 2, rim.shape[2]), F32)
    for start in spans(rows + 2 * depth):
        taps = [moved[start : start + SPAN + 2] for moved in around] + [empty]
        taps = jnp.concatenate(taps, axis=0).astype(BF16)
        put(ha, 0, start, jnp.dot(wf[...], taps, preferred_element_type=F32))
    source, target = ha, hb
    for layer in range(wh.shape[0]):
        for start in spans(rows + 2 * (depth - 1 - layer)):
            put(target, layer + 1, start, over_columns(wh[layer], source, start))
        source, target = target, source
    for start in spans(rows):
        o_ref[z, start : start + SPAN] = over_columns(wl[...], source, start)[0:SPAN]


def piece_kernel(
    k, place_ref, blk, net, rim, zf, zh, zl, zw, zm, af, ah, al, o_ref, sa, sb, ca, xa, xb
):
    rows = o_ref.shape[1]
    depth = (rim.shape[1] - rows) // 2
    above, below = place_ref[1] > 0, place_ref[1] < place_ref[2] - 1
    o_ref[...] = net[...]

    @pl.when(place_ref[0] == 1)
    def _():
        axial_piece(k, rows, above, below, rim, af, ah, al, o_ref, xa, xb)

    if k < 2:

        @pl.when(place_ref[0] == 2)
        def _():
            half = o_ref.shape[2] // 2
            sagittal_piece(k, half, rows, above, below, rim, zf, zw, zm, o_ref, sa, sb)

    @pl.when(place_ref[0] == 3)
    def _():
        coronal_piece(k * (rows // 4), rows // 4, depth, rim, zf, zh, zl, o_ref, ca)


def piece(k, place, blocks, net, prepared):
    slices, rows, columns = net.shape
    reach = rows + 6
    return pl.pallas_call(
        functools.partial(piece_kernel, k),
        out_shape=jax.ShapeDtypeStruct(net.shape, F32),
        in_specs=[in_smem()] + [in_vmem()] * (2 + len(prepared)),
        out_specs=in_vmem(),
        scratch_shapes=[pltpu.VMEM((reach * 128, columns // 2), BF16)] * 2
        + [pltpu.VMEM((rows // 4, 384, columns), BF16)]
        + [pltpu.VMEM((3, reach * 32, columns), BF16)] * 2,
        compiler_params=params(),
        name=f"piece_{k}",
    )(place, near(blocks), net, *prepared)


def swapped(groups, k):
    return [(g[n], g[(n + k) % len(g)]) for g in groups for n in range(len(g))]


def stage_groups(count):
    near = 4
    strided = 4
    far = count // (near * strided)
    at = lambda f, s, n: (f * strided + s) * near + n
    return [
        [[at(f, s, n) for f in range(far)] for s in range(strided) for n in range(near)],
        [[at(f, s, n) for s in range(strided)] for f in range(far) for n in range(near)],
        [[at(f, s, n) for n in range(near)] for f in range(far) for s in range(strided)],
    ]


def added_up(values, groups):
    total = values.astype(F32)
    for k in range(1, len(groups[0])):
        total = total + lax.ppermute(values, "tile", swapped(groups, k)).astype(F32)
    return total.astype(values.dtype)


def first_transfers(current, agent_place, depth):
    count = lax.axis_size("tile")
    rows = current.shape[1]
    head = jnp.concatenate([part[0:depth] for part in current], axis=0)
    tail = jnp.concatenate([part[rows - depth :] for part in current], axis=0)

    def slices_to(k):
        return [(t, k * count + t) for t in range(count)]

    def onward(a):
        return [(a * count + t, a * count + t + 1) for t in range(count - 1)]

    def backward(a):
        return [(b, a) for a, b in onward(a)]

    is_data = agent_place == 0
    both = ("agent", "tile")
    got = []
    for k, rim, pairs in (
        (1, tail, onward(2)),
        (2, tail, onward(1)),
        (3, head, backward(1) + backward(2)),
    ):
        got.append(lax.ppermute(jnp.where(is_data, current[k], rim), both, slices_to(k) + pairs))
    return got


def per_device(
    states,
    sinogram,
    blocks,
    block_angle,
    block_detector,
    block_tile,
    conv_first,
    conv_hidden,
    conv_last,
):
    current = states[0]
    tile_count = lax.axis_size("tile")
    tile_place = lax.axis_index("tile")
    agent_place = lax.axis_index("agent")
    place = jnp.stack([agent_place, tile_place, jnp.int32(tile_count)]).astype(jnp.int32)
    ray_total = sinogram.shape[0] * tile_count
    ray_index = block_angle * (current.shape[2] // 128) + block_detector

    got = first_transfers(current, agent_place, conv_hidden.shape[1] + 2)
    sums, start, blocks_here = project(
        place, block_angle, block_detector, block_tile, states, got, sinogram, blocks, ray_total
    )

    groups = stage_groups(tile_count)
    net = jnp.zeros_like(current)
    x_data = start
    prepared, k = None, 0
    for step in range(DATA_STEPS):
        for n, group in enumerate(groups):
            sums, net = lax.optimization_barrier((sums, net))
            if n == 0 and step == 0:
                prepared = prepare(place, got, current, conv_first, conv_hidden, conv_last)
            elif n > 0:
                net = piece(k, place, blocks_here, net, prepared)
                k += 1
            sums = added_up(sums, group)
        if step < DATA_STEPS - 1:
            x_data, sums = back_project(
                place, ray_index, block_tile, sums, x_data, sinogram, blocks_here
            )
    sent = back_reflect(ray_index, block_tile, sums, x_data, start, current, net, blocks_here)
    everything = lax.all_gather(sent, "agent")
    return finish(place, everything, current, net)[None]


def solution(mesh):
    placed = (
        P("agent", None, "tile", None),
        P("tile", None, None),
        P("tile", None, None),
        P("tile"),
        P("tile"),
        P("tile"),
        P(),
        P(),
        P(),
    )
    return jax.shard_map(
        per_device,
        mesh=mesh,
        in_specs=placed,
        out_specs=P("agent", None, "tile", None),
        check_vma=False,
    )
```

```python
import functools

import jax
import jax.numpy as jnp
import numpy as np
from jax import lax
from jax.experimental import pallas as pl
from jax.experimental.pallas import tpu as pltpu
from jax.sharding import PartitionSpec as P

DATA_STEPS = 2
F32, BF16 = jnp.float32, jnp.bfloat16
VMEM_LIMIT = 32 << 20
TOGETHER = 4
UNROLL = 16
CHUNK = 64
PIECES = ((0,), (1, 2), (3,))
SPAN = 6


def params():
    return pltpu.CompilerParams(vmem_limit_bytes=VMEM_LIMIT)


def in_vmem():
    return pl.BlockSpec(memory_space=pltpu.VMEM)


def near(x):
    return pltpu.with_memory_space_constraint(x, pltpu.VMEM)


def in_smem():
    return pl.BlockSpec(memory_space=pltpu.SMEM)


def low_rows():
    return lax.broadcasted_iota(jnp.int32, (8, 128), 0) < 4


def four_blocks(blk, b):
    size = blk.shape[1]
    left = blk[pl.ds(b, 2)].reshape(2 * size, size)
    right = blk[pl.ds(b + 2, 2)].reshape(2 * size, size)
    return jnp.concatenate([left, right], axis=1)


def row(ref, index):
    return ref[pl.ds(index, 8, stride=0), :]


def add_rows(acc, index, value):
    acc[index] = acc[index] + value


def project_blocks(ray_of, tile_ref, pix, blk, acc, ready=None):
    low = low_rows()
    zero = jnp.zeros((8, 128), F32)

    def body(i, carry):
        if ready is not None:
            ready(i)
        outs = []
        for u in range(UNROLL):
            b = (i * UNROLL + u) * TOGETHER
            t = [row(pix, tile_ref[b + k]) for k in range(TOGETHER)]
            upper = jnp.concatenate([jnp.where(low, t[0], t[1]), zero], axis=0)
            lower = jnp.concatenate([zero, jnp.where(low, t[2], t[3])], axis=0)
            lhs = jnp.concatenate([upper.astype(BF16), lower.astype(BF16)], axis=1)
            outs.append(
                lax.dot_general(
                    lhs, four_blocks(blk, b), (((1,), (1,)), ((), ())), preferred_element_type=F32
                )
            )
        for u in range(UNROLL):
            b = (i * UNROLL + u) * TOGETHER
            out = outs[u]
            add_rows(acc, ray_of(b), jnp.where(low, out[0:8, 0:128], 0.0))
            add_rows(acc, ray_of(b + 1), jnp.where(low, 0.0, out[0:8, 128:256]))
            add_rows(acc, ray_of(b + 2), jnp.where(low, out[8:16, 0:128], 0.0))
            add_rows(acc, ray_of(b + 3), jnp.where(low, 0.0, out[8:16, 128:256]))
        return carry

    lax.fori_loop(0, blk.shape[0] // (TOGETHER * UNROLL), body, 0)


def back_blocks(ray_ref, tile_ref, res, blk, acc):
    low = low_rows()

    def body(i, carry):
        outs = []
        for u in range(UNROLL):
            b = (i * UNROLL + u) * TOGETHER
            t = [row(res, ray_ref[b + k]) for k in range(TOGETHER)]
            left = jnp.concatenate([jnp.where(low, t[0], 0.0), jnp.where(low, t[2], 0.0)], axis=0)
            right = jnp.concatenate([jnp.where(low, 0.0, t[1]), jnp.where(low, 0.0, t[3])], axis=0)
            lhs = jnp.concatenate([left.astype(BF16), right.astype(BF16)], axis=1)
            outs.append(jnp.dot(lhs, four_blocks(blk, b), preferred_element_type=F32))
        for u in range(UNROLL):
            b = (i * UNROLL + u) * TOGETHER
            upper, lower = outs[u][0:8, 0:128], outs[u][8:16, 128:256]
            add_rows(acc, tile_ref[b], jnp.where(low, upper, 0.0))
            add_rows(acc, tile_ref[b + 1], jnp.where(low, 0.0, upper))
            add_rows(acc, tile_ref[b + 2], jnp.where(low, lower, 0.0))
            add_rows(acc, tile_ref[b + 3], jnp.where(low, 0.0, lower))
        return carry

    lax.fori_loop(0, blk.shape[0] // (TOGETHER * UNROLL), body, 0)


def tiles_of(x_shape):
    wide = x_shape[1] // 128
    return [(r, c, slice(c * 128, c * 128 + 128)) for r in range(x_shape[0]) for c in range(wide)]


def load_pixels(value, pix):
    wide = value.shape[1] // 128
    for r, c, columns in tiles_of(value.shape):
        pix[r * wide + c : r * wide + c + 1] = value[r : r + 1, columns]


def moved_by(x, back):
    wide = x.shape[1] // 128
    rows = back.shape[0]
    columns = []
    for c in range(wide):
        own = pl.ds(c, rows // wide, stride=wide)
        columns.append(back[own, 0, :] + back[own, 4, :])
    return x - 0.8 * jnp.concatenate(columns, axis=1)


def store_rays(place_ref, sino_ref, acc, total, o_ref):
    total[0 : acc.shape[0]] = acc[:, 0, :] + acc[:, 4, :]
    own = sino_ref.shape[0]
    mine = pl.ds(pl.multiple_of(place_ref[1] * own, own), own)
    for z in range(sino_ref.shape[1]):

        @pl.when(place_ref[0] == z)
        def _():
            total[mine] = total[mine] - sino_ref[:, z, :]

    o_ref[...] = total[0 : acc.shape[0]].astype(o_ref.dtype)


def project_kernel(
    place_ref,
    angle_in,
    detector_in,
    tile_in,
    states_in,
    got_1,
    got_2,
    got_3,
    sino_in,
    blk_in,
    o_ref,
    start_ref,
    blk,
    angle,
    detector,
    tile,
    first_slice,
    sino,
    pix,
    acc,
    total,
    small_sems,
    block_sems,
):
    small = [
        pltpu.make_async_copy(source, target, small_sems.at[n])
        for n, (source, target) in enumerate(
            [
                (states_in.at[0, 0], first_slice),
                (angle_in, angle),
                (detector_in, detector),
                (tile_in, tile),
                (sino_in, sino),
            ]
        )
    ]
    for copy in small:
        copy.start()
    chunk = CHUNK

    def chunk_copy(i):
        part = pl.ds(i * chunk, chunk)
        return pltpu.make_async_copy(blk_in.at[part], blk.at[part], block_sems.at[i])

    ahead = 2
    count = blk.shape[0] // chunk
    for i in range(ahead):
        chunk_copy(i).start()

    def ready(i):
        chunk_copy(i).wait()

        @pl.when(i + ahead < count)
        def _():
            chunk_copy(i + ahead).start()

    acc[...] = jnp.zeros_like(acc)
    for copy in small:
        copy.wait()
    for k, value in enumerate((first_slice, got_1, got_2, got_3)):

        @pl.when(place_ref[0] == k)
        def _():
            start_ref[...] = value[...]

    load_pixels(start_ref[...], pix)
    wide = first_slice.shape[1] // 128
    project_blocks(
        lambda b: angle[b] * wide + detector[b],
        tile,
        pix,
        blk,
        acc,
        ready,
    )
    store_rays(place_ref, sino, acc, total, o_ref)


def project(place, angle, detector, tile, states, got, sinogram, blocks, ray_total):
    shape = got[0].shape
    count = blocks.shape[0]
    far = pl.BlockSpec(memory_space=pltpu.HBM)
    stay = lambda x: pltpu.with_memory_space_constraint(x, pltpu.HBM)
    return pl.pallas_call(
        project_kernel,
        out_shape=(
            jax.ShapeDtypeStruct((ray_total, 128), BF16),
            jax.ShapeDtypeStruct(shape, F32),
            pltpu.VMEM(blocks.shape, BF16),
        ),
        in_specs=[in_smem()] + [far] * 4 + [in_vmem()] * 3 + [far] * 2,
        out_specs=(in_vmem(),) * 3,
        scratch_shapes=[
            pltpu.SMEM((count,), jnp.int32),
            pltpu.SMEM((count,), jnp.int32),
            pltpu.SMEM((count,), jnp.int32),
            pltpu.VMEM(shape, F32),
            pltpu.VMEM(sinogram.shape, F32),
            pltpu.VMEM((shape[0] * shape[1] // 128 + 8, 128), F32),
            pltpu.VMEM((ray_total, 8, 128), F32),
            pltpu.VMEM((ray_total + 8, 128), F32),
            pltpu.SemaphoreType.DMA((5,)),
            pltpu.SemaphoreType.DMA((count // CHUNK,)),
        ],
        compiler_params=params(),
        name="project",
    )(
        place,
        stay(angle),
        stay(detector),
        stay(tile),
        stay(states),
        *got,
        stay(sinogram),
        stay(blocks),
    )


def back_project_kernel(
    place_ref, ray_ref, tile_ref, r_ref, x_ref, sino_ref, blk, x_out, o_ref, res, pix, back, acc
):
    res[0 : r_ref.shape[0]] = r_ref[...].astype(F32)
    back[...] = jnp.zeros_like(back)
    back_blocks(ray_ref, tile_ref, res, blk, back)
    moved = moved_by(x_ref[...], back)
    x_out[...] = moved
    load_pixels(moved, pix)
    acc[...] = jnp.zeros_like(acc)
    project_blocks(lambda b: ray_ref[b], tile_ref, pix, blk, acc)
    store_rays(place_ref, sino_ref, acc, res, o_ref)


def back_project(place, ray_index, tile_index, residual, x, sinogram, blocks):
    ray_total = residual.shape[0]
    tiles = x.size // 128
    return pl.pallas_call(
        back_project_kernel,
        out_shape=(
            jax.ShapeDtypeStruct(x.shape, F32),
            jax.ShapeDtypeStruct(residual.shape, BF16),
        ),
        in_specs=[in_smem()] * 3 + [in_vmem()] * 4,
        out_specs=(in_vmem(), in_vmem()),
        scratch_shapes=[
            pltpu.VMEM((ray_total + 8, 128), F32),
            pltpu.VMEM((tiles + 8, 128), F32),
            pltpu.VMEM((tiles, 8, 128), F32),
            pltpu.VMEM((ray_total, 8, 128), F32),
        ],
        compiler_params=params(),
        name="back_project",
    )(place, ray_index, tile_index, residual, x, sinogram, near(blocks))


def back_kernel(ray_ref, tile_ref, r_ref, x_ref, start_ref, cur_ref, net_ref, blk, o_ref, res, back):
    res[0 : r_ref.shape[0]] = r_ref[...].astype(F32)
    back[...] = jnp.zeros_like(back)
    for z in range(net_ref.shape[0]):
        o_ref[z + 1] = (cur_ref[z] - 2.0 * net_ref[z]).astype(o_ref.dtype)
    back_blocks(ray_ref, tile_ref, res, blk, back)
    o_ref[0] = (2.0 * moved_by(x_ref[...], back) - start_ref[...]).astype(o_ref.dtype)


def back_reflect(ray_index, tile_index, residual, x, start, current, net, blocks):
    ray_total = residual.shape[0]
    tiles = x.size // 128
    return pl.pallas_call(
        back_kernel,
        out_shape=jax.ShapeDtypeStruct((1 + net.shape[0], *x.shape), BF16),
        in_specs=[in_smem()] * 2 + [in_vmem()] * 6,
        out_specs=in_vmem(),
        scratch_shapes=[
            pltpu.VMEM((ray_total + 8, 128), F32),
            pltpu.VMEM((tiles, 8, 128), F32),
        ],
        compiler_params=params(),
        name="back_reflect",
    )(ray_index, tile_index, residual, x, start, current, net, near(blocks))


def finish_kernel(place_ref, all_ref, cur_ref, net_ref, o_ref):
    for z in range(o_ref.shape[0]):
        data = all_ref[z, 0].astype(F32)
        total = data
        for k in range(1, all_ref.shape[0]):
            total = total + all_ref[k, 1 + z].astype(F32)

        @pl.when(place_ref[0] == 0)
        def _():
            o_ref[z] = 0.25 * total + 0.5 * (cur_ref[z] - data)

        @pl.when(place_ref[0] != 0)
        def _():
            o_ref[z] = 0.25 * total + net_ref[z]


def finish(place, everything, current, net):
    return pl.pallas_call(
        finish_kernel,
        out_shape=jax.ShapeDtypeStruct(current.shape, F32),
        in_specs=[in_smem()] + [in_vmem()] * 3,
        out_specs=in_vmem(),
        compiler_params=params(),
        name="finish",
    )(place, everything, current, net)


def lanes(parts, count, height, width):
    empty = jnp.zeros((height, width), F32)
    return jnp.concatenate([parts.get(n, empty) for n in range(count)], axis=1)


def slice_band(first, hidden, last, o, zf, zh, zl, turn):
    turn[...] = jnp.zeros_like(turn)
    for j in range(3):
        for z in range(4):
            near = {y: z - y + 1 for y in range(4) if 0 <= z - y + 1 < 3}
            n = j * 4 + z
            parts = {y: first[o, i, j : j + 1, :].astype(F32) for y, i in near.items()}
            turn[n : n + 1, 0:128] = lanes(parts, 4, 1, 32)
    zf[...] = jnp.transpose(turn[0:128, 0:128])[:, 0:16].astype(BF16)
    for layer in range(hidden.shape[1]):
        for j in range(3):
            for z in range(4):
                near = {y: z - y + 1 for y in range(4) if 0 <= z - y + 1 < 3}
                parts = {y: hidden[o, layer, i, j].astype(F32) for y, i in near.items()}
                turn[z * 32 : z * 32 + 32, 0:128] = lanes(parts, 4, 32, 32)
            zh[layer, :, j * 128 : j * 128 + 128] = jnp.transpose(turn[0:128, 0:128]).astype(BF16)
    rows = []
    for y in range(4):
        parts = {
            j * 4 + z: last[o, z - y + 1, j : j + 1, :].astype(F32)
            for j in range(3)
            for z in range(4)
            if 0 <= z - y + 1 < 3
        }
        rows.append(lanes(parts, 12, 1, 32))
    zl[...] = jnp.concatenate(rows + [jnp.zeros((4, 384), F32)], axis=0).astype(BF16)


def widen(zh, zl, zw, zm):
    for layer in range(zh.shape[0]):
        zw[layer, 0:128, 0:384] = zh[layer]
        zw[layer, 0:128, 384:512] = jnp.zeros((128, 128), BF16)
        zw[layer, 128:256, 0:128] = jnp.zeros((128, 128), BF16)
        zw[layer, 128:256, 128:512] = zh[layer]
    plain = zl[...].astype(F32)
    rows = []
    for z in range(4):
        for a in range(4):
            parts = {a + n: plain[z : z + 1, n * 128 : n * 128 + 128] for n in range(3)}
            rows.append(lanes(parts, 6, 1, 128))
    zm[...] = jnp.concatenate(rows, axis=0).astype(BF16)


def row_band(first, hidden, last, af, ah, al, turn):
    turn[...] = jnp.zeros_like(turn)
    for j in range(3):
        for y in range(SPAN + 2):
            parts = {m: first[0, y - m, j : j + 1, :].astype(F32) for m in range(SPAN) if 0 <= y - m < 3}
            n = j * (SPAN + 2) + y
            turn[n : n + 1] = lanes(parts, 8, 1, 32)
    af[...] = jnp.transpose(turn[0:128])[0 : SPAN * 32, 0:32].astype(BF16)
    for layer in range(hidden.shape[1]):
        for j in range(3):
            for y in range(SPAN + 2):
                parts = {m: hidden[0, layer, y - m, j].astype(F32) for m in range(SPAN) if 0 <= y - m < 3}
                turn[y * 32 : y * 32 + 32] = lanes(parts, 8, 32, 32)
            ah[layer, j] = jnp.transpose(turn[...])[0 : SPAN * 32].astype(BF16)
    for j in range(3):
        rows = []
        for m in range(SPAN):
            parts = {m + i: last[0, i, j : j + 1, :].astype(F32) for i in range(3)}
            rows.append(lanes(parts, 8, 1, 32))
        rows.append(jnp.zeros((2, 256), F32))
        al[j] = jnp.concatenate(rows, axis=0).astype(BF16)


def prepare_kernel(
    place_ref, before, after, cur, first, hidden, last, rim, zf, zh, zl, zw, zm, af, ah, al, turn
):
    depth = before.shape[1]
    rows = cur.shape[1]
    rim[:, 0:depth] = before[...].astype(BF16).astype(F32)
    rim[:, depth : depth + rows] = cur[...].astype(BF16).astype(F32)
    rim[:, depth + rows :] = after[...].astype(BF16).astype(F32)

    @pl.when(place_ref[0] == 1)
    def _():
        row_band(first, hidden, last, af, ah, al, turn)

    @pl.when(place_ref[0] == 2)
    def _():
        slice_band(first, hidden, last, 1, zf, zh, zl, turn)
        widen(zh, zl, zw, zm)

    @pl.when(place_ref[0] == 3)
    def _():
        slice_band(first, hidden, last, 2, zf, zh, zl, turn)


def prepare(place, rim, current, first, hidden, last):
    layers = hidden.shape[1]
    slices, rows, columns = current.shape
    depth = rim[0].shape[1]
    whole = jax.ShapeDtypeStruct((slices, rows + 2 * depth, columns), F32)
    shapes = [
        (128, 16),
        (layers, 128, 384),
        (8, 384),
        (layers, 256, 512),
        (16, 768),
        (SPAN * 32, 32),
        (layers, 3, SPAN * 32, 256),
        (3, 8, 256),
    ]
    return pl.pallas_call(
        prepare_kernel,
        out_shape=[whole] + [jax.ShapeDtypeStruct(s, BF16) for s in shapes],
        in_specs=[in_smem()] + [in_vmem()] * 6,
        out_specs=[in_vmem()] * 9,
        scratch_shapes=[pltpu.VMEM((256, 256), F32)],
        compiler_params=params(),
        name="prepare",
    )(place, *rim, current, first, hidden, last)


def side_by_side(value):
    columns = value.shape[1]
    place = lax.broadcasted_iota(jnp.int32, value.shape, 1)
    before = jnp.where(place == 0, 0.0, pltpu.roll(value, 1, axis=1))
    after = jnp.where(place == columns - 1, 0.0, pltpu.roll(value, columns - 1, axis=1))
    return before, value, after


def relu_rows(value, keep):
    value = jnp.maximum(value, 0.0)
    return value if keep is None else jnp.where(keep, value, 0.0)


def sagittal_piece(part, columns, rows, above, below, rim, wf, wh, wl, o_ref, ha, hb):
    width = wf.shape[0]
    depth = wh.shape[0] + 1
    across = slice(part * columns, (part + 1) * columns)

    def kept(layer, y):
        reach = depth - layer
        return above if y < reach else below if y >= reach + rows else None

    empty = jnp.zeros((4, columns), F32)
    for y in range(rows + 2 * depth):
        taps = [rim[:, y + j, across] for j in range(3)] + [empty]
        taps = jnp.concatenate(taps, axis=0).astype(BF16)
        value = jnp.dot(wf[...], taps, preferred_element_type=F32)
        ha[y * width : (y + 1) * width] = relu_rows(value, kept(0, y)).astype(BF16)
    source, target = ha, hb
    for layer in range(wh.shape[0]):
        for y in range(0, rows + 2 * (depth - 1 - layer), 2):
            value = jnp.dot(
                wh[layer], source[y * width : (y + 4) * width], preferred_element_type=F32
            )
            for k in range(2):
                part_k = value[k * width : (k + 1) * width]
                target[(y + k) * width : (y + k + 1) * width] = relu_rows(
                    part_k, kept(layer + 1, y + k)
                ).astype(BF16)
        source, target = target, source
    for y in range(0, rows, 4):
        net = jnp.dot(wl[...], source[y * width : (y + 6) * width], preferred_element_type=F32)
        for z in range(4):
            o_ref[z, y : y + 4, across] = net[z * 4 : z * 4 + 4]


def coronal_piece(start, count, depth, rim, wf, wh, wl, o_ref, h):
    columns = rim.shape[2]
    width = wf.shape[0]
    empty = jnp.zeros((4, columns), F32)
    values = []
    for r in range(count):
        taps = jnp.concatenate([*side_by_side(rim[:, depth + start + r, :]), empty], axis=0)
        values.append(jnp.dot(wf[...], taps.astype(BF16), preferred_element_type=F32))
    for layer in range(wh.shape[0] + 1):
        matrix = wh[layer] if layer < wh.shape[0] else wl[...]
        for r in range(count):
            for j, moved in enumerate(side_by_side(jnp.maximum(values[r], 0.0))):
                h[r, j * width : (j + 1) * width] = moved.astype(BF16)
            values[r] = jnp.dot(matrix, h[r], preferred_element_type=F32)
    for r in range(count):
        o_ref[:, start + r, :] = values[r][0:4]


def spans(rows):
    starts = list(range(0, rows - SPAN, SPAN))
    return starts + [rows - SPAN]


def axial_piece(z, rows, above, below, rim, wf, wh, wl, o_ref, ha, hb):
    channels = wh.shape[3] // (SPAN + 2)
    depth = wh.shape[0] + 1

    def put(target, layer, start, value):
        value = jnp.maximum(value, 0.0)
        reach = depth - layer
        parts = []
        for k in range(SPAN):
            part = value[k * channels : (k + 1) * channels]
            y = start + k
            if y < reach:
                part = jnp.where(above, part, 0.0)
            elif y >= reach + rows:
                part = jnp.where(below, part, 0.0)
            parts.append(part)
        value = jnp.concatenate(parts, axis=0)
        for j, moved in enumerate(side_by_side(value)):
            target[j, start * channels : (start + SPAN) * channels] = moved.astype(BF16)

    def over_columns(matrices, source, start):
        total = None
        for j in range(3):
            window = source[j, start * channels : (start + SPAN + 2) * channels]
            part = jnp.dot(matrices[j], window, preferred_element_type=F32)
            total = part if total is None else total + part
        return total

    around = side_by_side(rim[z])
    empty = jnp.zeros((SPAN + 2, rim.shape[2]), F32)
    for start in spans(rows + 2 * depth):
        taps = [moved[start : start + SPAN + 2] for moved in around] + [empty]
        taps = jnp.concatenate(taps, axis=0).astype(BF16)
        put(ha, 0, start, jnp.dot(wf[...], taps, preferred_element_type=F32))
    source, target = ha, hb
    for layer in range(wh.shape[0]):
        for start in spans(rows + 2 * (depth - 1 - layer)):
            put(target, layer + 1, start, over_columns(wh[layer], source, start))
        source, target = target, source
    for start in spans(rows):
        o_ref[z, start : start + SPAN] = over_columns(wl[...], source, start)[0:SPAN]


def piece_kernel(
    k, place_ref, blk, net, rim, zf, zh, zl, zw, zm, af, ah, al, o_ref, sa, sb, ca, xa, xb
):
    rows = o_ref.shape[1]
    depth = (rim.shape[1] - rows) // 2
    above, below = place_ref[1] > 0, place_ref[1] < place_ref[2] - 1
    o_ref[...] = net[...]

    @pl.when(place_ref[0] == 1)
    def _():
        axial_piece(k, rows, above, below, rim, af, ah, al, o_ref, xa, xb)

    if k < 2:

        @pl.when(place_ref[0] == 2)
        def _():
            half = o_ref.shape[2] // 2
            sagittal_piece(k, half, rows, above, below, rim, zf, zw, zm, o_ref, sa, sb)

    @pl.when(place_ref[0] == 3)
    def _():
        coronal_piece(k * (rows // 4), rows // 4, depth, rim, zf, zh, zl, o_ref, ca)


def piece(k, place, blocks, net, prepared):
    slices, rows, columns = net.shape
    reach = rows + 6
    return pl.pallas_call(
        functools.partial(piece_kernel, k),
        out_shape=jax.ShapeDtypeStruct(net.shape, F32),
        in_specs=[in_smem()] + [in_vmem()] * (2 + len(prepared)),
        out_specs=in_vmem(),
        scratch_shapes=[pltpu.VMEM((reach * 128, columns // 2), BF16)] * 2
        + [pltpu.VMEM((rows // 4, 384, columns), BF16)]
        + [pltpu.VMEM((3, reach * 32, columns), BF16)] * 2,
        compiler_params=params(),
        name=f"piece_{k}",
    )(place, near(blocks), net, *prepared)


def swapped(groups, k):
    return [(g[n], g[(n + k) % len(g)]) for g in groups for n in range(len(g))]


def stage_groups(count):
    near = 4
    strided = 4
    far = count // (near * strided)
    at = lambda f, s, n: (f * strided + s) * near + n
    return [
        [[at(f, s, n) for f in range(far)] for s in range(strided) for n in range(near)],
        [[at(f, s, n) for s in range(strided)] for f in range(far) for n in range(near)],
        [[at(f, s, n) for n in range(near)] for f in range(far) for s in range(strided)],
    ]


def added_up(values, groups):
    total = values.astype(F32)
    for k in range(1, len(groups[0])):
        total = total + lax.ppermute(values, "tile", swapped(groups, k)).astype(F32)
    return total.astype(values.dtype)


def rims(cells, depth):
    count = lax.axis_size("tile")
    pairs = [(a * count + t, a * count + t + 1) for a in (1, 2) for t in range(count - 1)]
    both = ("agent", "tile")
    before = lax.ppermute(cells[:, cells.shape[1] - depth :], both, pairs)
    after = lax.ppermute(cells[:, 0:depth], both, [(b, a) for a, b in pairs])
    return before, after


def slices_sent(current):
    return [lax.ppermute(current[k], "agent", [(0, k)]) for k in range(1, current.shape[0])]


def per_device(
    states,
    sinogram,
    blocks,
    block_angle,
    block_detector,
    block_tile,
    conv_first,
    conv_hidden,
    conv_last,
):
    current = states[0]
    tile_count = lax.axis_size("tile")
    tile_place = lax.axis_index("tile")
    agent_place = lax.axis_index("agent")
    place = jnp.stack([agent_place, tile_place, jnp.int32(tile_count)]).astype(jnp.int32)
    ray_total = sinogram.shape[0] * tile_count
    ray_index = block_angle * (current.shape[2] // 128) + block_detector

    got = slices_sent(current)
    sums, start, blocks_here = project(
        place, block_angle, block_detector, block_tile, states, got, sinogram, blocks, ray_total
    )

    groups = stage_groups(tile_count)
    net = jnp.zeros_like(current)
    x_data = start
    for step in range(DATA_STEPS):
        for n, group in enumerate(groups):
            sums, net = lax.optimization_barrier((sums, net))
            if step == DATA_STEPS - 1:
                if n == 0:
                    prepared = prepare(place, rim, current, conv_first, conv_hidden, conv_last)
                for k in PIECES[n]:
                    net = piece(k, place, blocks_here, net, prepared)
            if step == DATA_STEPS - 2 and n == len(groups) - 1:
                around, sums = lax.optimization_barrier((current, sums))
                rim = rims(around, conv_hidden.shape[1] + 2)
                rim, sums = lax.optimization_barrier((rim, added_up(sums, group)))
            else:
                sums = added_up(sums, group)
        if step < DATA_STEPS - 1:
            x_data, sums = back_project(
                place, ray_index, block_tile, sums, x_data, sinogram, blocks_here
            )
    sent = back_reflect(ray_index, block_tile, sums, x_data, start, current, net, blocks_here)
    everything = lax.all_gather(sent, "agent")
    return finish(place, everything, current, net)[None]


def solution(mesh):
    placed = (
        P("agent", None, "tile", None),
        P("tile", None, None),
        P("tile", None, None),
        P("tile"),
        P("tile"),
        P("tile"),
        P(),
        P(),
        P(),
    )
    return jax.shard_map(
        per_device,
        mesh=mesh,
        in_specs=placed,
        out_specs=P("agent", None, "tile", None),
        check_vma=False,
    )
```

```python
import functools

import jax
import jax.numpy as jnp
import numpy as np
from jax import lax
from jax.experimental import pallas as pl
from jax.experimental.pallas import tpu as pltpu
from jax.sharding import PartitionSpec as P

DATA_STEPS = 2
F32, BF16 = jnp.float32, jnp.bfloat16
VMEM_LIMIT = 32 << 20
TOGETHER = 4
UNROLL = 16
RIM = 4
CHUNK = 64
PIECES = ((0,), (1, 2), (3,))
SPAN = 6


def params():
    return pltpu.CompilerParams(vmem_limit_bytes=VMEM_LIMIT)


def in_vmem():
    return pl.BlockSpec(memory_space=pltpu.VMEM)


def near(x):
    return pltpu.with_memory_space_constraint(x, pltpu.VMEM)


def in_smem():
    return pl.BlockSpec(memory_space=pltpu.SMEM)


def low_rows():
    return lax.broadcasted_iota(jnp.int32, (8, 128), 0) < 4


def four_blocks(blk, b):
    size = blk.shape[1]
    left = blk[pl.ds(b, 2)].reshape(2 * size, size)
    right = blk[pl.ds(b + 2, 2)].reshape(2 * size, size)
    return jnp.concatenate([left, right], axis=1)


def row(ref, index):
    return ref[pl.ds(index, 8, stride=0), :]


def add_rows(acc, index, value):
    acc[index] = acc[index] + value


def project_blocks(ray_of, tile_ref, pix, blk, acc, ready=None):
    low = low_rows()
    zero = jnp.zeros((8, 128), F32)

    def body(i, carry):
        if ready is not None:
            ready(i)
        outs = []
        for u in range(UNROLL):
            b = (i * UNROLL + u) * TOGETHER
            t = [row(pix, tile_ref[b + k]) for k in range(TOGETHER)]
            upper = jnp.concatenate([jnp.where(low, t[0], t[1]), zero], axis=0)
            lower = jnp.concatenate([zero, jnp.where(low, t[2], t[3])], axis=0)
            lhs = jnp.concatenate([upper.astype(BF16), lower.astype(BF16)], axis=1)
            outs.append(
                lax.dot_general(
                    lhs, four_blocks(blk, b), (((1,), (1,)), ((), ())), preferred_element_type=F32
                )
            )
        for u in range(UNROLL):
            b = (i * UNROLL + u) * TOGETHER
            out = outs[u]
            add_rows(acc, ray_of(b), jnp.where(low, out[0:8, 0:128], 0.0))
            add_rows(acc, ray_of(b + 1), jnp.where(low, 0.0, out[0:8, 128:256]))
            add_rows(acc, ray_of(b + 2), jnp.where(low, out[8:16, 0:128], 0.0))
            add_rows(acc, ray_of(b + 3), jnp.where(low, 0.0, out[8:16, 128:256]))
        return carry

    lax.fori_loop(0, blk.shape[0] // (TOGETHER * UNROLL), body, 0)


def back_blocks(ray_ref, tile_ref, res, blk, acc):
    low = low_rows()

    def body(i, carry):
        outs = []
        for u in range(UNROLL):
            b = (i * UNROLL + u) * TOGETHER
            t = [row(res, ray_ref[b + k]) for k in range(TOGETHER)]
            left = jnp.concatenate([jnp.where(low, t[0], 0.0), jnp.where(low, t[2], 0.0)], axis=0)
            right = jnp.concatenate([jnp.where(low, 0.0, t[1]), jnp.where(low, 0.0, t[3])], axis=0)
            lhs = jnp.concatenate([left.astype(BF16), right.astype(BF16)], axis=1)
            outs.append(jnp.dot(lhs, four_blocks(blk, b), preferred_element_type=F32))
        for u in range(UNROLL):
            b = (i * UNROLL + u) * TOGETHER
            upper, lower = outs[u][0:8, 0:128], outs[u][8:16, 128:256]
            add_rows(acc, tile_ref[b], jnp.where(low, upper, 0.0))
            add_rows(acc, tile_ref[b + 1], jnp.where(low, 0.0, upper))
            add_rows(acc, tile_ref[b + 2], jnp.where(low, lower, 0.0))
            add_rows(acc, tile_ref[b + 3], jnp.where(low, 0.0, lower))
        return carry

    lax.fori_loop(0, blk.shape[0] // (TOGETHER * UNROLL), body, 0)


def tiles_of(x_shape):
    wide = x_shape[1] // 128
    return [(r, c, slice(c * 128, c * 128 + 128)) for r in range(x_shape[0]) for c in range(wide)]


def load_pixels(value, pix):
    wide = value.shape[1] // 128
    for r, c, columns in tiles_of(value.shape):
        pix[r * wide + c : r * wide + c + 1] = value[r : r + 1, columns]


def moved_by(x, back):
    wide = x.shape[1] // 128
    rows = back.shape[0]
    columns = []
    for c in range(wide):
        own = pl.ds(c, rows // wide, stride=wide)
        columns.append(back[own, 0, :] + back[own, 4, :])
    return x - 0.8 * jnp.concatenate(columns, axis=1)


def store_rays(place_ref, sino_ref, acc, total, o_ref):
    total[0 : acc.shape[0]] = acc[:, 0, :] + acc[:, 4, :]
    own = sino_ref.shape[0]
    mine = pl.ds(pl.multiple_of(place_ref[1] * own, own), own)
    for z in range(sino_ref.shape[1]):

        @pl.when(place_ref[0] == z)
        def _():
            total[mine] = total[mine] - sino_ref[:, z, :]

    o_ref[0 : acc.shape[0]] = total[0 : acc.shape[0]].astype(o_ref.dtype)


def in_pieces(cur, first):
    pieces = []
    for z in range(cur.shape[0]):
        for c in range(cur.shape[2] // 128):
            pieces.append(cur[z, first : first + RIM, c * 128 : c * 128 + 128])
    return jnp.concatenate(pieces, axis=0)


def project_kernel(
    place_ref,
    angle_in,
    detector_in,
    tile_in,
    states_in,
    got_1,
    got_2,
    got_3,
    sino_in,
    blk_in,
    o_ref,
    start_ref,
    blk,
    angle,
    detector,
    tile,
    cur,
    sino,
    pix,
    acc,
    total,
    small_sems,
    block_sems,
):
    small = [
        pltpu.make_async_copy(source, target, small_sems.at[n])
        for n, (source, target) in enumerate(
            [
                (states_in.at[0], cur),
                (angle_in, angle),
                (detector_in, detector),
                (tile_in, tile),
                (sino_in, sino),
            ]
        )
    ]
    for copy in small:
        copy.start()
    chunk = CHUNK

    def chunk_copy(i):
        part = pl.ds(i * chunk, chunk)
        return pltpu.make_async_copy(blk_in.at[part], blk.at[part], block_sems.at[i])

    ahead = 2
    count = blk.shape[0] // chunk
    for i in range(ahead):
        chunk_copy(i).start()

    def ready(i):
        chunk_copy(i).wait()

        @pl.when(i + ahead < count)
        def _():
            chunk_copy(i + ahead).start()

    acc[...] = jnp.zeros_like(acc)
    for copy in small:
        copy.wait()
    @pl.when(place_ref[0] == 0)
    def _():
        start_ref[...] = cur[0]

    for k, value in enumerate((got_1, got_2, got_3)):

        @pl.when(place_ref[0] == k + 1)
        def _():
            start_ref[...] = value[...]

    rows = acc.shape[0]
    edge = RIM * cur.shape[0] * cur.shape[2] // 128
    o_ref[rows : rows + edge] = in_pieces(cur, cur.shape[1] - RIM).astype(BF16)
    o_ref[rows + edge :] = in_pieces(cur, 0).astype(BF16)
    load_pixels(start_ref[...], pix)
    wide = cur.shape[2] // 128
    project_blocks(
        lambda b: angle[b] * wide + detector[b],
        tile,
        pix,
        blk,
        acc,
        ready,
    )
    store_rays(place_ref, sino, acc, total, o_ref)


def project(place, angle, detector, tile, states, got, sinogram, blocks, ray_total):
    shape = got[0].shape
    count = blocks.shape[0]
    edge = RIM * states.shape[1] * states.shape[3] // 128
    far = pl.BlockSpec(memory_space=pltpu.HBM)
    stay = lambda x: pltpu.with_memory_space_constraint(x, pltpu.HBM)
    return pl.pallas_call(
        project_kernel,
        out_shape=(
            jax.ShapeDtypeStruct((ray_total + 2 * edge, 128), BF16),
            jax.ShapeDtypeStruct(shape, F32),
            pltpu.VMEM(blocks.shape, BF16),
        ),
        in_specs=[in_smem()] + [far] * 4 + [in_vmem()] * 3 + [far] * 2,
        out_specs=(in_vmem(),) * 3,
        scratch_shapes=[
            pltpu.SMEM((count,), jnp.int32),
            pltpu.SMEM((count,), jnp.int32),
            pltpu.SMEM((count,), jnp.int32),
            pltpu.VMEM(states.shape[1:], F32),
            pltpu.VMEM(sinogram.shape, F32),
            pltpu.VMEM((shape[0] * shape[1] // 128 + 8, 128), F32),
            pltpu.VMEM((ray_total, 8, 128), F32),
            pltpu.VMEM((ray_total + 8, 128), F32),
            pltpu.SemaphoreType.DMA((5,)),
            pltpu.SemaphoreType.DMA((count // CHUNK,)),
        ],
        compiler_params=params(),
        name="project",
    )(
        place,
        stay(angle),
        stay(detector),
        stay(tile),
        stay(states),
        *got,
        stay(sinogram),
        stay(blocks),
    )


def back_project_kernel(
    place_ref, ray_ref, tile_ref, r_ref, x_ref, sino_ref, blk, x_out, o_ref, res, pix, back, acc
):
    res[0 : r_ref.shape[0]] = r_ref[...].astype(F32)
    back[...] = jnp.zeros_like(back)
    back_blocks(ray_ref, tile_ref, res, blk, back)
    moved = moved_by(x_ref[...], back)
    x_out[...] = moved
    load_pixels(moved, pix)
    acc[...] = jnp.zeros_like(acc)
    project_blocks(lambda b: ray_ref[b], tile_ref, pix, blk, acc)
    store_rays(place_ref, sino_ref, acc, res, o_ref)


def back_project(place, ray_index, tile_index, residual, x, sinogram, blocks):
    ray_total = residual.shape[0]
    tiles = x.size // 128
    return pl.pallas_call(
        back_project_kernel,
        out_shape=(
            jax.ShapeDtypeStruct(x.shape, F32),
            jax.ShapeDtypeStruct(residual.shape, BF16),
        ),
        in_specs=[in_smem()] * 3 + [in_vmem()] * 4,
        out_specs=(in_vmem(), in_vmem()),
        scratch_shapes=[
            pltpu.VMEM((ray_total + 8, 128), F32),
            pltpu.VMEM((tiles + 8, 128), F32),
            pltpu.VMEM((tiles, 8, 128), F32),
            pltpu.VMEM((ray_total, 8, 128), F32),
        ],
        compiler_params=params(),
        name="back_project",
    )(place, ray_index, tile_index, residual, x, sinogram, near(blocks))


def back_kernel(ray_ref, tile_ref, r_ref, x_ref, start_ref, cur_ref, net_ref, blk, o_ref, res, back):
    res[0 : r_ref.shape[0]] = r_ref[...].astype(F32)
    back[...] = jnp.zeros_like(back)
    for z in range(net_ref.shape[0]):
        o_ref[z + 1] = (cur_ref[z] - 2.0 * net_ref[z]).astype(o_ref.dtype)
    back_blocks(ray_ref, tile_ref, res, blk, back)
    o_ref[0] = (2.0 * moved_by(x_ref[...], back) - start_ref[...]).astype(o_ref.dtype)


def back_reflect(ray_index, tile_index, residual, x, start, current, net, blocks):
    ray_total = residual.shape[0]
    tiles = x.size // 128
    return pl.pallas_call(
        back_kernel,
        out_shape=jax.ShapeDtypeStruct((1 + net.shape[0], *x.shape), BF16),
        in_specs=[in_smem()] * 2 + [in_vmem()] * 6,
        out_specs=in_vmem(),
        scratch_shapes=[
            pltpu.VMEM((ray_total + 8, 128), F32),
            pltpu.VMEM((tiles, 8, 128), F32),
        ],
        compiler_params=params(),
        name="back_reflect",
    )(ray_index, tile_index, residual, x, start, current, net, near(blocks))


def finish_kernel(place_ref, all_ref, cur_ref, net_ref, o_ref):
    for z in range(o_ref.shape[0]):
        data = all_ref[z, 0].astype(F32)
        total = data
        for k in range(1, all_ref.shape[0]):
            total = total + all_ref[k, 1 + z].astype(F32)

        @pl.when(place_ref[0] == 0)
        def _():
            o_ref[z] = 0.25 * total + 0.5 * (cur_ref[z] - data)

        @pl.when(place_ref[0] != 0)
        def _():
            o_ref[z] = 0.25 * total + net_ref[z]


def finish(place, everything, current, net):
    return pl.pallas_call(
        finish_kernel,
        out_shape=jax.ShapeDtypeStruct(current.shape, F32),
        in_specs=[in_smem()] + [in_vmem()] * 3,
        out_specs=in_vmem(),
        compiler_params=params(),
        name="finish",
    )(place, everything, current, net)


def lanes(parts, count, height, width):
    empty = jnp.zeros((height, width), F32)
    return jnp.concatenate([parts.get(n, empty) for n in range(count)], axis=1)


def slice_band(first, hidden, last, o, zf, zh, zl, turn):
    turn[...] = jnp.zeros_like(turn)
    for j in range(3):
        for z in range(4):
            near = {y: z - y + 1 for y in range(4) if 0 <= z - y + 1 < 3}
            n = j * 4 + z
            parts = {y: first[o, i, j : j + 1, :].astype(F32) for y, i in near.items()}
            turn[n : n + 1, 0:128] = lanes(parts, 4, 1, 32)
    zf[...] = jnp.transpose(turn[0:128, 0:128])[:, 0:16].astype(BF16)
    for layer in range(hidden.shape[1]):
        for j in range(3):
            for z in range(4):
                near = {y: z - y + 1 for y in range(4) if 0 <= z - y + 1 < 3}
                parts = {y: hidden[o, layer, i, j].astype(F32) for y, i in near.items()}
                turn[z * 32 : z * 32 + 32, 0:128] = lanes(parts, 4, 32, 32)
            zh[layer, :, j * 128 : j * 128 + 128] = jnp.transpose(turn[0:128, 0:128]).astype(BF16)
    rows = []
    for y in range(4):
        parts = {
            j * 4 + z: last[o, z - y + 1, j : j + 1, :].astype(F32)
            for j in range(3)
            for z in range(4)
            if 0 <= z - y + 1 < 3
        }
        rows.append(lanes(parts, 12, 1, 32))
    zl[...] = jnp.concatenate(rows + [jnp.zeros((4, 384), F32)], axis=0).astype(BF16)


def widen(zh, zl, zw, zm):
    for layer in range(zh.shape[0]):
        zw[layer, 0:128, 0:384] = zh[layer]
        zw[layer, 0:128, 384:512] = jnp.zeros((128, 128), BF16)
        zw[layer, 128:256, 0:128] = jnp.zeros((128, 128), BF16)
        zw[layer, 128:256, 128:512] = zh[layer]
    plain = zl[...].astype(F32)
    rows = []
    for z in range(4):
        for a in range(4):
            parts = {a + n: plain[z : z + 1, n * 128 : n * 128 + 128] for n in range(3)}
            rows.append(lanes(parts, 6, 1, 128))
    zm[...] = jnp.concatenate(rows, axis=0).astype(BF16)


def row_band(first, hidden, last, af, ah, al, turn):
    turn[...] = jnp.zeros_like(turn)
    for j in range(3):
        for y in range(SPAN + 2):
            parts = {m: first[0, y - m, j : j + 1, :].astype(F32) for m in range(SPAN) if 0 <= y - m < 3}
            n = j * (SPAN + 2) + y
            turn[n : n + 1] = lanes(parts, 8, 1, 32)
    af[...] = jnp.transpose(turn[0:128])[0 : SPAN * 32, 0:32].astype(BF16)
    for layer in range(hidden.shape[1]):
        for j in range(3):
            for y in range(SPAN + 2):
                parts = {m: hidden[0, layer, y - m, j].astype(F32) for m in range(SPAN) if 0 <= y - m < 3}
                turn[y * 32 : y * 32 + 32] = lanes(parts, 8, 32, 32)
            ah[layer, j] = jnp.transpose(turn[...])[0 : SPAN * 32].astype(BF16)
    for j in range(3):
        rows = []
        for m in range(SPAN):
            parts = {m + i: last[0, i, j : j + 1, :].astype(F32) for i in range(3)}
            rows.append(lanes(parts, 8, 1, 32))
        rows.append(jnp.zeros((2, 256), F32))
        al[j] = jnp.concatenate(rows, axis=0).astype(BF16)


def prepare_kernel(
    place_ref, before, after, cur, first, hidden, last, rim, zf, zh, zl, zw, zm, af, ah, al, turn
):
    rows = cur.shape[1]
    wide = cur.shape[2] // 128
    rim[:, RIM : RIM + rows] = cur[...].astype(BF16).astype(F32)
    above = jnp.where(place_ref[1] > 0, before[...].astype(F32), 0.0)
    below = jnp.where(place_ref[1] < place_ref[2] - 1, after[...].astype(F32), 0.0)
    for z in range(cur.shape[0]):
        for c in range(wide):
            n = (z * wide + c) * RIM
            rim[z, 0:RIM, c * 128 : c * 128 + 128] = above[n : n + RIM]
            rim[z, RIM + rows :, c * 128 : c * 128 + 128] = below[n : n + RIM]

    @pl.when(place_ref[0] == 1)
    def _():
        row_band(first, hidden, last, af, ah, al, turn)

    @pl.when(place_ref[0] == 2)
    def _():
        slice_band(first, hidden, last, 1, zf, zh, zl, turn)
        widen(zh, zl, zw, zm)

    @pl.when(place_ref[0] == 3)
    def _():
        slice_band(first, hidden, last, 2, zf, zh, zl, turn)


def prepare(place, rim, current, first, hidden, last):
    layers = hidden.shape[1]
    slices, rows, columns = current.shape
    whole = jax.ShapeDtypeStruct((slices, rows + 2 * RIM, columns), F32)
    shapes = [
        (128, 16),
        (layers, 128, 384),
        (8, 384),
        (layers, 256, 512),
        (16, 768),
        (SPAN * 32, 32),
        (layers, 3, SPAN * 32, 256),
        (3, 8, 256),
    ]
    return pl.pallas_call(
        prepare_kernel,
        out_shape=[whole] + [jax.ShapeDtypeStruct(s, BF16) for s in shapes],
        in_specs=[in_smem()] + [in_vmem()] * 6,
        out_specs=[in_vmem()] * 9,
        scratch_shapes=[pltpu.VMEM((256, 256), F32)],
        compiler_params=params(),
        name="prepare",
    )(place, *rim, current, first, hidden, last)


def side_by_side(value):
    columns = value.shape[1]
    place = lax.broadcasted_iota(jnp.int32, value.shape, 1)
    before = jnp.where(place == 0, 0.0, pltpu.roll(value, 1, axis=1))
    after = jnp.where(place == columns - 1, 0.0, pltpu.roll(value, columns - 1, axis=1))
    return before, value, after


def relu_rows(value, keep):
    value = jnp.maximum(value, 0.0)
    return value if keep is None else jnp.where(keep, value, 0.0)


def sagittal_piece(part, columns, rows, above, below, rim, wf, wh, wl, o_ref, ha, hb):
    width = wf.shape[0]
    depth = wh.shape[0] + 1
    across = slice(part * columns, (part + 1) * columns)

    def kept(layer, y):
        reach = depth - layer
        return above if y < reach else below if y >= reach + rows else None

    empty = jnp.zeros((4, columns), F32)
    for y in range(rows + 2 * depth):
        taps = [rim[:, y + j, across] for j in range(3)] + [empty]
        taps = jnp.concatenate(taps, axis=0).astype(BF16)
        value = jnp.dot(wf[...], taps, preferred_element_type=F32)
        ha[y * width : (y + 1) * width] = relu_rows(value, kept(0, y)).astype(BF16)
    source, target = ha, hb
    for layer in range(wh.shape[0]):
        for y in range(0, rows + 2 * (depth - 1 - layer), 2):
            value = jnp.dot(
                wh[layer], source[y * width : (y + 4) * width], preferred_element_type=F32
            )
            for k in range(2):
                part_k = value[k * width : (k + 1) * width]
                target[(y + k) * width : (y + k + 1) * width] = relu_rows(
                    part_k, kept(layer + 1, y + k)
                ).astype(BF16)
        source, target = target, source
    for y in range(0, rows, 4):
        net = jnp.dot(wl[...], source[y * width : (y + 6) * width], preferred_element_type=F32)
        for z in range(4):
            o_ref[z, y : y + 4, across] = net[z * 4 : z * 4 + 4]


def coronal_piece(start, count, depth, rim, wf, wh, wl, o_ref, h):
    columns = rim.shape[2]
    width = wf.shape[0]
    empty = jnp.zeros((4, columns), F32)
    values = []
    for r in range(count):
        taps = jnp.concatenate([*side_by_side(rim[:, depth + start + r, :]), empty], axis=0)
        values.append(jnp.dot(wf[...], taps.astype(BF16), preferred_element_type=F32))
    for layer in range(wh.shape[0] + 1):
        matrix = wh[layer] if layer < wh.shape[0] else wl[...]
        for r in range(count):
            for j, moved in enumerate(side_by_side(jnp.maximum(values[r], 0.0))):
                h[r, j * width : (j + 1) * width] = moved.astype(BF16)
            values[r] = jnp.dot(matrix, h[r], preferred_element_type=F32)
    for r in range(count):
        o_ref[:, start + r, :] = values[r][0:4]


def spans(rows):
    starts = list(range(0, rows - SPAN, SPAN))
    return starts + [rows - SPAN]


def axial_piece(z, rows, above, below, rim, wf, wh, wl, o_ref, ha, hb):
    channels = wh.shape[3] // (SPAN + 2)
    depth = wh.shape[0] + 1

    def put(target, layer, start, value):
        value = jnp.maximum(value, 0.0)
        reach = depth - layer
        parts = []
        for k in range(SPAN):
            part = value[k * channels : (k + 1) * channels]
            y = start + k
            if y < reach:
                part = jnp.where(above, part, 0.0)
            elif y >= reach + rows:
                part = jnp.where(below, part, 0.0)
            parts.append(part)
        value = jnp.concatenate(parts, axis=0)
        for j, moved in enumerate(side_by_side(value)):
            target[j, start * channels : (start + SPAN) * channels] = moved.astype(BF16)

    def over_columns(matrices, source, start):
        total = None
        for j in range(3):
            window = source[j, start * channels : (start + SPAN + 2) * channels]
            part = jnp.dot(matrices[j], window, preferred_element_type=F32)
            total = part if total is None else total + part
        return total

    around = side_by_side(rim[z])
    empty = jnp.zeros((SPAN + 2, rim.shape[2]), F32)
    for start in spans(rows + 2 * depth):
        taps = [moved[start : start + SPAN + 2] for moved in around] + [empty]
        taps = jnp.concatenate(taps, axis=0).astype(BF16)
        put(ha, 0, start, jnp.dot(wf[...], taps, preferred_element_type=F32))
    source, target = ha, hb
    for layer in range(wh.shape[0]):
        for start in spans(rows + 2 * (depth - 1 - layer)):
            put(target, layer + 1, start, over_columns(wh[layer], source, start))
        source, target = target, source
    for start in spans(rows):
        o_ref[z, start : start + SPAN] = over_columns(wl[...], source, start)[0:SPAN]


def piece_kernel(
    k, place_ref, blk, net, rim, zf, zh, zl, zw, zm, af, ah, al, o_ref, sa, sb, ca, xa, xb
):
    rows = o_ref.shape[1]
    depth = (rim.shape[1] - rows) // 2
    above, below = place_ref[1] > 0, place_ref[1] < place_ref[2] - 1
    o_ref[...] = net[...]

    @pl.when(place_ref[0] == 1)
    def _():
        axial_piece(k, rows, above, below, rim, af, ah, al, o_ref, xa, xb)

    if k < 2:

        @pl.when(place_ref[0] == 2)
        def _():
            half = o_ref.shape[2] // 2
            sagittal_piece(k, half, rows, above, below, rim, zf, zw, zm, o_ref, sa, sb)

    @pl.when(place_ref[0] == 3)
    def _():
        coronal_piece(k * (rows // 4), rows // 4, depth, rim, zf, zh, zl, o_ref, ca)


def piece(k, place, blocks, net, prepared):
    slices, rows, columns = net.shape
    reach = rows + 6
    return pl.pallas_call(
        functools.partial(piece_kernel, k),
        out_shape=jax.ShapeDtypeStruct(net.shape, F32),
        in_specs=[in_smem()] + [in_vmem()] * (2 + len(prepared)),
        out_specs=in_vmem(),
        scratch_shapes=[pltpu.VMEM((reach * 128, columns // 2), BF16)] * 2
        + [pltpu.VMEM((rows // 4, 384, columns), BF16)]
        + [pltpu.VMEM((3, reach * 32, columns), BF16)] * 2,
        compiler_params=params(),
        name=f"piece_{k}",
    )(place, near(blocks), net, *prepared)


def swapped(groups, k):
    return [(g[n], g[(n + k) % len(g)]) for g in groups for n in range(len(g))]


def stage_groups(count):
    near = 4
    strided = 4
    far = count // (near * strided)
    at = lambda f, s, n: (f * strided + s) * near + n
    return [
        [[at(f, s, n) for f in range(far)] for s in range(strided) for n in range(near)],
        [[at(f, s, n) for s in range(strided)] for f in range(far) for n in range(near)],
        [[at(f, s, n) for n in range(near)] for f in range(far) for s in range(strided)],
    ]


def added_up(values, groups):
    total = values.astype(F32)
    for k in range(1, len(groups[0])):
        total = total + lax.ppermute(values, "tile", swapped(groups, k)).astype(F32)
    return total.astype(values.dtype)


def added_up_with_rims(sums, groups, ends):
    far, strided, near = groups
    rows = sums.shape[0] * 2 // 3
    edge = (sums.shape[0] - rows) // 2
    got = lax.ppermute(sums, "tile", swapped(far, 1))
    tail, head = sums[rows : rows + edge], sums[rows + edge :]
    onward, backward = got[rows : rows + edge], got[rows + edge :]
    sums = (sums[0:rows].astype(F32) + got[0:rows].astype(F32)).astype(BF16)
    for n, group in enumerate((strided, near)):
        first, last = ends[n]
        onward = jnp.where(last, onward, tail)
        backward = jnp.where(first, backward, head)
        sums, onward, backward = lax.optimization_barrier((sums, onward, backward))
        up = lax.ppermute(jnp.concatenate([sums, onward]), "tile", swapped(group, 1))
        across = lax.ppermute(sums, "tile", swapped(group, 2))
        down = lax.ppermute(jnp.concatenate([sums, backward]), "tile", swapped(group, 3))
        onward, backward = up[rows:], down[rows:]
        total = sums.astype(F32) + up[0:rows].astype(F32)
        total = total + across.astype(F32) + down[0:rows].astype(F32)
        sums = total.astype(BF16)
    return sums, (onward, backward)


def slices_sent(current):
    return [lax.ppermute(current[k], "agent", [(0, k)]) for k in range(1, current.shape[0])]


def per_device(
    states,
    sinogram,
    blocks,
    block_angle,
    block_detector,
    block_tile,
    conv_first,
    conv_hidden,
    conv_last,
):
    current = states[0]
    tile_count = lax.axis_size("tile")
    tile_place = lax.axis_index("tile")
    agent_place = lax.axis_index("agent")
    place = jnp.stack([agent_place, tile_place, jnp.int32(tile_count)]).astype(jnp.int32)
    ray_total = sinogram.shape[0] * tile_count
    ray_index = block_angle * (current.shape[2] // 128) + block_detector

    within = [lax.shift_right_logical(tile_place, 2) & 3, tile_place & 3]
    ends = [(at == 0, at == 3) for at in within]
    got, ends = lax.optimization_barrier((slices_sent(current), ends))
    sums, start, blocks_here = project(
        place, block_angle, block_detector, block_tile, states, got, sinogram, blocks, ray_total
    )

    groups = stage_groups(tile_count)
    net = jnp.zeros_like(current)
    x_data = start
    sums, rim = added_up_with_rims(sums, groups, ends)
    for _ in range(DATA_STEPS - 2):
        x_data, sums = back_project(
            place, ray_index, block_tile, sums, x_data, sinogram, blocks_here
        )
        for group in groups:
            sums = added_up(sums, group)
    x_data, sums = back_project(place, ray_index, block_tile, sums, x_data, sinogram, blocks_here)
    for n, group in enumerate(groups):
        sums, net = lax.optimization_barrier((sums, net))
        if n == 0:
            prepared = prepare(place, rim, current, conv_first, conv_hidden, conv_last)
        for k in PIECES[n]:
            net = piece(k, place, blocks_here, net, prepared)
        sums = added_up(sums, group)
    sent = back_reflect(ray_index, block_tile, sums, x_data, start, current, net, blocks_here)
    everything = lax.all_gather(sent, "agent")
    return finish(place, everything, current, net)[None]


def solution(mesh):
    placed = (
        P("agent", None, "tile", None),
        P("tile", None, None),
        P("tile", None, None),
        P("tile"),
        P("tile"),
        P("tile"),
        P(),
        P(),
        P(),
    )
    return jax.shard_map(
        per_device,
        mesh=mesh,
        in_specs=placed,
        out_specs=P("agent", None, "tile", None),
        check_vma=False,
    )
```

```python
import functools

import jax
import jax.numpy as jnp
import numpy as np
from jax import lax
from jax.experimental import pallas as pl
from jax.experimental.pallas import tpu as pltpu
from jax.sharding import PartitionSpec as P

DATA_STEPS = 2
F32, BF16 = jnp.float32, jnp.bfloat16
VMEM_LIMIT = 32 << 20
TOGETHER = 4
UNROLL = 16
HOLDERS = (1, 3)
HELD = 2
RIM = 4
CHUNK = 64
PIECES = ((0,), (1, 2), (3,))
SPAN = 6


def params():
    return pltpu.CompilerParams(vmem_limit_bytes=VMEM_LIMIT)


def in_vmem():
    return pl.BlockSpec(memory_space=pltpu.VMEM)


def near(x):
    return pltpu.with_memory_space_constraint(x, pltpu.VMEM)


def in_smem():
    return pl.BlockSpec(memory_space=pltpu.SMEM)


def low_rows():
    return lax.broadcasted_iota(jnp.int32, (8, 128), 0) < 4


def four_blocks(blk, b):
    size = blk.shape[1]
    left = blk[pl.ds(b, 2)].reshape(2 * size, size)
    right = blk[pl.ds(b + 2, 2)].reshape(2 * size, size)
    return jnp.concatenate([left, right], axis=1)


def add_rows(acc, index, value):
    acc[index] = acc[index] + value


def project_blocks(ray_of, tile_ref, pix, blk, acc, ready=None):
    low = low_rows()
    zero = jnp.zeros((8, 128), F32)

    def body(i, carry):
        if ready is not None:
            ready(i)
        outs = []
        for u in range(UNROLL):
            b = (i * UNROLL + u) * TOGETHER
            t = [pix[tile_ref[b + k]] for k in range(TOGETHER)]
            upper = jnp.concatenate([jnp.where(low, t[0], t[1]), zero], axis=0)
            lower = jnp.concatenate([zero, jnp.where(low, t[2], t[3])], axis=0)
            lhs = jnp.concatenate([upper.astype(BF16), lower.astype(BF16)], axis=1)
            outs.append(
                lax.dot_general(
                    lhs, four_blocks(blk, b), (((1,), (1,)), ((), ())), preferred_element_type=F32
                )
            )
        for u in range(UNROLL):
            b = (i * UNROLL + u) * TOGETHER
            out = outs[u]
            add_rows(acc, ray_of(b), jnp.where(low, out[0:8, 0:128], 0.0))
            add_rows(acc, ray_of(b + 1), jnp.where(low, 0.0, out[0:8, 128:256]))
            add_rows(acc, ray_of(b + 2), jnp.where(low, out[8:16, 0:128], 0.0))
            add_rows(acc, ray_of(b + 3), jnp.where(low, 0.0, out[8:16, 128:256]))
        return carry

    lax.fori_loop(0, blk.shape[0] // (TOGETHER * UNROLL), body, 0)


def back_blocks(ray_ref, tile_ref, res, blk, acc):
    low = low_rows()

    def body(i, carry):
        outs = []
        for u in range(UNROLL):
            b = (i * UNROLL + u) * TOGETHER
            t = [res[ray_ref[b + k]] for k in range(TOGETHER)]
            left = jnp.concatenate([jnp.where(low, t[0], 0.0), jnp.where(low, t[2], 0.0)], axis=0)
            right = jnp.concatenate([jnp.where(low, 0.0, t[1]), jnp.where(low, 0.0, t[3])], axis=0)
            lhs = jnp.concatenate([left.astype(BF16), right.astype(BF16)], axis=1)
            outs.append(jnp.dot(lhs, four_blocks(blk, b), preferred_element_type=F32))
        for u in range(UNROLL):
            b = (i * UNROLL + u) * TOGETHER
            upper, lower = outs[u][0:8, 0:128], outs[u][8:16, 128:256]
            add_rows(acc, tile_ref[b], jnp.where(low, upper, 0.0))
            add_rows(acc, tile_ref[b + 1], jnp.where(low, 0.0, upper))
            add_rows(acc, tile_ref[b + 2], jnp.where(low, lower, 0.0))
            add_rows(acc, tile_ref[b + 3], jnp.where(low, 0.0, lower))
        return carry

    lax.fori_loop(0, blk.shape[0] // (TOGETHER * UNROLL), body, 0)


def twice(ref, index, n, value):
    ref[index, n, :] = value
    ref[index, n + 4, :] = value


def load_pixels(x, pix):
    for n in range(HELD):
        for c in range(x.shape[2] // 128):
            own = pl.ds(c, x.shape[1], stride=x.shape[2] // 128)
            twice(pix, own, n, x[n, :, c * 128 : c * 128 + 128])


def load_residual(r_ref, res):
    rays = res.shape[0]
    for n in range(HELD):
        twice(res, slice(None), n, r_ref[n * rays : (n + 1) * rays].astype(F32))


def moved_by(x, back):
    parts = []
    for n in range(HELD):
        columns = []
        for c in range(x.shape[2] // 128):
            own = pl.ds(c, x.shape[1], stride=x.shape[2] // 128)
            columns.append(back[own, n, :] + back[own, n + 4, :])
        parts.append(x[n] - 0.8 * jnp.concatenate(columns, axis=1))
    return parts


def store_rays(place_ref, sino_ref, acc, total, o_ref):
    rays = acc.shape[0]
    own = sino_ref.shape[0]
    mine = pl.ds(pl.multiple_of(place_ref[1] * own, own), own)
    for n in range(HELD):
        total[...] = acc[:, n, :] + acc[:, n + 4, :]
        for half in range(sino_ref.shape[1] // HELD):

            @pl.when(place_ref[0] // 2 == half)
            def _():
                total[mine] = total[mine] - sino_ref[:, half * HELD + n, :]

        o_ref[n * rays : (n + 1) * rays] = total[...].astype(o_ref.dtype)


def in_pieces(cur, first):
    pieces = []
    for z in range(cur.shape[0]):
        for c in range(cur.shape[2] // 128):
            pieces.append(cur[z, first : first + RIM, c * 128 : c * 128 + 128])
    return jnp.concatenate(pieces, axis=0)


def project_kernel(
    place_ref,
    angle_in,
    detector_in,
    tile_in,
    states_in,
    got_1,
    got_3,
    sino_in,
    blk_in,
    o_ref,
    edge_ref,
    start_ref,
    blk,
    angle,
    detector,
    tile,
    cur,
    sino,
    pix,
    acc,
    total,
    small_sems,
    block_sems,
):
    small = [
        pltpu.make_async_copy(source, target, small_sems.at[n])
        for n, (source, target) in enumerate(
            [
                (states_in.at[0], cur),
                (angle_in, angle),
                (detector_in, detector),
                (tile_in, tile),
                (sino_in, sino),
            ]
        )
    ]
    for copy in small:
        copy.start()
    chunk = CHUNK

    def chunk_copy(i):
        part = pl.ds(i * chunk, chunk)
        return pltpu.make_async_copy(blk_in.at[part], blk.at[part], block_sems.at[i])

    ahead = 2
    count = blk.shape[0] // chunk
    for i in range(ahead):
        chunk_copy(i).start()

    def ready(i):
        chunk_copy(i).wait()

        @pl.when(i + ahead < count)
        def _():
            chunk_copy(i + ahead).start()

    acc[...] = jnp.zeros_like(acc)
    for copy in small:
        copy.wait()
    start_ref[...] = got_1[...] + got_3[...]
    tail = in_pieces(cur, cur.shape[1] - RIM).astype(BF16)
    head = in_pieces(cur, 0).astype(BF16)
    edge = tail.shape[0]
    edge_ref[0:edge] = tail
    edge_ref[edge:] = head
    sums = o_ref.shape[0] - edge
    at_end = (place_ref[1] // 4) % 4 == 3

    @pl.when(at_end)
    def _():
        o_ref[sums:] = tail

    @pl.when(jnp.logical_not(at_end))
    def _():
        o_ref[sums:] = head

    load_pixels(start_ref, pix)
    wide = cur.shape[2] // 128
    project_blocks(
        lambda b: angle[b] * wide + detector[b],
        tile,
        pix,
        blk,
        acc,
        ready,
    )
    store_rays(place_ref, sino, acc, total, o_ref)


def project(place, angle, detector, tile, states, got, sinogram, blocks, ray_total):
    shape = got[0].shape
    count = blocks.shape[0]
    edge = RIM * states.shape[1] * states.shape[3] // 128
    far = pl.BlockSpec(memory_space=pltpu.HBM)
    stay = lambda x: pltpu.with_memory_space_constraint(x, pltpu.HBM)
    return pl.pallas_call(
        project_kernel,
        out_shape=(
            jax.ShapeDtypeStruct((HELD * ray_total + edge, 128), BF16),
            jax.ShapeDtypeStruct((2 * edge, 128), BF16),
            jax.ShapeDtypeStruct(shape, F32),
            pltpu.VMEM(blocks.shape, BF16),
        ),
        in_specs=[in_smem()] + [far] * 4 + [in_vmem()] * 2 + [far] * 2,
        out_specs=(in_vmem(),) * 4,
        scratch_shapes=[
            pltpu.SMEM((count,), jnp.int32),
            pltpu.SMEM((count,), jnp.int32),
            pltpu.SMEM((count,), jnp.int32),
            pltpu.VMEM(states.shape[1:], F32),
            pltpu.VMEM(sinogram.shape, F32),
            pltpu.VMEM((shape[1] * shape[2] // 128, 8, 128), F32),
            pltpu.VMEM((ray_total, 8, 128), F32),
            pltpu.VMEM((ray_total, 128), F32),
            pltpu.SemaphoreType.DMA((5,)),
            pltpu.SemaphoreType.DMA((count // CHUNK,)),
        ],
        compiler_params=params(),
        name="project",
    )(
        place,
        stay(angle),
        stay(detector),
        stay(tile),
        stay(states),
        *got,
        stay(sinogram),
        stay(blocks),
    )


def back_project_kernel(
    place_ref, ray_ref, tile_ref, r_ref, x_ref, sino_ref, blk, x_out, o_ref, res, pix, back, acc, total
):
    load_residual(r_ref, res)
    back[...] = jnp.zeros_like(back)
    back_blocks(ray_ref, tile_ref, res, blk, back)
    for n, moved in enumerate(moved_by(x_ref, back)):
        x_out[n] = moved
    load_pixels(x_out, pix)
    acc[...] = jnp.zeros_like(acc)
    project_blocks(lambda b: ray_ref[b], tile_ref, pix, blk, acc)
    store_rays(place_ref, sino_ref, acc, total, o_ref)


def back_project(place, ray_index, tile_index, residual, x, sinogram, blocks):
    ray_total = residual.shape[0] // HELD
    tiles = x.shape[1] * x.shape[2] // 128
    return pl.pallas_call(
        back_project_kernel,
        out_shape=(
            jax.ShapeDtypeStruct(x.shape, F32),
            jax.ShapeDtypeStruct(residual.shape, BF16),
        ),
        in_specs=[in_smem()] * 3 + [in_vmem()] * 4,
        out_specs=(in_vmem(), in_vmem()),
        scratch_shapes=[
            pltpu.VMEM((ray_total, 8, 128), F32),
            pltpu.VMEM((tiles, 8, 128), F32),
            pltpu.VMEM((tiles, 8, 128), F32),
            pltpu.VMEM((ray_total, 8, 128), F32),
            pltpu.VMEM((ray_total, 128), F32),
        ],
        compiler_params=params(),
        name="back_project",
    )(place, ray_index, tile_index, residual, x, sinogram, near(blocks))


def back_kernel(ray_ref, tile_ref, r_ref, x_ref, start_ref, cur_ref, net_ref, blk, o_ref, res, back):
    load_residual(r_ref, res)
    back[...] = jnp.zeros_like(back)
    for z in range(net_ref.shape[0]):
        o_ref[HELD + z] = (cur_ref[z] - 2.0 * net_ref[z]).astype(o_ref.dtype)
    back_blocks(ray_ref, tile_ref, res, blk, back)
    for n, moved in enumerate(moved_by(x_ref, back)):
        o_ref[n] = (2.0 * moved - start_ref[n]).astype(o_ref.dtype)


def back_reflect(ray_index, tile_index, residual, x, start, current, net, blocks):
    ray_total = residual.shape[0] // HELD
    tiles = x.shape[1] * x.shape[2] // 128
    return pl.pallas_call(
        back_kernel,
        out_shape=jax.ShapeDtypeStruct((HELD + net.shape[0], *x.shape[1:]), BF16),
        in_specs=[in_smem()] * 2 + [in_vmem()] * 6,
        out_specs=in_vmem(),
        scratch_shapes=[
            pltpu.VMEM((ray_total, 8, 128), F32),
            pltpu.VMEM((tiles, 8, 128), F32),
        ],
        compiler_params=params(),
        name="back_reflect",
    )(ray_index, tile_index, residual, x, start, current, net, near(blocks))


def finish_kernel(place_ref, all_ref, cur_ref, net_ref, o_ref):
    for z in range(o_ref.shape[0]):
        data = all_ref[HOLDERS[z // HELD], z % HELD].astype(F32)
        total = data
        for k in range(1, all_ref.shape[0]):
            total = total + all_ref[k, HELD + z].astype(F32)

        @pl.when(place_ref[0] == 0)
        def _():
            o_ref[z] = 0.25 * total + 0.5 * (cur_ref[z] - data)

        @pl.when(place_ref[0] != 0)
        def _():
            o_ref[z] = 0.25 * total + net_ref[z]


def finish(place, everything, current, net):
    return pl.pallas_call(
        finish_kernel,
        out_shape=jax.ShapeDtypeStruct(current.shape, F32),
        in_specs=[in_smem()] + [in_vmem()] * 3,
        out_specs=in_vmem(),
        compiler_params=params(),
        name="finish",
    )(place, everything, current, net)


def lanes(parts, count, height, width):
    empty = jnp.zeros((height, width), F32)
    return jnp.concatenate([parts.get(n, empty) for n in range(count)], axis=1)


def slice_band(first, hidden, last, o, zf, zh, zl, turn):
    turn[...] = jnp.zeros_like(turn)
    for j in range(3):
        for z in range(4):
            near = {y: z - y + 1 for y in range(4) if 0 <= z - y + 1 < 3}
            n = j * 4 + z
            parts = {y: first[o, i, j : j + 1, :].astype(F32) for y, i in near.items()}
            turn[n : n + 1, 0:128] = lanes(parts, 4, 1, 32)
    zf[...] = jnp.transpose(turn[0:128, 0:128])[:, 0:16].astype(BF16)
    for layer in range(hidden.shape[1]):
        for j in range(3):
            for z in range(4):
                near = {y: z - y + 1 for y in range(4) if 0 <= z - y + 1 < 3}
                parts = {y: hidden[o, layer, i, j].astype(F32) for y, i in near.items()}
                turn[z * 32 : z * 32 + 32, 0:128] = lanes(parts, 4, 32, 32)
            zh[layer, :, j * 128 : j * 128 + 128] = jnp.transpose(turn[0:128, 0:128]).astype(BF16)
    rows = []
    for y in range(4):
        parts = {
            j * 4 + z: last[o, z - y + 1, j : j + 1, :].astype(F32)
            for j in range(3)
            for z in range(4)
            if 0 <= z - y + 1 < 3
        }
        rows.append(lanes(parts, 12, 1, 32))
    zl[...] = jnp.concatenate(rows + [jnp.zeros((4, 384), F32)], axis=0).astype(BF16)


def widen(zh, zl, zw, zm):
    for layer in range(zh.shape[0]):
        zw[layer, 0:128, 0:384] = zh[layer]
        zw[layer, 0:128, 384:512] = jnp.zeros((128, 128), BF16)
        zw[layer, 128:256, 0:128] = jnp.zeros((128, 128), BF16)
        zw[layer, 128:256, 128:512] = zh[layer]
    plain = zl[...].astype(F32)
    rows = []
    for z in range(4):
        for a in range(4):
            parts = {a + n: plain[z : z + 1, n * 128 : n * 128 + 128] for n in range(3)}
            rows.append(lanes(parts, 6, 1, 128))
    zm[...] = jnp.concatenate(rows, axis=0).astype(BF16)


def row_band(first, hidden, last, af, ah, al, turn):
    turn[...] = jnp.zeros_like(turn)
    for j in range(3):
        for y in range(SPAN + 2):
            parts = {m: first[0, y - m, j : j + 1, :].astype(F32) for m in range(SPAN) if 0 <= y - m < 3}
            n = j * (SPAN + 2) + y
            turn[n : n + 1] = lanes(parts, 8, 1, 32)
    af[...] = jnp.transpose(turn[0:128])[0 : SPAN * 32, 0:32].astype(BF16)
    for layer in range(hidden.shape[1]):
        for j in range(3):
            for y in range(SPAN + 2):
                parts = {m: hidden[0, layer, y - m, j].astype(F32) for m in range(SPAN) if 0 <= y - m < 3}
                turn[y * 32 : y * 32 + 32] = lanes(parts, 8, 32, 32)
            ah[layer, j] = jnp.transpose(turn[...])[0 : SPAN * 32].astype(BF16)
    for j in range(3):
        rows = []
        for m in range(SPAN):
            parts = {m + i: last[0, i, j : j + 1, :].astype(F32) for i in range(3)}
            rows.append(lanes(parts, 8, 1, 32))
        rows.append(jnp.zeros((2, 256), F32))
        al[j] = jnp.concatenate(rows, axis=0).astype(BF16)


def prepare_kernel(
    place_ref, first, hidden, last, zf, zh, zl, zw, zm, af, ah, al, turn
):
    @pl.when(place_ref[0] == 1)
    def _():
        row_band(first, hidden, last, af, ah, al, turn)

    @pl.when(place_ref[0] == 2)
    def _():
        slice_band(first, hidden, last, 1, zf, zh, zl, turn)
        widen(zh, zl, zw, zm)

    @pl.when(place_ref[0] == 3)
    def _():
        slice_band(first, hidden, last, 2, zf, zh, zl, turn)


def prepare(place, first, hidden, last):
    layers = hidden.shape[1]
    shapes = [
        (128, 16),
        (layers, 128, 384),
        (8, 384),
        (layers, 256, 512),
        (16, 768),
        (SPAN * 32, 32),
        (layers, 3, SPAN * 32, 256),
        (3, 8, 256),
    ]
    return pl.pallas_call(
        prepare_kernel,
        out_shape=[jax.ShapeDtypeStruct(s, BF16) for s in shapes],
        in_specs=[in_smem()] + [in_vmem()] * 3,
        out_specs=[in_vmem()] * 8,
        scratch_shapes=[pltpu.VMEM((256, 256), F32)],
        compiler_params=params(),
        name="prepare",
    )(place, first, hidden, last)


def side_by_side(value):
    columns = value.shape[1]
    place = lax.broadcasted_iota(jnp.int32, value.shape, 1)
    before = jnp.where(place == 0, 0.0, pltpu.roll(value, 1, axis=1))
    after = jnp.where(place == columns - 1, 0.0, pltpu.roll(value, columns - 1, axis=1))
    return before, value, after


def relu_rows(value, keep):
    value = jnp.maximum(value, 0.0)
    return value if keep is None else jnp.where(keep, value, 0.0)


def sagittal_piece(part, columns, rows, above, below, rim, wf, wh, wl, o_ref, ha, hb):
    width = wf.shape[0]
    depth = wh.shape[0] + 1
    across = slice(part * columns, (part + 1) * columns)

    def kept(layer, y):
        reach = depth - layer
        return above if y < reach else below if y >= reach + rows else None

    empty = jnp.zeros((4, columns), F32)
    for y in range(rows + 2 * depth):
        taps = [rim[:, y + j, across] for j in range(3)] + [empty]
        taps = jnp.concatenate(taps, axis=0).astype(BF16)
        value = jnp.dot(wf[...], taps, preferred_element_type=F32)
        ha[y * width : (y + 1) * width] = relu_rows(value, kept(0, y)).astype(BF16)
    source, target = ha, hb
    for layer in range(wh.shape[0]):
        for y in range(0, rows + 2 * (depth - 1 - layer), 2):
            value = jnp.dot(
                wh[layer], source[y * width : (y + 4) * width], preferred_element_type=F32
            )
            for k in range(2):
                part_k = value[k * width : (k + 1) * width]
                target[(y + k) * width : (y + k + 1) * width] = relu_rows(
                    part_k, kept(layer + 1, y + k)
                ).astype(BF16)
        source, target = target, source
    for y in range(0, rows, 4):
        net = jnp.dot(wl[...], source[y * width : (y + 6) * width], preferred_element_type=F32)
        for z in range(4):
            o_ref[z, y : y + 4, across] = net[z * 4 : z * 4 + 4]


def coronal_piece(start, count, depth, rim, wf, wh, wl, o_ref, h):
    columns = rim.shape[2]
    width = wf.shape[0]
    empty = jnp.zeros((4, columns), F32)
    values = []
    for r in range(count):
        taps = jnp.concatenate([*side_by_side(rim[:, depth + start + r, :]), empty], axis=0)
        values.append(jnp.dot(wf[...], taps.astype(BF16), preferred_element_type=F32))
    for layer in range(wh.shape[0] + 1):
        matrix = wh[layer] if layer < wh.shape[0] else wl[...]
        for r in range(count):
            for j, moved in enumerate(side_by_side(jnp.maximum(values[r], 0.0))):
                h[r, j * width : (j + 1) * width] = moved.astype(BF16)
            values[r] = jnp.dot(matrix, h[r], preferred_element_type=F32)
    for r in range(count):
        o_ref[:, start + r, :] = values[r][0:4]


def spans(rows):
    starts = list(range(0, rows - SPAN, SPAN))
    return starts + [rows - SPAN]


def axial_piece(z, rows, above, below, rim, wf, wh, wl, o_ref, ha, hb):
    channels = wh.shape[3] // (SPAN + 2)
    depth = wh.shape[0] + 1

    def put(target, layer, start, value):
        value = jnp.maximum(value, 0.0)
        reach = depth - layer
        parts = []
        for k in range(SPAN):
            part = value[k * channels : (k + 1) * channels]
            y = start + k
            if y < reach:
                part = jnp.where(above, part, 0.0)
            elif y >= reach + rows:
                part = jnp.where(below, part, 0.0)
            parts.append(part)
        value = jnp.concatenate(parts, axis=0)
        for j, moved in enumerate(side_by_side(value)):
            target[j, start * channels : (start + SPAN) * channels] = moved.astype(BF16)

    def over_columns(matrices, source, start):
        total = None
        for j in range(3):
            window = source[j, start * channels : (start + SPAN + 2) * channels]
            part = jnp.dot(matrices[j], window, preferred_element_type=F32)
            total = part if total is None else total + part
        return total

    around = side_by_side(rim[z])
    empty = jnp.zeros((SPAN + 2, rim.shape[2]), F32)
    for start in spans(rows + 2 * depth):
        taps = [moved[start : start + SPAN + 2] for moved in around] + [empty]
        taps = jnp.concatenate(taps, axis=0).astype(BF16)
        put(ha, 0, start, jnp.dot(wf[...], taps, preferred_element_type=F32))
    source, target = ha, hb
    for layer in range(wh.shape[0]):
        for start in spans(rows + 2 * (depth - 1 - layer)):
            put(target, layer + 1, start, over_columns(wh[layer], source, start))
        source, target = target, source
    for start in spans(rows):
        o_ref[z, start : start + SPAN] = over_columns(wl[...], source, start)[0:SPAN]


def piece_kernel(
    k,
    place_ref,
    blk,
    net,
    before,
    after,
    cur,
    zf,
    zh,
    zl,
    zw,
    zm,
    af,
    ah,
    al,
    o_ref,
    rim,
    sa,
    sb,
    ca,
    xa,
    xb,
):
    rows = o_ref.shape[1]
    depth = RIM
    above, below = place_ref[1] > 0, place_ref[1] < place_ref[2] - 1
    o_ref[...] = net[...]

    @pl.when(place_ref[0] > 0)
    def _():
        wide = cur.shape[2] // 128
        rim[:, RIM : RIM + rows] = cur[...].astype(BF16).astype(F32)
        over = jnp.where(above, before[...].astype(F32), 0.0)
        under = jnp.where(below, after[...].astype(F32), 0.0)
        for z in range(cur.shape[0]):
            for c in range(wide):
                n = (z * wide + c) * RIM
                rim[z, 0:RIM, c * 128 : c * 128 + 128] = over[n : n + RIM]
                rim[z, RIM + rows :, c * 128 : c * 128 + 128] = under[n : n + RIM]

    @pl.when(place_ref[0] == 1)
    def _():
        axial_piece(k, rows, above, below, rim, af, ah, al, o_ref, xa, xb)

    if k < 2:

        @pl.when(place_ref[0] == 2)
        def _():
            half = o_ref.shape[2] // 2
            sagittal_piece(k, half, rows, above, below, rim, zf, zw, zm, o_ref, sa, sb)

    @pl.when(place_ref[0] == 3)
    def _():
        coronal_piece(k * (rows // 4), rows // 4, depth, rim, zf, zh, zl, o_ref, ca)


def piece(k, place, blocks, net, rim, current, prepared):
    slices, rows, columns = net.shape
    reach = rows + 6
    assert reach == rows + 2 * RIM - 2
    return pl.pallas_call(
        functools.partial(piece_kernel, k),
        out_shape=jax.ShapeDtypeStruct(net.shape, F32),
        in_specs=[in_smem()] + [in_vmem()] * (5 + len(prepared)),
        out_specs=in_vmem(),
        scratch_shapes=[pltpu.VMEM((slices, rows + 2 * RIM, columns), F32)]
        + [pltpu.VMEM((reach * 128, columns // 2), BF16)] * 2
        + [pltpu.VMEM((rows // 4, 384, columns), BF16)]
        + [pltpu.VMEM((3, reach * 32, columns), BF16)] * 2,
        compiler_params=params(),
        name=f"piece_{k}",
    )(place, near(blocks), net, *rim, current, *prepared)


def swapped(groups, k, agents):
    count = sum(len(g) for g in groups)
    pairs = [(g[n], g[(n + k) % len(g)]) for g in groups for n in range(len(g))]
    return [(a * count + i, a * count + j) for a in agents for i, j in pairs]


def stage_groups(count):
    near = 4
    strided = 4
    far = count // (near * strided)
    at = lambda f, s, n: (f * strided + s) * near + n
    return [
        [[at(f, s, n) for f in range(far)] for s in range(strided) for n in range(near)],
        [[at(f, s, n) for s in range(strided)] for f in range(far) for n in range(near)],
        [[at(f, s, n) for n in range(near)] for f in range(far) for s in range(strided)],
    ]


BOTH = ("agent", "tile")


def added_up(values, groups):
    total = values.astype(F32)
    for k in range(1, len(groups[0])):
        total = total + lax.ppermute(values, BOTH, swapped(groups, k, HOLDERS)).astype(F32)
    return total.astype(values.dtype)


def added_up_with_rims(first, own, groups, ends, between):
    agents = (1, 2, 3)
    far, strided, near_by = groups
    edge = own.shape[0] // 2
    rows = first.shape[0] - edge
    got = lax.ppermute(first, BOTH, swapped(far, 1, agents))
    tail, head = own[0:edge], own[edge:]
    onward = backward = got[rows:]
    sums = (first[0:rows].astype(F32) + got[0:rows].astype(F32)).astype(BF16)
    made = None
    for n, group in enumerate((strided, near_by)):
        at_first, at_last = ends[n]
        onward = jnp.where(at_last, onward, tail)
        backward = jnp.where(at_first, backward, head)
        sums, onward, backward = lax.optimization_barrier((sums, onward, backward))
        if n == 0:
            made = between(sums)
        up = lax.ppermute(jnp.concatenate([sums, onward]), BOTH, swapped(group, 1, agents))
        across = lax.ppermute(sums, BOTH, swapped(group, 2, agents))
        down = lax.ppermute(jnp.concatenate([sums, backward]), BOTH, swapped(group, 3, agents))
        onward, backward = up[rows:], down[rows:]
        total = sums.astype(F32) + up[0:rows].astype(F32)
        total = total + across.astype(F32) + down[0:rows].astype(F32)
        sums = total.astype(BF16)
        if n == 0:
            sums, made = lax.optimization_barrier((sums, made))
    return sums, (onward, backward), made


def slices_sent(current):
    return [
        lax.ppermute(current[n * HELD : (n + 1) * HELD], "agent", [(0, holder)])
        for n, holder in enumerate(HOLDERS)
    ]


def per_device(
    states,
    sinogram,
    blocks,
    block_angle,
    block_detector,
    block_tile,
    conv_first,
    conv_hidden,
    conv_last,
):
    current = states[0]
    tile_count = lax.axis_size("tile")
    tile_place = lax.axis_index("tile")
    agent_place = lax.axis_index("agent")
    place = jnp.stack([agent_place, tile_place, jnp.int32(tile_count)]).astype(jnp.int32)
    ray_total = sinogram.shape[0] * tile_count
    ray_index = block_angle * (current.shape[2] // 128) + block_detector

    within = [lax.shift_right_logical(tile_place, 2) & 3, tile_place & 3]
    ends = [(at == 0, at == 3) for at in within]
    got, ends = lax.optimization_barrier((slices_sent(current), ends))
    first, own, start, blocks_here = project(
        place, block_angle, block_detector, block_tile, states, got, sinogram, blocks, ray_total
    )

    groups = stage_groups(tile_count)
    net = jnp.zeros_like(current)
    x_data = start

    def weights(sums):
        tied, _ = lax.optimization_barrier((place, sums))
        return prepare(tied, conv_first, conv_hidden, conv_last)

    sums, rim, prepared = added_up_with_rims(first, own, groups, ends, weights)
    for _ in range(DATA_STEPS - 2):
        x_data, sums = back_project(
            place, ray_index, block_tile, sums, x_data, sinogram, blocks_here
        )
        for group in groups:
            sums = added_up(sums, group)
    x_data, sums = back_project(place, ray_index, block_tile, sums, x_data, sinogram, blocks_here)
    for n, group in enumerate(groups):
        sums, net = lax.optimization_barrier((sums, net))
        for k in PIECES[n]:
            net = piece(k, place, blocks_here, net, rim, current, prepared)
        sums = added_up(sums, group)
    sent = back_reflect(ray_index, block_tile, sums, x_data, start, current, net, blocks_here)
    everything = lax.all_gather(sent, "agent")
    return finish(place, everything, current, net)[None]


def solution(mesh):
    placed = (
        P("agent", None, "tile", None),
        P("tile", None, None),
        P("tile", None, None),
        P("tile"),
        P("tile"),
        P("tile"),
        P(),
        P(),
        P(),
    )
    return jax.shard_map(
        per_device,
        mesh=mesh,
        in_specs=placed,
        out_specs=P("agent", None, "tile", None),
        check_vma=False,
    )
```

```python
import functools

import jax
import jax.numpy as jnp
import numpy as np
from jax import lax
from jax.experimental import pallas as pl
from jax.experimental.pallas import tpu as pltpu
from jax.sharding import PartitionSpec as P

DATA_STEPS = 2
F32, BF16 = jnp.float32, jnp.bfloat16
VMEM_LIMIT = 32 << 20
TOGETHER = 4
UNROLL = 64
RIM = 4
CHUNK = 64
PIECES = ((0,), (1, 2), (3,))
SPAN = 6


def params():
    return pltpu.CompilerParams(vmem_limit_bytes=VMEM_LIMIT)


def in_vmem():
    return pl.BlockSpec(memory_space=pltpu.VMEM)


def near(x):
    return pltpu.with_memory_space_constraint(x, pltpu.VMEM)


def in_smem():
    return pl.BlockSpec(memory_space=pltpu.SMEM)


def low_rows():
    return lax.broadcasted_iota(jnp.int32, (8, 128), 0) < 4


def four_blocks(blk, b):
    size = blk.shape[1]
    left = blk[pl.ds(b, 2)].reshape(2 * size, size)
    right = blk[pl.ds(b + 2, 2)].reshape(2 * size, size)
    return jnp.concatenate([left, right], axis=1)


def row(ref, index):
    return ref[pl.ds(index, 8, stride=0), :]


def add_rows(acc, index, value):
    acc[index] = acc[index] + value


def project_blocks(ray_of, tile_ref, pix, blk, acc, ready=None, unroll=UNROLL):
    low = low_rows()
    zero = jnp.zeros((8, 128), F32)

    def body(i, carry):
        if ready is not None:
            ready(i)
        outs = []
        for u in range(unroll):
            b = (i * unroll + u) * TOGETHER
            t = [row(pix, tile_ref[b + k]) for k in range(TOGETHER)]
            upper = jnp.concatenate([jnp.where(low, t[0], t[1]), zero], axis=0)
            lower = jnp.concatenate([zero, jnp.where(low, t[2], t[3])], axis=0)
            lhs = jnp.concatenate([upper.astype(BF16), lower.astype(BF16)], axis=1)
            outs.append(
                lax.dot_general(
                    lhs, four_blocks(blk, b), (((1,), (1,)), ((), ())), preferred_element_type=F32
                )
            )
        for u in range(unroll):
            b = (i * unroll + u) * TOGETHER
            out = outs[u]
            add_rows(acc, ray_of(b), jnp.where(low, out[0:8, 0:128], 0.0))
            add_rows(acc, ray_of(b + 1), jnp.where(low, 0.0, out[0:8, 128:256]))
            add_rows(acc, ray_of(b + 2), jnp.where(low, out[8:16, 0:128], 0.0))
            add_rows(acc, ray_of(b + 3), jnp.where(low, 0.0, out[8:16, 128:256]))
        return carry

    lax.fori_loop(0, blk.shape[0] // (TOGETHER * unroll), body, 0)


def back_blocks(ray_ref, tile_ref, res, blk, acc):
    low = low_rows()

    def body(i, carry):
        outs = []
        for u in range(UNROLL):
            b = (i * UNROLL + u) * TOGETHER
            t = [row(res, ray_ref[b + k]) for k in range(TOGETHER)]
            left = jnp.concatenate([jnp.where(low, t[0], 0.0), jnp.where(low, t[2], 0.0)], axis=0)
            right = jnp.concatenate([jnp.where(low, 0.0, t[1]), jnp.where(low, 0.0, t[3])], axis=0)
            lhs = jnp.concatenate([left.astype(BF16), right.astype(BF16)], axis=1)
            outs.append(jnp.dot(lhs, four_blocks(blk, b), preferred_element_type=F32))
        for u in range(UNROLL):
            b = (i * UNROLL + u) * TOGETHER
            upper, lower = outs[u][0:8, 0:128], outs[u][8:16, 128:256]
            add_rows(acc, tile_ref[b], jnp.where(low, upper, 0.0))
            add_rows(acc, tile_ref[b + 1], jnp.where(low, 0.0, upper))
            add_rows(acc, tile_ref[b + 2], jnp.where(low, lower, 0.0))
            add_rows(acc, tile_ref[b + 3], jnp.where(low, 0.0, lower))
        return carry

    lax.fori_loop(0, blk.shape[0] // (TOGETHER * UNROLL), body, 0)


def tiles_of(x_shape):
    wide = x_shape[1] // 128
    return [(r, c, slice(c * 128, c * 128 + 128)) for r in range(x_shape[0]) for c in range(wide)]


def load_pixels(value, pix):
    wide = value.shape[1] // 128
    for r, c, columns in tiles_of(value.shape):
        pix[r * wide + c : r * wide + c + 1] = value[r : r + 1, columns]


def moved_by(x, back):
    wide = x.shape[1] // 128
    rows = back.shape[0]
    columns = []
    for c in range(wide):
        own = pl.ds(c, rows // wide, stride=wide)
        columns.append(back[own, 0, :] + back[own, 4, :])
    return x - 0.8 * jnp.concatenate(columns, axis=1)


def store_rays(place_ref, sino_ref, acc, total, o_ref):
    total[0 : acc.shape[0]] = acc[:, 0, :] + acc[:, 4, :]
    own = sino_ref.shape[0]
    mine = pl.ds(pl.multiple_of(place_ref[1] * own, own), own)
    for z in range(sino_ref.shape[1]):

        @pl.when(place_ref[0] == z)
        def _():
            total[mine] = total[mine] - sino_ref[:, z, :]

    o_ref[0 : acc.shape[0]] = total[0 : acc.shape[0]].astype(o_ref.dtype)


def in_pieces(cur, first):
    pieces = []
    for z in range(cur.shape[0]):
        for c in range(cur.shape[2] // 128):
            pieces.append(cur[z, first : first + RIM, c * 128 : c * 128 + 128])
    return jnp.concatenate(pieces, axis=0)


def project_kernel(
    place_ref,
    angle_in,
    detector_in,
    tile_in,
    states_in,
    got_1,
    got_2,
    got_3,
    sino_in,
    blk_in,
    o_ref,
    edge_ref,
    start_ref,
    blk,
    angle,
    detector,
    tile,
    cur,
    sino,
    pix,
    acc,
    total,
    small_sems,
    block_sems,
):
    small = [
        pltpu.make_async_copy(source, target, small_sems.at[n])
        for n, (source, target) in enumerate(
            [
                (states_in.at[0], cur),
                (angle_in, angle),
                (detector_in, detector),
                (tile_in, tile),
                (sino_in, sino),
            ]
        )
    ]
    for copy in small:
        copy.start()
    chunk = CHUNK

    def chunk_copy(i):
        part = pl.ds(i * chunk, chunk)
        return pltpu.make_async_copy(blk_in.at[part], blk.at[part], block_sems.at[i])

    ahead = 2
    count = blk.shape[0] // chunk
    for i in range(ahead):
        chunk_copy(i).start()

    def ready(i):
        chunk_copy(i).wait()

        @pl.when(i + ahead < count)
        def _():
            chunk_copy(i + ahead).start()

    acc[...] = jnp.zeros_like(acc)
    for copy in small:
        copy.wait()
    @pl.when(place_ref[0] == 0)
    def _():
        start_ref[...] = cur[0]

    for k, value in enumerate((got_1, got_2, got_3)):

        @pl.when(place_ref[0] == k + 1)
        def _():
            start_ref[...] = value[...]

    tail = in_pieces(cur, cur.shape[1] - RIM).astype(BF16)
    head = in_pieces(cur, 0).astype(BF16)
    edge = tail.shape[0]
    edge_ref[0:edge] = tail
    edge_ref[edge:] = head
    rows = acc.shape[0]
    at_end = (place_ref[1] // 4) % 4 == 3

    @pl.when(at_end)
    def _():
        o_ref[rows:] = tail

    @pl.when(jnp.logical_not(at_end))
    def _():
        o_ref[rows:] = head

    load_pixels(start_ref[...], pix)
    wide = cur.shape[2] // 128
    project_blocks(
        lambda b: angle[b] * wide + detector[b],
        tile,
        pix,
        blk,
        acc,
        ready,
        CHUNK // TOGETHER,
    )
    store_rays(place_ref, sino, acc, total, o_ref)


def project(place, angle, detector, tile, states, got, sinogram, blocks, ray_total):
    shape = got[0].shape
    count = blocks.shape[0]
    edge = RIM * states.shape[1] * states.shape[3] // 128
    far = pl.BlockSpec(memory_space=pltpu.HBM)
    stay = lambda x: pltpu.with_memory_space_constraint(x, pltpu.HBM)
    return pl.pallas_call(
        project_kernel,
        out_shape=(
            jax.ShapeDtypeStruct((ray_total + edge, 128), BF16),
            jax.ShapeDtypeStruct((2 * edge, 128), BF16),
            jax.ShapeDtypeStruct(shape, F32),
            pltpu.VMEM(blocks.shape, BF16),
        ),
        in_specs=[in_smem()] + [far] * 4 + [in_vmem()] * 3 + [far] * 2,
        out_specs=(in_vmem(),) * 4,
        scratch_shapes=[
            pltpu.SMEM((count,), jnp.int32),
            pltpu.SMEM((count,), jnp.int32),
            pltpu.SMEM((count,), jnp.int32),
            pltpu.VMEM(states.shape[1:], F32),
            pltpu.VMEM(sinogram.shape, F32),
            pltpu.VMEM((shape[0] * shape[1] // 128 + 8, 128), F32),
            pltpu.VMEM((ray_total, 8, 128), F32),
            pltpu.VMEM((ray_total + 8, 128), F32),
            pltpu.SemaphoreType.DMA((5,)),
            pltpu.SemaphoreType.DMA((count // CHUNK,)),
        ],
        compiler_params=params(),
        name="project",
    )(
        place,
        stay(angle),
        stay(detector),
        stay(tile),
        stay(states),
        *got,
        stay(sinogram),
        stay(blocks),
    )


def back_project_kernel(
    place_ref, ray_ref, tile_ref, r_ref, x_ref, sino_ref, blk, x_out, o_ref, res, pix, back, acc
):
    res[0 : r_ref.shape[0]] = r_ref[...].astype(F32)
    back[...] = jnp.zeros_like(back)
    back_blocks(ray_ref, tile_ref, res, blk, back)
    moved = moved_by(x_ref[...], back)
    x_out[...] = moved
    load_pixels(moved, pix)
    acc[...] = jnp.zeros_like(acc)
    project_blocks(lambda b: ray_ref[b], tile_ref, pix, blk, acc)
    store_rays(place_ref, sino_ref, acc, res, o_ref)


def back_project(place, ray_index, tile_index, residual, x, sinogram, blocks):
    ray_total = residual.shape[0]
    tiles = x.size // 128
    return pl.pallas_call(
        back_project_kernel,
        out_shape=(
            jax.ShapeDtypeStruct(x.shape, F32),
            jax.ShapeDtypeStruct(residual.shape, BF16),
        ),
        in_specs=[in_smem()] * 3 + [in_vmem()] * 4,
        out_specs=(in_vmem(), in_vmem()),
        scratch_shapes=[
            pltpu.VMEM((ray_total + 8, 128), F32),
            pltpu.VMEM((tiles + 8, 128), F32),
            pltpu.VMEM((tiles, 8, 128), F32),
            pltpu.VMEM((ray_total, 8, 128), F32),
        ],
        compiler_params=params(),
        name="back_project",
    )(place, ray_index, tile_index, residual, x, sinogram, near(blocks))


def back_kernel(ray_ref, tile_ref, r_ref, x_ref, start_ref, cur_ref, net_ref, blk, o_ref, res, back):
    res[0 : r_ref.shape[0]] = r_ref[...].astype(F32)
    back[...] = jnp.zeros_like(back)
    for z in range(net_ref.shape[0]):
        o_ref[z + 1] = (cur_ref[z] - 2.0 * net_ref[z]).astype(o_ref.dtype)
    back_blocks(ray_ref, tile_ref, res, blk, back)
    o_ref[0] = (2.0 * moved_by(x_ref[...], back) - start_ref[...]).astype(o_ref.dtype)


def back_reflect(ray_index, tile_index, residual, x, start, current, net, blocks):
    ray_total = residual.shape[0]
    tiles = x.size // 128
    return pl.pallas_call(
        back_kernel,
        out_shape=jax.ShapeDtypeStruct((1 + net.shape[0], *x.shape), BF16),
        in_specs=[in_smem()] * 2 + [in_vmem()] * 6,
        out_specs=in_vmem(),
        scratch_shapes=[
            pltpu.VMEM((ray_total + 8, 128), F32),
            pltpu.VMEM((tiles, 8, 128), F32),
        ],
        compiler_params=params(),
        name="back_reflect",
    )(ray_index, tile_index, residual, x, start, current, net, near(blocks))


def finish_kernel(place_ref, all_ref, cur_ref, net_ref, o_ref):
    for z in range(o_ref.shape[0]):
        data = all_ref[z, 0].astype(F32)
        total = data
        for k in range(1, all_ref.shape[0]):
            total = total + all_ref[k, 1 + z].astype(F32)

        @pl.when(place_ref[0] == 0)
        def _():
            o_ref[z] = 0.25 * total + 0.5 * (cur_ref[z] - data)

        @pl.when(place_ref[0] != 0)
        def _():
            o_ref[z] = 0.25 * total + net_ref[z]


def finish(place, everything, current, net):
    return pl.pallas_call(
        finish_kernel,
        out_shape=jax.ShapeDtypeStruct(current.shape, F32),
        in_specs=[in_smem()] + [in_vmem()] * 3,
        out_specs=in_vmem(),
        compiler_params=params(),
        name="finish",
    )(place, everything, current, net)


def lanes(parts, count, height, width):
    empty = jnp.zeros((height, width), F32)
    return jnp.concatenate([parts.get(n, empty) for n in range(count)], axis=1)


def slice_band(first, hidden, last, o, zf, zh, zl, turn):
    turn[...] = jnp.zeros_like(turn)
    for j in range(3):
        for z in range(4):
            near = {y: z - y + 1 for y in range(4) if 0 <= z - y + 1 < 3}
            n = j * 4 + z
            parts = {y: first[o, i, j : j + 1, :].astype(F32) for y, i in near.items()}
            turn[n : n + 1, 0:128] = lanes(parts, 4, 1, 32)
    zf[...] = jnp.transpose(turn[0:128, 0:128])[:, 0:16].astype(BF16)
    for layer in range(hidden.shape[1]):
        for j in range(3):
            for z in range(4):
                near = {y: z - y + 1 for y in range(4) if 0 <= z - y + 1 < 3}
                parts = {y: hidden[o, layer, i, j].astype(F32) for y, i in near.items()}
                turn[z * 32 : z * 32 + 32, 0:128] = lanes(parts, 4, 32, 32)
            zh[layer, :, j * 128 : j * 128 + 128] = jnp.transpose(turn[0:128, 0:128]).astype(BF16)
    rows = []
    for y in range(4):
        parts = {
            j * 4 + z: last[o, z - y + 1, j : j + 1, :].astype(F32)
            for j in range(3)
            for z in range(4)
            if 0 <= z - y + 1 < 3
        }
        rows.append(lanes(parts, 12, 1, 32))
    zl[...] = jnp.concatenate(rows + [jnp.zeros((4, 384), F32)], axis=0).astype(BF16)


def widen(zh, zl, zw, zm):
    for layer in range(zh.shape[0]):
        zw[layer, 0:128, 0:384] = zh[layer]
        zw[layer, 0:128, 384:512] = jnp.zeros((128, 128), BF16)
        zw[layer, 128:256, 0:128] = jnp.zeros((128, 128), BF16)
        zw[layer, 128:256, 128:512] = zh[layer]
    plain = zl[...].astype(F32)
    rows = []
    for z in range(4):
        for a in range(4):
            parts = {a + n: plain[z : z + 1, n * 128 : n * 128 + 128] for n in range(3)}
            rows.append(lanes(parts, 6, 1, 128))
    zm[...] = jnp.concatenate(rows, axis=0).astype(BF16)


def row_band(first, hidden, last, af, ah, al, turn):
    turn[...] = jnp.zeros_like(turn)
    for j in range(3):
        for y in range(SPAN + 2):
            parts = {m: first[0, y - m, j : j + 1, :].astype(F32) for m in range(SPAN) if 0 <= y - m < 3}
            n = j * (SPAN + 2) + y
            turn[n : n + 1] = lanes(parts, 8, 1, 32)
    af[...] = jnp.transpose(turn[0:128])[0 : SPAN * 32, 0:32].astype(BF16)
    for layer in range(hidden.shape[1]):
        for j in range(3):
            for y in range(SPAN + 2):
                parts = {m: hidden[0, layer, y - m, j].astype(F32) for m in range(SPAN) if 0 <= y - m < 3}
                turn[y * 32 : y * 32 + 32] = lanes(parts, 8, 32, 32)
            ah[layer, j] = jnp.transpose(turn[...])[0 : SPAN * 32].astype(BF16)
    for j in range(3):
        rows = []
        for m in range(SPAN):
            parts = {m + i: last[0, i, j : j + 1, :].astype(F32) for i in range(3)}
            rows.append(lanes(parts, 8, 1, 32))
        rows.append(jnp.zeros((2, 256), F32))
        al[j] = jnp.concatenate(rows, axis=0).astype(BF16)


def prepare_kernel(
    place_ref, before, after, cur, first, hidden, last, rim, zf, zh, zl, zw, zm, af, ah, al, turn
):
    rows = cur.shape[1]
    wide = cur.shape[2] // 128
    rim[:, RIM : RIM + rows] = cur[...].astype(BF16).astype(F32)
    above = jnp.where(place_ref[1] > 0, before[...].astype(F32), 0.0)
    below = jnp.where(place_ref[1] < place_ref[2] - 1, after[...].astype(F32), 0.0)
    for z in range(cur.shape[0]):
        for c in range(wide):
            n = (z * wide + c) * RIM
            rim[z, 0:RIM, c * 128 : c * 128 + 128] = above[n : n + RIM]
            rim[z, RIM + rows :, c * 128 : c * 128 + 128] = below[n : n + RIM]

    @pl.when(place_ref[0] == 1)
    def _():
        row_band(first, hidden, last, af, ah, al, turn)

    @pl.when(place_ref[0] == 2)
    def _():
        slice_band(first, hidden, last, 1, zf, zh, zl, turn)
        widen(zh, zl, zw, zm)

    @pl.when(place_ref[0] == 3)
    def _():
        slice_band(first, hidden, last, 2, zf, zh, zl, turn)


def prepare(place, rim, current, first, hidden, last):
    layers = hidden.shape[1]
    slices, rows, columns = current.shape
    whole = jax.ShapeDtypeStruct((slices, rows + 2 * RIM, columns), F32)
    shapes = [
        (128, 16),
        (layers, 128, 384),
        (8, 384),
        (layers, 256, 512),
        (16, 768),
        (SPAN * 32, 32),
        (layers, 3, SPAN * 32, 256),
        (3, 8, 256),
    ]
    return pl.pallas_call(
        prepare_kernel,
        out_shape=[whole] + [jax.ShapeDtypeStruct(s, BF16) for s in shapes],
        in_specs=[in_smem()] + [in_vmem()] * 6,
        out_specs=[in_vmem()] * 9,
        scratch_shapes=[pltpu.VMEM((256, 256), F32)],
        compiler_params=params(),
        name="prepare",
    )(place, *rim, current, first, hidden, last)


def side_by_side(value):
    columns = value.shape[1]
    place = lax.broadcasted_iota(jnp.int32, value.shape, 1)
    before = jnp.where(place == 0, 0.0, pltpu.roll(value, 1, axis=1))
    after = jnp.where(place == columns - 1, 0.0, pltpu.roll(value, columns - 1, axis=1))
    return before, value, after


def relu_rows(value, keep):
    value = jnp.maximum(value, 0.0)
    return value if keep is None else jnp.where(keep, value, 0.0)


def sagittal_piece(part, columns, rows, above, below, rim, wf, wh, wl, o_ref, ha, hb):
    width = wf.shape[0]
    depth = wh.shape[0] + 1
    across = slice(part * columns, (part + 1) * columns)

    def kept(layer, y):
        reach = depth - layer
        return above if y < reach else below if y >= reach + rows else None

    empty = jnp.zeros((4, columns), F32)
    for y in range(rows + 2 * depth):
        taps = [rim[:, y + j, across] for j in range(3)] + [empty]
        taps = jnp.concatenate(taps, axis=0).astype(BF16)
        value = jnp.dot(wf[...], taps, preferred_element_type=F32)
        ha[y * width : (y + 1) * width] = relu_rows(value, kept(0, y)).astype(BF16)
    source, target = ha, hb
    for layer in range(wh.shape[0]):
        for y in range(0, rows + 2 * (depth - 1 - layer), 2):
            value = jnp.dot(
                wh[layer], source[y * width : (y + 4) * width], preferred_element_type=F32
            )
            for k in range(2):
                part_k = value[k * width : (k + 1) * width]
                target[(y + k) * width : (y + k + 1) * width] = relu_rows(
                    part_k, kept(layer + 1, y + k)
                ).astype(BF16)
        source, target = target, source
    for y in range(0, rows, 4):
        net = jnp.dot(wl[...], source[y * width : (y + 6) * width], preferred_element_type=F32)
        for z in range(4):
            o_ref[z, y : y + 4, across] = net[z * 4 : z * 4 + 4]


def coronal_piece(start, count, depth, rim, wf, wh, wl, o_ref, h):
    columns = rim.shape[2]
    width = wf.shape[0]
    empty = jnp.zeros((4, columns), F32)
    values = []
    for r in range(count):
        taps = jnp.concatenate([*side_by_side(rim[:, depth + start + r, :]), empty], axis=0)
        values.append(jnp.dot(wf[...], taps.astype(BF16), preferred_element_type=F32))
    for layer in range(wh.shape[0] + 1):
        matrix = wh[layer] if layer < wh.shape[0] else wl[...]
        for r in range(count):
            for j, moved in enumerate(side_by_side(jnp.maximum(values[r], 0.0))):
                h[r, j * width : (j + 1) * width] = moved.astype(BF16)
            values[r] = jnp.dot(matrix, h[r], preferred_element_type=F32)
    for r in range(count):
        o_ref[:, start + r, :] = values[r][0:4]


def spans(rows):
    starts = list(range(0, rows - SPAN, SPAN))
    return starts + [rows - SPAN]


def axial_piece(z, rows, above, below, rim, wf, wh, wl, o_ref, ha, hb):
    channels = wh.shape[3] // (SPAN + 2)
    depth = wh.shape[0] + 1

    def put(target, layer, start, value):
        value = jnp.maximum(value, 0.0)
        reach = depth - layer
        parts = []
        for k in range(SPAN):
            part = value[k * channels : (k + 1) * channels]
            y = start + k
            if y < reach:
                part = jnp.where(above, part, 0.0)
            elif y >= reach + rows:
                part = jnp.where(below, part, 0.0)
            parts.append(part)
        value = jnp.concatenate(parts, axis=0)
        for j, moved in enumerate(side_by_side(value)):
            target[j, start * channels : (start + SPAN) * channels] = moved.astype(BF16)

    def over_columns(matrices, source, start):
        total = None
        for j in range(3):
            window = source[j, start * channels : (start + SPAN + 2) * channels]
            part = jnp.dot(matrices[j], window, preferred_element_type=F32)
            total = part if total is None else total + part
        return total

    around = side_by_side(rim[z])
    empty = jnp.zeros((SPAN + 2, rim.shape[2]), F32)
    for start in spans(rows + 2 * depth):
        taps = [moved[start : start + SPAN + 2] for moved in around] + [empty]
        taps = jnp.concatenate(taps, axis=0).astype(BF16)
        put(ha, 0, start, jnp.dot(wf[...], taps, preferred_element_type=F32))
    source, target = ha, hb
    for layer in range(wh.shape[0]):
        for start in spans(rows + 2 * (depth - 1 - layer)):
            put(target, layer + 1, start, over_columns(wh[layer], source, start))
        source, target = target, source
    for start in spans(rows):
        o_ref[z, start : start + SPAN] = over_columns(wl[...], source, start)[0:SPAN]


def piece_kernel(
    k, place_ref, blk, net, rim, zf, zh, zl, zw, zm, af, ah, al, o_ref, sa, sb, ca, xa, xb
):
    rows = o_ref.shape[1]
    depth = (rim.shape[1] - rows) // 2
    above, below = place_ref[1] > 0, place_ref[1] < place_ref[2] - 1
    o_ref[...] = net[...]

    @pl.when(place_ref[0] == 1)
    def _():
        axial_piece(k, rows, above, below, rim, af, ah, al, o_ref, xa, xb)

    if k < 2:

        @pl.when(place_ref[0] == 2)
        def _():
            half = o_ref.shape[2] // 2
            sagittal_piece(k, half, rows, above, below, rim, zf, zw, zm, o_ref, sa, sb)

    @pl.when(place_ref[0] == 3)
    def _():
        coronal_piece(k * (rows // 4), rows // 4, depth, rim, zf, zh, zl, o_ref, ca)


def piece(k, place, blocks, net, prepared):
    slices, rows, columns = net.shape
    reach = rows + 6
    return pl.pallas_call(
        functools.partial(piece_kernel, k),
        out_shape=jax.ShapeDtypeStruct(net.shape, F32),
        in_specs=[in_smem()] + [in_vmem()] * (2 + len(prepared)),
        out_specs=in_vmem(),
        scratch_shapes=[pltpu.VMEM((reach * 128, columns // 2), BF16)] * 2
        + [pltpu.VMEM((rows // 4, 384, columns), BF16)]
        + [pltpu.VMEM((3, reach * 32, columns), BF16)] * 2,
        compiler_params=params(),
        name=f"piece_{k}",
    )(place, near(blocks), net, *prepared)


def swapped(groups, k):
    return [(g[n], g[(n + k) % len(g)]) for g in groups for n in range(len(g))]


def stage_groups(count):
    near = 4
    strided = 4
    far = count // (near * strided)
    at = lambda f, s, n: (f * strided + s) * near + n
    return [
        [[at(f, s, n) for f in range(far)] for s in range(strided) for n in range(near)],
        [[at(f, s, n) for s in range(strided)] for f in range(far) for n in range(near)],
        [[at(f, s, n) for n in range(near)] for f in range(far) for s in range(strided)],
    ]


def added_up(values, groups):
    total = values.astype(F32)
    for k in [k for k in (1, 3, 2) if k < len(groups[0])]:
        total = total + lax.ppermute(values, "tile", swapped(groups, k)).astype(F32)
    return total.astype(values.dtype)


def added_up_with_rims(first, own, groups, ends):
    far, strided, near = groups
    edge = own.shape[0] // 2
    rows = first.shape[0] - edge
    got = lax.ppermute(first, "tile", swapped(far, 1))
    tail, head = own[0:edge], own[edge:]
    onward = backward = got[rows:]
    sums = (first[0:rows].astype(F32) + got[0:rows].astype(F32)).astype(BF16)
    for n, group in enumerate((strided, near)):
        at_first, at_last = ends[n]
        onward = jnp.where(at_last, onward, tail)
        backward = jnp.where(at_first, backward, head)
        sums, onward, backward = lax.optimization_barrier((sums, onward, backward))
        up = lax.ppermute(jnp.concatenate([sums, onward]), "tile", swapped(group, 1))
        across = lax.ppermute(sums, "tile", swapped(group, 2))
        down = lax.ppermute(jnp.concatenate([sums, backward]), "tile", swapped(group, 3))
        onward, backward = up[rows:], down[rows:]
        total = sums.astype(F32) + up[0:rows].astype(F32)
        total = total + across.astype(F32) + down[0:rows].astype(F32)
        sums = total.astype(BF16)
    return sums, (onward, backward)


def slices_sent(current):
    return [lax.ppermute(current[k], "agent", [(0, k)]) for k in range(1, current.shape[0])]


def per_device(
    states,
    sinogram,
    blocks,
    block_angle,
    block_detector,
    block_tile,
    conv_first,
    conv_hidden,
    conv_last,
):
    current = states[0]
    tile_count = lax.axis_size("tile")
    tile_place = lax.axis_index("tile")
    agent_place = lax.axis_index("agent")
    place = jnp.stack([agent_place, tile_place, jnp.int32(tile_count)]).astype(jnp.int32)
    ray_total = sinogram.shape[0] * tile_count
    ray_index = block_angle * (current.shape[2] // 128) + block_detector

    within = [lax.shift_right_logical(tile_place, 2) & 3, tile_place & 3]
    ends = [(at == 0, at == 3) for at in within]
    got, ends = lax.optimization_barrier((slices_sent(current), ends))
    first, own, start, blocks_here = project(
        place, block_angle, block_detector, block_tile, states, got, sinogram, blocks, ray_total
    )

    groups = stage_groups(tile_count)
    net = jnp.zeros_like(current)
    x_data = start
    sums, rim = added_up_with_rims(first, own, groups, ends)
    for _ in range(DATA_STEPS - 2):
        x_data, sums = back_project(
            place, ray_index, block_tile, sums, x_data, sinogram, blocks_here
        )
        for group in groups:
            sums = added_up(sums, group)
    x_data, sums = back_project(place, ray_index, block_tile, sums, x_data, sinogram, blocks_here)
    for n, group in enumerate(groups):
        sums, net = lax.optimization_barrier((sums, net))
        if n == 0:
            prepared = prepare(place, rim, current, conv_first, conv_hidden, conv_last)
        for k in PIECES[n]:
            net = piece(k, place, blocks_here, net, prepared)
        sums = added_up(sums, group)
    sent = back_reflect(ray_index, block_tile, sums, x_data, start, current, net, blocks_here)
    everything = lax.all_gather(sent, "agent")
    return finish(place, everything, current, net)[None]


def solution(mesh):
    placed = (
        P("agent", None, "tile", None),
        P("tile", None, None),
        P("tile", None, None),
        P("tile"),
        P("tile"),
        P("tile"),
        P(),
        P(),
        P(),
    )
    return jax.shard_map(
        per_device,
        mesh=mesh,
        in_specs=placed,
        out_specs=P("agent", None, "tile", None),
        check_vma=False,
    )
```

```python
import functools

import jax
import jax.numpy as jnp
import numpy as np
from jax import lax
from jax.experimental import pallas as pl
from jax.experimental.pallas import tpu as pltpu
from jax.sharding import PartitionSpec as P

DATA_STEPS = 2
F32, BF16 = jnp.float32, jnp.bfloat16
VMEM_LIMIT = 32 << 20
TOGETHER = 4
UNROLL = 64
RIM = 4
CHUNK = 64
PIECES = ((0,), (1,), (2, 3))
SPAN = 6


def params():
    return pltpu.CompilerParams(vmem_limit_bytes=VMEM_LIMIT)


def in_vmem():
    return pl.BlockSpec(memory_space=pltpu.VMEM)


def near(x):
    return pltpu.with_memory_space_constraint(x, pltpu.VMEM)


def in_smem():
    return pl.BlockSpec(memory_space=pltpu.SMEM)


def low_rows():
    return lax.broadcasted_iota(jnp.int32, (8, 128), 0) < 4


def four_blocks(blk, b):
    size = blk.shape[1]
    left = blk[pl.ds(b, 2)].reshape(2 * size, size)
    right = blk[pl.ds(b + 2, 2)].reshape(2 * size, size)
    return jnp.concatenate([left, right], axis=1)


def row(ref, index):
    return ref[pl.ds(index, 8, stride=0), :]


def add_rows(acc, index, value):
    acc[index] = acc[index] + value


def project_blocks(ray_of, tile_ref, pix, blk, acc, ready=None, unroll=UNROLL):
    low = low_rows()
    zero = jnp.zeros((8, 128), F32)

    def body(i, carry):
        if ready is not None:
            ready(i)
        outs = []
        for u in range(unroll):
            b = (i * unroll + u) * TOGETHER
            t = [row(pix, tile_ref[b + k]) for k in range(TOGETHER)]
            upper = jnp.concatenate([jnp.where(low, t[0], t[1]), zero], axis=0)
            lower = jnp.concatenate([zero, jnp.where(low, t[2], t[3])], axis=0)
            lhs = jnp.concatenate([upper.astype(BF16), lower.astype(BF16)], axis=1)
            outs.append(
                lax.dot_general(
                    lhs, four_blocks(blk, b), (((1,), (1,)), ((), ())), preferred_element_type=F32
                )
            )
        for u in range(unroll):
            b = (i * unroll + u) * TOGETHER
            out = outs[u]
            add_rows(acc, ray_of(b), jnp.where(low, out[0:8, 0:128], 0.0))
            add_rows(acc, ray_of(b + 1), jnp.where(low, 0.0, out[0:8, 128:256]))
            add_rows(acc, ray_of(b + 2), jnp.where(low, out[8:16, 0:128], 0.0))
            add_rows(acc, ray_of(b + 3), jnp.where(low, 0.0, out[8:16, 128:256]))
        return carry

    lax.fori_loop(0, blk.shape[0] // (TOGETHER * unroll), body, 0)


def back_blocks(ray_ref, tile_ref, res, blk, acc):
    low = low_rows()

    def body(i, carry):
        outs = []
        for u in range(UNROLL):
            b = (i * UNROLL + u) * TOGETHER
            t = [row(res, ray_ref[b + k]) for k in range(TOGETHER)]
            left = jnp.concatenate([jnp.where(low, t[0], 0.0), jnp.where(low, t[2], 0.0)], axis=0)
            right = jnp.concatenate([jnp.where(low, 0.0, t[1]), jnp.where(low, 0.0, t[3])], axis=0)
            lhs = jnp.concatenate([left.astype(BF16), right.astype(BF16)], axis=1)
            outs.append(jnp.dot(lhs, four_blocks(blk, b), preferred_element_type=F32))
        for u in range(UNROLL):
            b = (i * UNROLL + u) * TOGETHER
            upper, lower = outs[u][0:8, 0:128], outs[u][8:16, 128:256]
            add_rows(acc, tile_ref[b], jnp.where(low, upper, 0.0))
            add_rows(acc, tile_ref[b + 1], jnp.where(low, 0.0, upper))
            add_rows(acc, tile_ref[b + 2], jnp.where(low, lower, 0.0))
            add_rows(acc, tile_ref[b + 3], jnp.where(low, 0.0, lower))
        return carry

    lax.fori_loop(0, blk.shape[0] // (TOGETHER * UNROLL), body, 0)


def tiles_of(x_shape):
    wide = x_shape[1] // 128
    return [(r, c, slice(c * 128, c * 128 + 128)) for r in range(x_shape[0]) for c in range(wide)]


def load_pixels(value, pix):
    wide = value.shape[1] // 128
    for r, c, columns in tiles_of(value.shape):
        pix[r * wide + c : r * wide + c + 1] = value[r : r + 1, columns]


def moved_by(x, back):
    wide = x.shape[1] // 128
    rows = back.shape[0]
    columns = []
    for c in range(wide):
        own = pl.ds(c, rows // wide, stride=wide)
        columns.append(back[own, 0, :] + back[own, 4, :])
    return x - 0.8 * jnp.concatenate(columns, axis=1)


def store_rays(place_ref, sino_ref, acc, total, o_ref):
    total[0 : acc.shape[0]] = acc[:, 0, :] + acc[:, 4, :]
    own = sino_ref.shape[0]
    mine = pl.ds(pl.multiple_of(place_ref[1] * own, own), own)
    for z in range(sino_ref.shape[1]):

        @pl.when(place_ref[0] == z)
        def _():
            total[mine] = total[mine] - sino_ref[:, z, :]

    o_ref[0 : acc.shape[0]] = total[0 : acc.shape[0]].astype(o_ref.dtype)


def in_pieces(cur, first):
    pieces = []
    for z in range(cur.shape[0]):
        for c in range(cur.shape[2] // 128):
            pieces.append(cur[z, first : first + RIM, c * 128 : c * 128 + 128])
    return jnp.concatenate(pieces, axis=0)


def project_kernel(
    place_ref,
    angle_in,
    detector_in,
    tile_in,
    states_in,
    got_1,
    got_2,
    got_3,
    sino_in,
    blk_in,
    o_ref,
    edge_ref,
    start_ref,
    blk,
    angle,
    detector,
    tile,
    cur,
    sino,
    pix,
    acc,
    total,
    small_sems,
    block_sems,
):
    small = [
        pltpu.make_async_copy(source, target, small_sems.at[n])
        for n, (source, target) in enumerate(
            [
                (states_in.at[0], cur),
                (angle_in, angle),
                (detector_in, detector),
                (tile_in, tile),
                (sino_in, sino),
            ]
        )
    ]
    for copy in small:
        copy.start()
    chunk = CHUNK

    def chunk_copy(i):
        part = pl.ds(i * chunk, chunk)
        return pltpu.make_async_copy(blk_in.at[part], blk.at[part], block_sems.at[i])

    ahead = 2
    count = blk.shape[0] // chunk
    for i in range(ahead):
        chunk_copy(i).start()

    def ready(i):
        chunk_copy(i).wait()

        @pl.when(i + ahead < count)
        def _():
            chunk_copy(i + ahead).start()

    acc[...] = jnp.zeros_like(acc)
    for copy in small:
        copy.wait()
    @pl.when(place_ref[0] == 0)
    def _():
        start_ref[...] = cur[0]

    for k, value in enumerate((got_1, got_2, got_3)):

        @pl.when(place_ref[0] == k + 1)
        def _():
            start_ref[...] = value[...]

    tail = in_pieces(cur, cur.shape[1] - RIM).astype(BF16)
    head = in_pieces(cur, 0).astype(BF16)
    edge = tail.shape[0]
    edge_ref[0:edge] = tail
    edge_ref[edge:] = head
    rows = acc.shape[0]
    at_end = (place_ref[1] // 4) % 4 == 3

    @pl.when(at_end)
    def _():
        o_ref[rows:] = tail

    @pl.when(jnp.logical_not(at_end))
    def _():
        o_ref[rows:] = head

    load_pixels(start_ref[...], pix)
    wide = cur.shape[2] // 128
    project_blocks(
        lambda b: angle[b] * wide + detector[b],
        tile,
        pix,
        blk,
        acc,
        ready,
        CHUNK // TOGETHER,
    )
    store_rays(place_ref, sino, acc, total, o_ref)


def project(place, angle, detector, tile, states, got, sinogram, blocks, ray_total):
    shape = got[0].shape
    count = blocks.shape[0]
    edge = RIM * states.shape[1] * states.shape[3] // 128
    far = pl.BlockSpec(memory_space=pltpu.HBM)
    stay = lambda x: pltpu.with_memory_space_constraint(x, pltpu.HBM)
    return pl.pallas_call(
        project_kernel,
        out_shape=(
            jax.ShapeDtypeStruct((ray_total + edge, 128), BF16),
            jax.ShapeDtypeStruct((2 * edge, 128), BF16),
            jax.ShapeDtypeStruct(shape, F32),
            pltpu.VMEM(blocks.shape, BF16),
        ),
        in_specs=[in_smem()] + [far] * 4 + [in_vmem()] * 3 + [far] * 2,
        out_specs=(in_vmem(),) * 4,
        scratch_shapes=[
            pltpu.SMEM((count,), jnp.int32),
            pltpu.SMEM((count,), jnp.int32),
            pltpu.SMEM((count,), jnp.int32),
            pltpu.VMEM(states.shape[1:], F32),
            pltpu.VMEM(sinogram.shape, F32),
            pltpu.VMEM((shape[0] * shape[1] // 128 + 8, 128), F32),
            pltpu.VMEM((ray_total, 8, 128), F32),
            pltpu.VMEM((ray_total + 8, 128), F32),
            pltpu.SemaphoreType.DMA((5,)),
            pltpu.SemaphoreType.DMA((count // CHUNK,)),
        ],
        compiler_params=params(),
        name="project",
    )(
        place,
        stay(angle),
        stay(detector),
        stay(tile),
        stay(states),
        *got,
        stay(sinogram),
        stay(blocks),
    )


def back_project_kernel(
    place_ref, ray_ref, tile_ref, r_ref, x_ref, sino_ref, blk, x_out, o_ref, res, pix, back, acc
):
    res[0 : r_ref.shape[0]] = r_ref[...].astype(F32)
    back[...] = jnp.zeros_like(back)
    back_blocks(ray_ref, tile_ref, res, blk, back)
    moved = moved_by(x_ref[...], back)
    x_out[...] = moved
    load_pixels(moved, pix)
    acc[...] = jnp.zeros_like(acc)
    project_blocks(lambda b: ray_ref[b], tile_ref, pix, blk, acc)
    store_rays(place_ref, sino_ref, acc, res, o_ref)


def back_project(place, ray_index, tile_index, residual, x, sinogram, blocks):
    ray_total = residual.shape[0]
    tiles = x.size // 128
    return pl.pallas_call(
        back_project_kernel,
        out_shape=(
            jax.ShapeDtypeStruct(x.shape, F32),
            jax.ShapeDtypeStruct(residual.shape, BF16),
        ),
        in_specs=[in_smem()] * 3 + [in_vmem()] * 4,
        out_specs=(in_vmem(), in_vmem()),
        scratch_shapes=[
            pltpu.VMEM((ray_total + 8, 128), F32),
            pltpu.VMEM((tiles + 8, 128), F32),
            pltpu.VMEM((tiles, 8, 128), F32),
            pltpu.VMEM((ray_total, 8, 128), F32),
        ],
        compiler_params=params(),
        name="back_project",
    )(place, ray_index, tile_index, residual, x, sinogram, near(blocks))


def back_kernel(ray_ref, tile_ref, r_ref, x_ref, start_ref, cur_ref, net_ref, blk, o_ref, res, back):
    res[0 : r_ref.shape[0]] = r_ref[...].astype(F32)
    back[...] = jnp.zeros_like(back)
    for z in range(net_ref.shape[0]):
        o_ref[z + 1] = (cur_ref[z] - 2.0 * net_ref[z]).astype(o_ref.dtype)
    back_blocks(ray_ref, tile_ref, res, blk, back)
    o_ref[0] = (2.0 * moved_by(x_ref[...], back) - start_ref[...]).astype(o_ref.dtype)


def back_reflect(ray_index, tile_index, residual, x, start, current, net, blocks):
    ray_total = residual.shape[0]
    tiles = x.size // 128
    return pl.pallas_call(
        back_kernel,
        out_shape=jax.ShapeDtypeStruct((1 + net.shape[0], *x.shape), BF16),
        in_specs=[in_smem()] * 2 + [in_vmem()] * 6,
        out_specs=in_vmem(),
        scratch_shapes=[
            pltpu.VMEM((ray_total + 8, 128), F32),
            pltpu.VMEM((tiles, 8, 128), F32),
        ],
        compiler_params=params(),
        name="back_reflect",
    )(ray_index, tile_index, residual, x, start, current, net, near(blocks))


def finish_kernel(place_ref, all_ref, cur_ref, net_ref, o_ref):
    for z in range(o_ref.shape[0]):
        data = all_ref[z, 0].astype(F32)
        total = data
        for k in range(1, all_ref.shape[0]):
            total = total + all_ref[k, 1 + z].astype(F32)

        @pl.when(place_ref[0] == 0)
        def _():
            o_ref[z] = 0.25 * total + 0.5 * (cur_ref[z] - data)

        @pl.when(place_ref[0] != 0)
        def _():
            o_ref[z] = 0.25 * total + net_ref[z]


def finish(place, everything, current, net):
    return pl.pallas_call(
        finish_kernel,
        out_shape=jax.ShapeDtypeStruct(current.shape, F32),
        in_specs=[in_smem()] + [in_vmem()] * 3,
        out_specs=in_vmem(),
        compiler_params=params(),
        name="finish",
    )(place, everything, current, net)


def lanes(parts, count, height, width):
    empty = jnp.zeros((height, width), F32)
    return jnp.concatenate([parts.get(n, empty) for n in range(count)], axis=1)


def slice_band(first, hidden, last, o, zf, zh, zl, turn):
    turn[...] = jnp.zeros_like(turn)
    for j in range(3):
        for z in range(4):
            near = {y: z - y + 1 for y in range(4) if 0 <= z - y + 1 < 3}
            n = j * 4 + z
            parts = {y: first[o, i, j : j + 1, :].astype(F32) for y, i in near.items()}
            turn[n : n + 1, 0:128] = lanes(parts, 4, 1, 32)
    zf[...] = jnp.transpose(turn[0:128, 0:128])[:, 0:16].astype(BF16)
    for layer in range(hidden.shape[1]):
        for j in range(3):
            for z in range(4):
                near = {y: z - y + 1 for y in range(4) if 0 <= z - y + 1 < 3}
                parts = {y: hidden[o, layer, i, j].astype(F32) for y, i in near.items()}
                turn[z * 32 : z * 32 + 32, 0:128] = lanes(parts, 4, 32, 32)
            zh[layer, :, j * 128 : j * 128 + 128] = jnp.transpose(turn[0:128, 0:128]).astype(BF16)
    rows = []
    for y in range(4):
        parts = {
            j * 4 + z: last[o, z - y + 1, j : j + 1, :].astype(F32)
            for j in range(3)
            for z in range(4)
            if 0 <= z - y + 1 < 3
        }
        rows.append(lanes(parts, 12, 1, 32))
    zl[...] = jnp.concatenate(rows + [jnp.zeros((4, 384), F32)], axis=0).astype(BF16)


def widen(zh, zl, zw, zm):
    for layer in range(zh.shape[0]):
        zw[layer, 0:128, 0:384] = zh[layer]
        zw[layer, 0:128, 384:512] = jnp.zeros((128, 128), BF16)
        zw[layer, 128:256, 0:128] = jnp.zeros((128, 128), BF16)
        zw[layer, 128:256, 128:512] = zh[layer]
    plain = zl[...].astype(F32)
    rows = []
    for z in range(4):
        for a in range(4):
            parts = {a + n: plain[z : z + 1, n * 128 : n * 128 + 128] for n in range(3)}
            rows.append(lanes(parts, 6, 1, 128))
    zm[...] = jnp.concatenate(rows, axis=0).astype(BF16)


def row_band(first, hidden, last, af, ah, al, turn):
    turn[...] = jnp.zeros_like(turn)
    for j in range(3):
        for y in range(SPAN + 2):
            parts = {m: first[0, y - m, j : j + 1, :].astype(F32) for m in range(SPAN) if 0 <= y - m < 3}
            n = j * (SPAN + 2) + y
            turn[n : n + 1] = lanes(parts, 8, 1, 32)
    af[...] = jnp.transpose(turn[0:128])[0 : SPAN * 32, 0:32].astype(BF16)
    for layer in range(hidden.shape[1]):
        for j in range(3):
            for y in range(SPAN + 2):
                parts = {m: hidden[0, layer, y - m, j].astype(F32) for m in range(SPAN) if 0 <= y - m < 3}
                turn[y * 32 : y * 32 + 32] = lanes(parts, 8, 32, 32)
            ah[layer, j] = jnp.transpose(turn[...])[0 : SPAN * 32].astype(BF16)
    for j in range(3):
        rows = []
        for m in range(SPAN):
            parts = {m + i: last[0, i, j : j + 1, :].astype(F32) for i in range(3)}
            rows.append(lanes(parts, 8, 1, 32))
        rows.append(jnp.zeros((2, 256), F32))
        al[j] = jnp.concatenate(rows, axis=0).astype(BF16)


def prepare_kernel(
    place_ref, before, after, cur, first, hidden, last, rim, zf, zh, zl, zw, zm, af, ah, al, turn
):
    rows = cur.shape[1]
    wide = cur.shape[2] // 128
    rim[:, RIM : RIM + rows] = cur[...].astype(BF16).astype(F32)
    above = jnp.where(place_ref[1] > 0, before[...].astype(F32), 0.0)
    below = jnp.where(place_ref[1] < place_ref[2] - 1, after[...].astype(F32), 0.0)
    for z in range(cur.shape[0]):
        for c in range(wide):
            n = (z * wide + c) * RIM
            rim[z, 0:RIM, c * 128 : c * 128 + 128] = above[n : n + RIM]
            rim[z, RIM + rows :, c * 128 : c * 128 + 128] = below[n : n + RIM]

    @pl.when(place_ref[0] == 1)
    def _():
        row_band(first, hidden, last, af, ah, al, turn)

    @pl.when(place_ref[0] == 2)
    def _():
        slice_band(first, hidden, last, 1, zf, zh, zl, turn)
        widen(zh, zl, zw, zm)

    @pl.when(place_ref[0] == 3)
    def _():
        slice_band(first, hidden, last, 2, zf, zh, zl, turn)


def prepare(place, rim, current, first, hidden, last):
    layers = hidden.shape[1]
    slices, rows, columns = current.shape
    whole = jax.ShapeDtypeStruct((slices, rows + 2 * RIM, columns), F32)
    shapes = [
        (128, 16),
        (layers, 128, 384),
        (8, 384),
        (layers, 256, 512),
        (16, 768),
        (SPAN * 32, 32),
        (layers, 3, SPAN * 32, 256),
        (3, 8, 256),
    ]
    return pl.pallas_call(
        prepare_kernel,
        out_shape=[whole] + [jax.ShapeDtypeStruct(s, BF16) for s in shapes],
        in_specs=[in_smem()] + [in_vmem()] * 6,
        out_specs=[in_vmem()] * 9,
        scratch_shapes=[pltpu.VMEM((256, 256), F32)],
        compiler_params=params(),
        name="prepare",
    )(place, *rim, current, first, hidden, last)


def side_by_side(value):
    columns = value.shape[1]
    place = lax.broadcasted_iota(jnp.int32, value.shape, 1)
    before = jnp.where(place == 0, 0.0, pltpu.roll(value, 1, axis=1))
    after = jnp.where(place == columns - 1, 0.0, pltpu.roll(value, columns - 1, axis=1))
    return before, value, after


def relu_rows(value, keep):
    value = jnp.maximum(value, 0.0)
    return value if keep is None else jnp.where(keep, value, 0.0)


def sagittal_piece(part, columns, rows, above, below, rim, wf, wh, wl, o_ref, ha, hb):
    width = wf.shape[0]
    depth = wh.shape[0] + 1
    across = slice(part * columns, (part + 1) * columns)

    def kept(layer, y):
        reach = depth - layer
        return above if y < reach else below if y >= reach + rows else None

    empty = jnp.zeros((4, columns), F32)
    for y in range(rows + 2 * depth):
        taps = [rim[:, y + j, across] for j in range(3)] + [empty]
        taps = jnp.concatenate(taps, axis=0).astype(BF16)
        value = jnp.dot(wf[...], taps, preferred_element_type=F32)
        ha[y * width : (y + 1) * width] = relu_rows(value, kept(0, y)).astype(BF16)
    source, target = ha, hb
    for layer in range(wh.shape[0]):
        for y in range(0, rows + 2 * (depth - 1 - layer), 2):
            value = jnp.dot(
                wh[layer], source[y * width : (y + 4) * width], preferred_element_type=F32
            )
            for k in range(2):
                part_k = value[k * width : (k + 1) * width]
                target[(y + k) * width : (y + k + 1) * width] = relu_rows(
                    part_k, kept(layer + 1, y + k)
                ).astype(BF16)
        source, target = target, source
    for y in range(0, rows, 4):
        net = jnp.dot(wl[...], source[y * width : (y + 6) * width], preferred_element_type=F32)
        for z in range(4):
            o_ref[z, y : y + 4, across] = net[z * 4 : z * 4 + 4]


def coronal_piece(start, count, depth, rim, wf, wh, wl, o_ref, h):
    columns = rim.shape[2]
    width = wf.shape[0]
    empty = jnp.zeros((4, columns), F32)
    values = []
    for r in range(count):
        taps = jnp.concatenate([*side_by_side(rim[:, depth + start + r, :]), empty], axis=0)
        values.append(jnp.dot(wf[...], taps.astype(BF16), preferred_element_type=F32))
    for layer in range(wh.shape[0] + 1):
        matrix = wh[layer] if layer < wh.shape[0] else wl[...]
        for r in range(count):
            for j, moved in enumerate(side_by_side(jnp.maximum(values[r], 0.0))):
                h[r, j * width : (j + 1) * width] = moved.astype(BF16)
            values[r] = jnp.dot(matrix, h[r], preferred_element_type=F32)
    for r in range(count):
        o_ref[:, start + r, :] = values[r][0:4]


def spans(rows):
    starts = list(range(0, rows - SPAN, SPAN))
    return starts + [rows - SPAN]


def axial_piece(z, rows, above, below, rim, wf, wh, wl, o_ref, ha, hb):
    channels = wh.shape[3] // (SPAN + 2)
    depth = wh.shape[0] + 1

    def put(target, layer, start, value):
        value = jnp.maximum(value, 0.0)
        reach = depth - layer
        parts = []
        for k in range(SPAN):
            part = value[k * channels : (k + 1) * channels]
            y = start + k
            if y < reach:
                part = jnp.where(above, part, 0.0)
            elif y >= reach + rows:
                part = jnp.where(below, part, 0.0)
            parts.append(part)
        value = jnp.concatenate(parts, axis=0)
        for j, moved in enumerate(side_by_side(value)):
            target[j, start * channels : (start + SPAN) * channels] = moved.astype(BF16)

    def over_columns(matrices, source, start):
        total = None
        for j in range(3):
            window = source[j, start * channels : (start + SPAN + 2) * channels]
            part = jnp.dot(matrices[j], window, preferred_element_type=F32)
            total = part if total is None else total + part
        return total

    around = side_by_side(rim[z])
    empty = jnp.zeros((SPAN + 2, rim.shape[2]), F32)
    for start in spans(rows + 2 * depth):
        taps = [moved[start : start + SPAN + 2] for moved in around] + [empty]
        taps = jnp.concatenate(taps, axis=0).astype(BF16)
        put(ha, 0, start, jnp.dot(wf[...], taps, preferred_element_type=F32))
    source, target = ha, hb
    for layer in range(wh.shape[0]):
        for start in spans(rows + 2 * (depth - 1 - layer)):
            put(target, layer + 1, start, over_columns(wh[layer], source, start))
        source, target = target, source
    for start in spans(rows):
        o_ref[z, start : start + SPAN] = over_columns(wl[...], source, start)[0:SPAN]


def piece_kernel(
    k, place_ref, blk, net, rim, zf, zh, zl, zw, zm, af, ah, al, o_ref, sa, sb, ca, xa, xb
):
    rows = o_ref.shape[1]
    depth = (rim.shape[1] - rows) // 2
    above, below = place_ref[1] > 0, place_ref[1] < place_ref[2] - 1
    o_ref[...] = net[...]

    @pl.when(place_ref[0] == 1)
    def _():
        axial_piece(k, rows, above, below, rim, af, ah, al, o_ref, xa, xb)

    if k < 2:

        @pl.when(place_ref[0] == 2)
        def _():
            half = o_ref.shape[2] // 2
            sagittal_piece(k, half, rows, above, below, rim, zf, zw, zm, o_ref, sa, sb)

    @pl.when(place_ref[0] == 3)
    def _():
        coronal_piece(k * (rows // 4), rows // 4, depth, rim, zf, zh, zl, o_ref, ca)


def piece(k, place, blocks, net, prepared):
    slices, rows, columns = net.shape
    reach = rows + 6
    return pl.pallas_call(
        functools.partial(piece_kernel, k),
        out_shape=jax.ShapeDtypeStruct(net.shape, F32),
        in_specs=[in_smem()] + [in_vmem()] * (2 + len(prepared)),
        out_specs=in_vmem(),
        scratch_shapes=[pltpu.VMEM((reach * 128, columns // 2), BF16)] * 2
        + [pltpu.VMEM((rows // 4, 384, columns), BF16)]
        + [pltpu.VMEM((3, reach * 32, columns), BF16)] * 2,
        compiler_params=params(),
        name=f"piece_{k}",
    )(place, near(blocks), net, *prepared)


def swapped(groups, k):
    return [(g[n], g[(n + k) % len(g)]) for g in groups for n in range(len(g))]


def stage_groups(count):
    near = 4
    strided = 4
    far = count // (near * strided)
    at = lambda f, s, n: (f * strided + s) * near + n
    return [
        [[at(f, s, n) for f in range(far)] for s in range(strided) for n in range(near)],
        [[at(f, s, n) for s in range(strided)] for f in range(far) for n in range(near)],
        [[at(f, s, n) for n in range(near)] for f in range(far) for s in range(strided)],
    ]


def added_up(values, groups):
    total = values.astype(F32)
    for k in [k for k in (1, 3, 2) if k < len(groups[0])]:
        total = total + lax.ppermute(values, "tile", swapped(groups, k)).astype(F32)
    return total.astype(values.dtype)


def added_up_with_rims(first, own, groups, ends):
    far, strided, near = groups
    edge = own.shape[0] // 2
    rows = first.shape[0] - edge
    got = lax.ppermute(first, "tile", swapped(far, 1))
    tail, head = own[0:edge], own[edge:]
    onward = backward = got[rows:]
    sums = (first[0:rows].astype(F32) + got[0:rows].astype(F32)).astype(BF16)
    for n, group in enumerate((strided, near)):
        at_first, at_last = ends[n]
        sums, onward, backward = lax.optimization_barrier((sums, onward, backward))
        onward = jnp.where(at_last, onward, tail)
        backward = jnp.where(at_first, backward, head)
        up = lax.ppermute(jnp.concatenate([sums, onward]), "tile", swapped(group, 1))
        across = lax.ppermute(sums, "tile", swapped(group, 2))
        down = lax.ppermute(jnp.concatenate([sums, backward]), "tile", swapped(group, 3))
        onward, backward = up[rows:], down[rows:]
        total = sums.astype(F32) + up[0:rows].astype(F32)
        total = total + across.astype(F32) + down[0:rows].astype(F32)
        sums = total.astype(BF16)
    return sums, (onward, backward)


def slices_sent(current):
    return [lax.ppermute(current[k], "agent", [(0, k)]) for k in range(1, current.shape[0])]


def per_device(
    states,
    sinogram,
    blocks,
    block_angle,
    block_detector,
    block_tile,
    conv_first,
    conv_hidden,
    conv_last,
):
    current = states[0]
    tile_count = lax.axis_size("tile")
    tile_place = lax.axis_index("tile")
    agent_place = lax.axis_index("agent")
    place = jnp.stack([agent_place, tile_place, jnp.int32(tile_count)]).astype(jnp.int32)
    ray_total = sinogram.shape[0] * tile_count
    ray_index = block_angle * (current.shape[2] // 128) + block_detector

    within = [lax.shift_right_logical(tile_place, 2) & 3, tile_place & 3]
    ends = [(at == 0, at == 3) for at in within]
    got, ends = lax.optimization_barrier((slices_sent(current), ends))
    first, own, start, blocks_here = project(
        place, block_angle, block_detector, block_tile, states, got, sinogram, blocks, ray_total
    )

    groups = stage_groups(tile_count)
    net = jnp.zeros_like(current)
    x_data = start
    sums, rim = added_up_with_rims(first, own, groups, ends)
    for _ in range(DATA_STEPS - 2):
        x_data, sums = back_project(
            place, ray_index, block_tile, sums, x_data, sinogram, blocks_here
        )
        for group in groups:
            sums = added_up(sums, group)
    x_data, sums = back_project(place, ray_index, block_tile, sums, x_data, sinogram, blocks_here)
    for n, group in enumerate(groups):
        sums, net = lax.optimization_barrier((sums, net))
        if n == 0:
            prepared = prepare(place, rim, current, conv_first, conv_hidden, conv_last)
        for k in PIECES[n]:
            net = piece(k, place, blocks_here, net, prepared)
        sums = added_up(sums, group)
    sent = back_reflect(ray_index, block_tile, sums, x_data, start, current, net, blocks_here)
    everything = lax.all_gather(sent, "agent")
    return finish(place, everything, current, net)[None]


def solution(mesh):
    placed = (
        P("agent", None, "tile", None),
        P("tile", None, None),
        P("tile", None, None),
        P("tile"),
        P("tile"),
        P("tile"),
        P(),
        P(),
        P(),
    )
    return jax.shard_map(
        per_device,
        mesh=mesh,
        in_specs=placed,
        out_specs=P("agent", None, "tile", None),
        check_vma=False,
    )
```
